256 devices in a mesh: seq: 128 (over y, z, x), head: 2 (over core).
Axes of the slice: x: 4, y: 4, z: 8, core: 2. Of those that a mesh axis runs over, the one named last changes fastest.
Arguments:
- queries: bfloat16 [8192, 1536], P('seq', 'head'), may hold values from -6 to 6
- key_vectors: bfloat16 [8192, 512], P('seq', 'head'), may hold values from -6 to 6
- value_vectors: bfloat16 [8192, 512], P('seq', 'head'), may hold values from -6 to 6
- lengths: int32 [64], replicated, may hold values from 1 to 256, 8192 in all
- out_weight: bfloat16 [1536, 1536], P('head', 'seq'), may hold values from -0.15625 to 0.15625
- residual: bfloat16 [8192, 1536], P(('seq', 'head')), may hold values from -6 to 6
- norm_gain: float32 [1536], replicated, may hold values from 0.1 to 1.9
- route_ids: int32 [8192, 6], P(('seq', 'head')), may hold values from 0 to 63, all different within a row; in each aligned block of 32 rows (0 to 31, 32 to 63, ...) at most 6 rows name the same one
- route_logits: float32 [8192, 6], P(('seq', 'head')), may hold values from -8 to 340
- shared_gate_up: bfloat16 [1536, 2, 1024], P(None, None, ('seq', 'head')), may hold values from -0.15625 to 0.15625
- shared_down: bfloat16 [1024, 1536], P(('seq', 'head')), may hold values from -0.1875 to 0.1875
- expert_gate_up: bfloat16 [128, 1536, 2, 256], P('seq'), may hold values from -0.15625 to 0.15625
- expert_down: bfloat16 [128, 256, 1536], P('seq'), may hold values from -0.25 to 0.25
- cache_blocks: bfloat16 [128, 128, 8, 4, 128], P('seq', None, None, 'head'), may hold values from -6 to 6
- block_table: int32 [128], replicated, may hold values from 0 to 127, each once
Outputs:
- layer_out: bfloat16 [8192, 1536], P(('seq', 'head'))
- cache_out: bfloat16 [128, 128, 8, 4, 128], P(None, 'seq', None, 'head')
The draws below stay inside these ranges and needn't reach their ends.
Inputs may be any that keep to these rules, and one draw needn't show every extreme that they name: The lengths sum to 8192. `route_ids`: each token names 6 different experts; among the tokens of one device no expert is named more than 6 times. `block_table`: every block appears once.
All inputs are finite; a program needn't handle non-finite values.
Results may differ from the reference program's by a relative error of at most 0.0095.
Values may be sent and summed in bfloat16 or wider, within the bound.
A program may use at most 64 MiB of HBM per device.

```python
import math
import jax
import jax.numpy as jnp
import numpy as np
from jax import lax

D = 1536
QH = 12
KVH = 4
HD = 128
EXPERTS = 64
TOP = 6
EFF = 512
SFF = 1024
TOK_DEV = 64
BLK = 128
CLAYERS = 4
TOKENS = 8192
REQS = 64
MOST = 256
HALF_FF = 256
HALVES = 128
CAP = 6
BLOCKS = 128
N_HEAD = 2
DEVICES = 256


def draw_queries(key, part):
    sample = jax.random.truncated_normal(jax.random.fold_in(key, 1), -6.0, 6.0, (TOKENS, QH * HD), jnp.float32)
    return sample.astype(jnp.bfloat16)


def draw_key_vectors(key, part):
    sample = jax.random.truncated_normal(jax.random.fold_in(key, 3), -6.0, 6.0, (TOKENS, KVH * HD), jnp.float32)
    return sample.astype(jnp.bfloat16)


def draw_route_logits(key, part):
    sample = 2.0 * jax.random.truncated_normal(jax.random.fold_in(key, 26), -4.0, 4.0, (TOKENS, TOP), jnp.float32)
    return sample


def level_of(rng, shape, shards, low, high):
    loudness = 1.0
    for axis_at, parts in shards:
        steps = jax.random.uniform(jax.random.fold_in(jax.random.fold_in(rng, 6), axis_at), (parts,), jnp.float32, low / len(shards), high / len(shards))
        loudness = loudness * jnp.repeat(jnp.exp(steps), shape[axis_at] // parts).reshape((-1,) + (1,) * (len(shape) - 1 - axis_at))
    return loudness


def split_up(amount, total, reach, slope):
    loads = [(1 << 20) // math.isqrt(rank ** slope) + 1 for rank in range(2, amount + 1)]
    spare, counts = total - reach - (amount - 1), [1] * (amount - 1)
    while spare > 0:
        free = [i for i in range(amount - 1) if counts[i] < reach]
        pool, left = sum([loads[i] for i in free]), spare
        for i in free:
            addition = min(reach - counts[i], max(1, left * loads[i] // pool), spare)
            counts[i] = counts[i] + addition
            spare = spare - addition
    return np.array([reach] + counts)


def ragged(stream_key, amount, total, reach, skew):
    if amount == 2:
        one = jax.random.randint(stream_key, (), max(1, total - reach), min(reach, total - 1) + 1)
        return jnp.stack([one, total - one])
    sizes = jnp.asarray(split_up(amount, total, reach, skew), jnp.int32)
    twos = (amount - 1) // 2
    donor, taker = sizes[1:1 + 2 * twos:2], sizes[2:2 + 2 * twos:2]
    room = jnp.minimum(donor - 1, reach - taker)
    moved = jax.random.randint(jax.random.fold_in(stream_key, 1), (twos,), 0, 1 << 20) % (room + 1)
    sizes = sizes.at[1:1 + 2 * twos:2].set(donor - moved).at[2:2 + 2 * twos:2].set(taker + moved)
    return sizes[jax.random.permutation(jax.random.fold_in(stream_key, 2), amount)]


def routed_block(own_key, own, number, rows, amount, top, bound, slope):
    order = jax.random.permutation(own_key, amount)
    heavy_load, ordinary = load_shares(amount, rows * top, bound, slope, True), load_shares(amount, rows * top, bound, slope, False)
    places = jnp.arange(amount)

    def named(sizes, offset_by):
        used = int((sizes > 0).sum())
        fixed = max(1, used // 4)
        moved = fixed + (places - fixed + offset_by * (used - fixed)) % max(1, amount - fixed)
        return jnp.zeros((amount,), jnp.int32).at[order[jnp.where(places < fixed, places, moved)]].set(jnp.asarray(sizes, jnp.int32))

    sizes = jnp.where(number % 4 == 0, named(heavy_load, number // 4), named(ordinary, number - number // 4 - 1))
    mixed = jax.random.permutation(jax.random.fold_in(own, 3), amount)
    source_of, sink = mixed[0:amount // 2 * 2:2], mixed[1:amount // 2 * 2:2]
    slack = jnp.minimum(sizes[source_of] - 1, bound - sizes[sink]) // 2
    slack = jnp.where((source_of == order[0]) | (sink == order[0]) | (sizes[sink] == 0), 0, jnp.maximum(slack, 0))
    moved = jax.random.randint(jax.random.fold_in(own, 4), (amount // 2,), 0, 1 << 20) % (slack + 1)
    sizes = sizes.at[source_of].add(-moved).at[sink].add(moved)
    members = jnp.searchsorted(jnp.cumsum(sizes), jnp.arange(rows * top), side="right").astype(jnp.int32)
    grid = members.reshape(top, rows).T
    grid = grid[jax.random.permutation(jax.random.fold_in(own, 1), rows)]
    offset_by = jax.random.randint(jax.random.fold_in(own, 2), (rows, 1), 0, top)
    return jnp.take_along_axis(grid, (jnp.arange(top)[None, :] + offset_by) % top, axis=1)


def load_shares(amount, total, reach, slope, full):
    portions = [(1 << 20) // math.isqrt(grade ** slope) + 1 for grade in range(1, amount + 1)]
    largest = reach if full else min(reach, max(-(-total // amount), total * portions[0] // sum(portions)))
    least = 1 if total - largest >= amount - 1 else 0
    counts, surplus = [largest] + [least] * (amount - 1), total - largest - least * (amount - 1)
    while surplus > 0:
        movable = [i for i in range(1, amount) if counts[i] < largest] or [i for i in range(1, amount) if counts[i] < reach]
        pool, remaining = sum([portions[i] for i in movable]), surplus
        for i in movable:
            addition = min(reach - counts[i], max(1, remaining * portions[i] // pool), surplus)
            counts[i] = counts[i] + addition
            surplus = surplus - addition
    return np.array(counts)


def bell_draw(key, shape, width, most, pieces=(), kind=jnp.bfloat16):
    level = level_of(key, shape, pieces, -0.22, 0.18) if pieces else 1.0
    drawn = jax.random.normal(key, shape, jnp.float32) * width * level
    return jnp.minimum(jnp.maximum(drawn, -most), most).astype(kind)


def setup_inputs(seed: int = 0) -> dict:
    arg_keys = jax.random.split(jax.random.key(seed), 16)
    queries = draw_queries(jax.random.fold_in(arg_keys[15], 71), 0)
    key_vectors = draw_key_vectors(jax.random.fold_in(arg_keys[15], 71), 0)
    value_vectors = bell_draw(arg_keys[2], (TOKENS, KVH * HD), 1.0, 6.0, ((0, 128), (1, 2)))
    lengths = ragged(arg_keys[3], REQS, TOKENS, MOST, 2).astype(jnp.int32)
    out_weight = bell_draw(arg_keys[4], (QH * HD, D), (QH * HD) ** -0.5, 0.15625, ((0, 2), (1, 128)))
    residual = bell_draw(arg_keys[5], (TOKENS, D), 1.0, 6.0, ((0, 256),))
    norm_gain = jnp.clip(1.0 + 0.18 * jax.random.normal(arg_keys[6], (D,), jnp.float32), 0.1, 1.9)
    route_ids_keys = jax.random.split(jax.random.fold_in(arg_keys[7], 1), TOKENS // (TOK_DEV // N_HEAD))
    route_ids_turns = jax.random.permutation(jax.random.fold_in(arg_keys[7], 3), TOKENS // (TOK_DEV // N_HEAD))
    route_ids = jax.vmap(lambda own, number: routed_block(jax.random.fold_in(arg_keys[7], 2), own, number, TOK_DEV // N_HEAD, EXPERTS, TOP, CAP, 2))(route_ids_keys, route_ids_turns).reshape((TOKENS, TOP))
    route_logits = draw_route_logits(jax.random.fold_in(arg_keys[15], 71), 0)
    shared_gate_up = bell_draw(arg_keys[9], (D, 2, SFF), D ** -0.5, 0.15625, ((2, 256),))
    shared_down = bell_draw(arg_keys[10], (SFF, D), SFF ** -0.5, 0.1875, ((0, 256),))
    expert_gate_up = bell_draw(arg_keys[11], (HALVES, D, 2, HALF_FF), D ** -0.5, 0.15625, ((0, 128),))
    expert_down = bell_draw(arg_keys[12], (HALVES, HALF_FF, D), EFF ** -0.5, 0.25, ((0, 128),))
    cache_blocks = bell_draw(arg_keys[13], (BLOCKS, BLK, 2 * CLAYERS, KVH, HD), 1.0, 6.0, ((0, 128), (3, 2)))
    block_table = jax.random.permutation(arg_keys[14], BLOCKS).astype(jnp.int32)
    return dict(queries=queries, key_vectors=key_vectors, value_vectors=value_vectors, lengths=lengths, out_weight=out_weight, residual=residual, norm_gain=norm_gain, route_ids=route_ids, route_logits=route_logits, shared_gate_up=shared_gate_up, shared_down=shared_down, expert_gate_up=expert_gate_up, expert_down=expert_down, cache_blocks=cache_blocks, block_table=block_table)


NEGATIVE = -1e+30
EPSILON = 1e-05

def segment_of(positions, lengths):
    request_ends = jnp.cumsum(lengths).astype(jnp.int32)
    passed = (request_ends[None, :] <= positions[:, None]).astype(jnp.int32)
    return lax.optimization_barrier(jnp.sum(passed, axis=1)).astype(jnp.int32)

def attend(queries, key_vectors, value_vectors, lengths):
    group_size = QH // KVH
    block_rows = 512
    pad_keys = jnp.concatenate([jnp.zeros((MOST, KVH * HD), key_vectors.dtype), key_vectors], axis=0)
    pad_values = jnp.concatenate([jnp.zeros((MOST, KVH * HD), value_vectors.dtype), value_vectors], axis=0)

    def one_block(block_index):
        first_row = (block_index * block_rows).astype(jnp.int32)
        query_part = lax.dynamic_slice_in_dim(queries, first_row, block_rows, 0)
        query_part = query_part.reshape(block_rows, KVH, group_size, HD).astype(jnp.float32)
        key_part = lax.dynamic_slice_in_dim(pad_keys, first_row, MOST + block_rows, 0)
        key_part = key_part.reshape(MOST + block_rows, KVH, HD).astype(jnp.float32)
        value_part = lax.dynamic_slice_in_dim(pad_values, first_row, MOST + block_rows, 0)
        value_part = value_part.reshape(MOST + block_rows, KVH, HD).astype(jnp.float32)
        query_pos = first_row + jnp.arange(block_rows, dtype=jnp.int32)
        key_pos = first_row - MOST + jnp.arange(MOST + block_rows, dtype=jnp.int32)
        visible = (key_pos[None, :] >= 0) & (key_pos[None, :] <= query_pos[:, None])
        visible = visible & (segment_of(key_pos, lengths)[None, :] == segment_of(query_pos, lengths)[:, None])
        scores = jnp.einsum('tkgd,wkd->kgtw', query_part, key_part) * (1.0 / math.sqrt(HD))
        scores = jnp.where(visible[None, None], scores, NEGATIVE)
        row_max = lax.optimization_barrier(jnp.max(scores, axis=-1, keepdims=True))
        weights = jnp.exp(scores - row_max)
        row_total = lax.optimization_barrier(jnp.sum(weights, axis=-1))
        rounded = lax.optimization_barrier(weights.astype(jnp.bfloat16)).astype(jnp.float32)
        weighted = jnp.einsum('kgtw,wkd->tkgd', rounded, value_part)
        heads = weighted / jnp.transpose(row_total, (2, 0, 1))[..., None]
        return heads.astype(jnp.bfloat16).reshape(block_rows, QH * HD)
    blocks = lax.map(one_block, jnp.arange(TOKENS // block_rows, dtype=jnp.int32))
    return blocks.reshape(TOKENS, QH * HD)

def reference(queries, key_vectors, value_vectors, lengths, out_weight, residual, norm_gain, route_ids, route_logits, shared_gate_up, shared_down, expert_gate_up, expert_down, cache_blocks, block_table):
    heads = attend(queries, key_vectors, value_vectors, lengths)
    attn_out = jnp.dot(heads, out_weight, preferred_element_type=jnp.float32)
    mixed = residual.astype(jnp.float32) + attn_out
    mean_square = lax.optimization_barrier(jnp.mean(mixed * mixed, axis=-1, keepdims=True))
    normed = (mixed * lax.rsqrt(mean_square + EPSILON) * norm_gain).astype(jnp.bfloat16)
    shared_both = jnp.einsum('td,dcf->tcf', normed.astype(jnp.float32), shared_gate_up.astype(jnp.float32))
    shared_act = (jax.nn.silu(shared_both[:, 0]) * shared_both[:, 1]).astype(jnp.bfloat16)
    shared_part = jnp.dot(shared_act, shared_down, preferred_element_type=jnp.float32)
    route_probs = jax.nn.softmax(route_logits, axis=-1)
    rows_block = TOK_DEV // N_HEAD
    flat_ids = route_ids.reshape(-1).astype(jnp.int32)
    onehot = (flat_ids.reshape(DEVICES, rows_block * TOP)[:, :, None] == jnp.arange(EXPERTS, dtype=jnp.int32)[None, None, :]).astype(jnp.int32)
    slot_rank = lax.optimization_barrier(jnp.sum((jnp.cumsum(onehot, axis=1) - 1) * onehot, axis=2)).reshape(-1).astype(jnp.int32)
    block_of = (jnp.arange(TOKENS * TOP, dtype=jnp.int32) // (rows_block * TOP)).astype(jnp.int32)
    slot_of = (block_of * CAP + slot_rank).astype(jnp.int32)
    token_of = (jnp.arange(TOKENS * TOP, dtype=jnp.int32) // TOP).astype(jnp.int32)
    weight_of = route_probs.reshape(-1)
    slot_count = DEVICES * CAP
    padded = jnp.concatenate([normed, jnp.zeros((1, D), normed.dtype)], axis=0)

    def one_expert(accumulated, expert):
        chosen = flat_ids == expert
        target = jnp.where(chosen, slot_of, slot_count).astype(jnp.int32)
        row_index = jnp.full((slot_count,), TOKENS, jnp.int32).at[target].set(token_of, mode='drop')
        row_scale = jnp.zeros((slot_count,), jnp.float32).at[target].set(weight_of, mode='drop')
        rows_in = padded[row_index]
        summed = jnp.zeros((slot_count, D), jnp.float32)
        for half_index in range(2):
            weight_row = half_index * EXPERTS + expert
            gate_up = jnp.dot(rows_in, expert_gate_up[weight_row].reshape(D, 2 * HALF_FF), preferred_element_type=jnp.float32)
            expert_act = (jax.nn.silu(gate_up[:, :HALF_FF]) * gate_up[:, HALF_FF:]).astype(jnp.bfloat16)
            half_out = jnp.dot(expert_act, expert_down[weight_row], preferred_element_type=jnp.float32)
            summed = summed + lax.optimization_barrier(half_out.astype(jnp.bfloat16)).astype(jnp.float32)
        accumulated = accumulated.at[row_index].add(row_scale[:, None] * summed, mode='drop')
        return (accumulated, None)
    routed, _ = lax.scan(one_expert, jnp.zeros((TOKENS, D), jnp.float32), jnp.arange(EXPERTS, dtype=jnp.int32))
    layer_out = (mixed + shared_part + routed).astype(jnp.bfloat16)
    cache_out = jnp.take(cache_blocks, block_table, axis=0)
    return (layer_out, cache_out)
```

```python
import functools
import math

import jax
import jax.numpy as jnp
from jax import lax
from jax.experimental import pallas as pl
from jax.experimental.pallas import tpu as pltpu
from jax.sharding import PartitionSpec as P

MESH = pl.DeviceIdType.MESH
HD = 128
NY, NZ, NX = 4, 8, 4
TOP = 6
CAP = 6
EXPERTS = 64
NEGATIVE = -1e30
EPSILON = 1e-05
F32 = jnp.float32
BF16 = jnp.bfloat16
ZORDER = (1, 7, 2, 6, 3, 5, 4)
NT = (((1,), (1,)), ((), ()))


def place():
    s = lax.axis_index("seq")
    h = lax.axis_index("head")
    y = lax.div(s, NZ * NX)
    z = lax.rem(lax.div(s, NX), NZ)
    x = lax.rem(s, NX)
    return s, h, y, z, x


def seq_of(y, z, x):
    return y * (NZ * NX) + z * NX + x


def up(i, by, n):
    return lax.rem(i + by, n)


def rcopy(src, dst, ssem, rsem, dev):
    return pltpu.make_async_remote_copy(
        src_ref=src, dst_ref=dst, send_sem=ssem, recv_sem=rsem, device_id=dev, device_id_type=MESH
    )


def greet(peers):
    barrier = pltpu.get_barrier_semaphore()
    for dev in peers:
        pl.semaphore_signal(barrier, inc=1, device_id=dev, device_id_type=MESH)
    pl.semaphore_wait(barrier, len(peers))


def iota(shape, axis):
    return lax.broadcasted_iota(jnp.int32, shape, axis)


def silu(v):
    return v / (1.0 + jnp.exp(-v))


def routing_table(ids, logits):
    tok = ids.shape[0]
    lane = iota((tok, 128), 1)
    top = jnp.max(logits, axis=-1, keepdims=True)
    e = jnp.exp(logits - top)
    probs = e / jnp.sum(e, axis=-1, keepdims=True)
    named = jnp.zeros((tok, 128), F32)
    weight = jnp.zeros((tok, 128), F32)
    for r in range(TOP):
        idr = ids[:, r : r + 1]
        named = named + jnp.where(lane == idr, 1.0, 0.0)
        weight = weight + jnp.where(lane - EXPERTS == idr, probs[:, r : r + 1], 0.0)
    before = jnp.where(iota((tok, tok), 1) < iota((tok, tok), 0), 1.0, 0.0)
    rank = jnp.dot(before.astype(BF16), named.astype(BF16), preferred_element_type=F32)
    return jnp.where(lane < EXPERTS, jnp.where(named > 0.5, rank, -1.0), weight)


def front_kernel(
    q_ref, k_ref, v_ref, len_ref, ow_ref, res_ref, gain_ref, ids_ref, log_ref,
    sh_ref, wg_ref, wd_ref, cache_ref,
    mixed_ref, xall_ref, rpall_ref, shall_ref, wgo_ref, wdo_ref, cmid_ref, chand_ref,
    kwin, vwin, owbuf, wc, hbuf, part, rbuf, nbuf, rpbuf,
    kv_s, kv_r, owz_s, owz_r, owx_s, owx_r, rp_s, rp_r, sh_s, sh_r, cz_s, cz_r, cp_s, cp_r,
    ex_s, ex_r, sib_s, sib_r, hy_s, hy_r, rs_s, rs_r, xz_s, xz_r, loc,
):
    s, h, y, z, x = place()
    seqs = NY * NZ * NX
    zdev = [(seq_of(y, up(z, d, NZ), x), h) for d in ZORDER]
    plane = [
        (dy, dx) for dy in range(NY) for dx in range(NX) if (dy, dx) != (0, 0)
    ]
    pdev = [(seq_of(up(y, dy, NY), z, up(x, dx, NX)), h) for dy, dx in plane]
    sib = (s, 1 - h)
    cross = [(seq_of(up(y, dy, NY), z, x), 1 - h) for dy in (1, 2, 3)]
    ahead = [(lax.rem(s + by, seqs), h) for by in range(1, 5)]
    behind = [(lax.rem(s + seqs - by, seqs), h) for by in range(1, 5)]
    greet(zdev + pdev + [sib] + cross + ahead + behind)

    pending = []

    def go(copy):
        copy.start()
        pending.append(copy)
        return copy

    kv = []
    for by in range(1, 5):
        rows = pl.ds(64 * (4 - by), 64)
        kv.append(go(rcopy(k_ref, kwin.at[rows], kv_s.at[0, by - 1], kv_r.at[0, by - 1], ahead[by - 1])))
        kv.append(go(rcopy(v_ref, vwin.at[rows], kv_s.at[1, by - 1], kv_r.at[1, by - 1], ahead[by - 1])))
    own = [
        pltpu.make_async_copy(k_ref, kwin.at[pl.ds(256, 64)], loc.at[0]),
        pltpu.make_async_copy(v_ref, vwin.at[pl.ds(256, 64)], loc.at[1]),
        pltpu.make_async_copy(ow_ref, owbuf.at[z, x], loc.at[2]),
        pltpu.make_async_copy(sh_ref, shall_ref.at[y, x, h], loc.at[3]),
        pltpu.make_async_copy(cache_ref.at[:, z], cmid_ref.at[z], loc.at[4]),
    ]
    for c in own:
        c.start()
    owz = [
        go(rcopy(ow_ref, owbuf.at[z, x], owz_s.at[i], owz_r.at[i], zdev[i])) for i in range(7)
    ]
    pair = (seq_of(up(y, 2, NY), z, x), h)
    rows_g, rows_d = pl.ds(h * 768, 768), pl.ds(h * 128, 128)
    ex = [
        go(rcopy(wg_ref.at[rows_g], wgo_ref.at[rows_g], ex_s.at[0], ex_r.at[0], pair)),
        go(rcopy(wd_ref.at[rows_d], wdo_ref.at[rows_d], ex_s.at[1], ex_r.at[1], pair)),
    ]
    shp = [
        go(rcopy(sh_ref, shall_ref.at[y, x, h], sh_s.at[i], sh_r.at[i], pdev[i])) for i in range(15)
    ]
    cz = [
        go(rcopy(cache_ref.at[:, up(z, d, NZ)], cmid_ref.at[z], cz_s.at[i], cz_r.at[i], zdev[i]))
        for i, d in enumerate(ZORDER)
    ]

    rpbuf[...] = routing_table(ids_ref[...], log_ref[...])
    rp = [go(rcopy(rpbuf, rpall_ref.at[z], rp_s.at[i], rp_r.at[i], zdev[i])) for i in range(7)]
    rp_own = pltpu.make_async_copy(rpbuf, rpall_ref.at[z], loc.at[5])
    rp_own.start()

    upper = jnp.where(iota((128, 128), 0) <= iota((128, 128), 1), 1.0, 0.0).astype(BF16)
    lens = jnp.broadcast_to(len_ref[...], (16, 128)).astype(BF16)
    ends = jnp.dot(lens, upper, preferred_element_type=F32)[0:1, :]
    qpos = (s * 64 + iota((64, 128), 0)).astype(F32)
    first = jnp.max(jnp.where(ends <= qpos, ends, 0.0), axis=-1, keepdims=True)
    kpos = (s * 64 - 256 + iota((64, 320), 1)).astype(F32)
    qcol = (s * 64 + iota((64, 320), 0)).astype(F32)
    seen = jnp.where((kpos >= first) & (kpos <= qcol), 0.0, NEGATIVE)
    seen3 = jnp.concatenate([seen, seen, seen], axis=0)

    own[2].wait()
    for c in owz:
        c.wait_recv()
    owx = []
    for d in (1, 3, 2):
        dev = (seq_of(y, z, up(x, d, NX)), h)
        owx.append(go(rcopy(owbuf.at[:, x], owbuf.at[:, x], owx_s.at[d - 1], owx_r.at[d - 1], dev)))

    own[0].wait()
    own[1].wait()
    for c in kv:
        c.wait_recv()
    for g in range(2):
        cols = slice(g * HD, (g + 1) * HD)
        qs = jnp.concatenate(
            [q_ref[:, (3 * g + i) * HD : (3 * g + i + 1) * HD] for i in range(3)], axis=0
        )
        sc = lax.dot_general(qs, kwin[:, cols], NT, preferred_element_type=F32)
        sc = jnp.where(seen3 < -1.0, NEGATIVE, sc * (1.0 / math.sqrt(HD)))
        w = jnp.exp(sc - jnp.max(sc, axis=-1, keepdims=True))
        total = jnp.sum(w, axis=-1, keepdims=True)
        o = jnp.dot(w.astype(BF16), vwin[:, cols], preferred_element_type=F32)
        o = (o / total).astype(BF16)
        for i in range(3):
            hbuf[y, :, (3 * g + i) * HD : (3 * g + i + 1) * HD] = o[i * 64 : (i + 1) * 64]

    hy = []
    for d in (1, 3, 2):
        dev = (seq_of(up(y, d, NY), z, x), h)
        hy.append(go(rcopy(hbuf.at[y], hbuf.at[y], hy_s.at[d - 1], hy_r.at[d - 1], dev)))

    own[4].wait()
    for c in cz:
        c.wait_recv()
    cp = []
    for i, (dy, dx) in enumerate(plane):
        src = cmid_ref.at[:, up(y, dy, NY), up(x, dx, NX)]
        cp.append(go(rcopy(src, chand_ref.at[y, :, x], cp_s.at[i], cp_r.at[i], pdev[i])))
    cp_own = pltpu.make_async_copy(cmid_ref.at[:, y, x], chand_ref.at[y, :, x], loc.at[6])
    cp_own.start()

    for c in owx:
        c.wait_recv()
    col, row = iota((384, 512), 0), iota((384, 512), 1)
    pick = jnp.where(row == lax.div(col, 12) * 16 + lax.rem(col, 12), 1.0, 0.0).astype(BF16)
    wc[...] = jnp.dot(pick, owbuf[...].reshape(512, 768), preferred_element_type=F32).astype(BF16)

    for c in hy:
        c.wait_recv()
    po = lax.dot_general(hbuf[...].reshape(256, 768), wc[...], NT, preferred_element_type=F32)
    part[...] = po.reshape(4, 2, 32, 384)
    rs = []
    for d in (1, 3, 2):
        yd = up(y, d, NY)
        for i, hd in enumerate((h, 1 - h)):
            rs.append(
                go(rcopy(part.at[yd, hd], rbuf.at[y, h], rs_s.at[i, d], rs_r.at[i, d], (seq_of(yd, z, x), hd)))
            )
    rs.append(go(rcopy(part.at[y, 1 - h], rbuf.at[y, h], rs_s.at[1, 0], rs_r.at[1, 0], sib)))
    rbuf[y, h] = part[y, h]
    for c in rs:
        c.wait_recv()
    attn = [rbuf[j, 0] + rbuf[j, 1] for j in range(NY)]
    mixed = res_ref[...].astype(F32) + jnp.concatenate(attn, axis=1)
    mixed_ref[...] = mixed
    ms = jnp.mean(mixed * mixed, axis=-1, keepdims=True)
    nbuf[...] = (mixed * lax.rsqrt(ms + EPSILON) * gain_ref[...]).astype(BF16)
    xz = [go(rcopy(nbuf, xall_ref.at[z], xz_s.at[i], xz_r.at[i], zdev[i])) for i in range(7)]
    x_own = pltpu.make_async_copy(nbuf, xall_ref.at[z], loc.at[7])
    x_own.start()

    own[3].wait()
    for c in shp:
        c.wait_recv()
    last = [go(rcopy(shall_ref.at[:, :, h], shall_ref.at[:, :, h], sib_s.at[0], sib_r.at[0], sib))]
    for c in ex:
        c.wait_recv()
    last.append(go(rcopy(wgo_ref.at[rows_g], wgo_ref.at[rows_g], sib_s.at[1], sib_r.at[1], sib)))
    last.append(go(rcopy(wdo_ref.at[rows_d], wdo_ref.at[rows_d], sib_s.at[2], sib_r.at[2], sib)))
    rp_own.wait()
    cp_own.wait()
    x_own.wait()
    for c in rp + cp + xz + last:
        c.wait_recv()
    for c in pending:
        c.wait_send()


def moe_kernel(
    x_hbm, rp_ref, sh_hbm, wg_hbm, wd_hbm, wgo_hbm, wdo_hbm, mixed_ref,
    out_ref,
    xb, shb, wgb, wdb, dsend, drecv, rsend, rrecv, pz, racc,
    d_s, d_r, r_s, r_r, z_s, z_r, loc,
):
    s, h, y, z, x = place()
    copies = [
        pltpu.make_async_copy(x_hbm, xb, loc.at[0]),
        pltpu.make_async_copy(sh_hbm, shb, loc.at[1]),
        pltpu.make_async_copy(wg_hbm, wgb.at[0], loc.at[2]),
        pltpu.make_async_copy(wgo_hbm, wgb.at[1], loc.at[3]),
        pltpu.make_async_copy(wd_hbm, wdb.at[0], loc.at[4]),
        pltpu.make_async_copy(wdo_hbm, wdb.at[1], loc.at[5]),
    ]
    for c in copies:
        c.start()
    zdev = [(seq_of(y, up(z, d, NZ), x), h) for d in ZORDER]
    hops = [(p, d) for p in range(2) for d in range(NX) if (p, d) != (0, 0)]
    dests = [(seq_of(up(y, p, NY), z, up(x, d, NX)), h) for p, d in hops]
    sources = [(seq_of(up(y, NY - p, NY), z, up(x, NX - d, NX)), h) for p, d in hops]
    greet(zdev + dests + sources)

    cols = 8 * 48
    lane = iota((128, cols), 1)
    half = lax.div(lane, 192)
    expert = lax.rem(y + half, 2) * 32 + z * NX + lax.rem(lax.div(lane, 48), NX)
    row = iota((128, cols), 0)
    rp = rp_ref[...].reshape(256, 128).astype(BF16)
    rank = jnp.dot(rp, jnp.where(row == expert, 1.0, 0.0).astype(BF16), preferred_element_type=F32)
    prob = jnp.dot(
        rp, jnp.where(row == expert + EXPERTS, 1.0, 0.0).astype(BF16), preferred_element_type=F32
    )
    tok = iota((256, cols), 0)
    slot = lax.rem(iota((256, cols), 1), 48)
    hit = (lax.div(tok, 32) == lax.div(slot, CAP)) & (rank == lax.rem(slot, CAP).astype(F32))
    pick = jnp.transpose(jnp.where(hit, 1.0, 0.0)).astype(BF16)
    weight = jnp.where(hit, prob, 0.0).astype(BF16)
    copies[0].wait()
    xs = xb[...].reshape(256, 1536)
    dsend[...] = (
        jnp.dot(pick, xs, preferred_element_type=F32).astype(BF16).reshape(8, 48, 1536)
    )
    pending = []

    def go(copy):
        copy.start()
        pending.append(copy)
        return copy

    sent = []
    for i, (p, d) in enumerate(hops):
        sent.append(
            go(rcopy(dsend.at[p * NX + up(x, d, NX)], drecv.at[p * NX + x], d_s.at[i], d_r.at[i], dests[i]))
        )
    drecv[x] = dsend[x]

    copies[1].wait()
    sh = shb[...].reshape(512, 1536)
    both = lax.dot_general(xs, sh, NT, preferred_element_type=F32)
    act = silu(pltpu.roll(both, 8, 1)) * pltpu.roll(both, 4, 1)
    live = lax.rem(lax.div(iota((256, 512), 1), 4), 4) == 2
    act = jnp.where(live, act, 0.0).astype(BF16)
    shared = jnp.dot(act, sh, preferred_element_type=F32)

    for c in copies[2:]:
        c.wait()
    for c in sent:
        c.wait_recv()
    rows = drecv[...].reshape(cols, 1536)
    acc = None
    for j in range(2):
        gu = jnp.dot(rows, wgb[j], preferred_element_type=F32)
        a = (silu(gu[:, :256]) * gu[:, 256:]).astype(BF16)
        o = jnp.dot(a, wdb[j], preferred_element_type=F32)
        acc = o if acc is None else acc + o
    rsend[...] = acc.astype(BF16).reshape(8, 48, 1536)
    back = []
    for i, (p, d) in enumerate(hops):
        src = rsend.at[p * NX + up(x, NX - d, NX)]
        back.append(go(rcopy(src, rrecv.at[p * NX + x], r_s.at[i], r_r.at[i], sources[i])))
    rrecv[x] = rsend[x]
    for c in back:
        c.wait_recv()
    tot = shared + jnp.dot(weight, rrecv[...].reshape(cols, 1536), preferred_element_type=F32)
    pz[...] = tot.astype(BF16).reshape(8, 32, 1536)
    red = [
        go(rcopy(pz.at[up(z, d, NZ)], racc.at[z], z_s.at[i], z_r.at[i], zdev[i]))
        for i, d in enumerate(ZORDER)
    ]
    racc[z] = pz[z]
    for c in red:
        c.wait_recv()
    out = mixed_ref[...]
    for j in range(NZ):
        out = out + racc[j].astype(F32)
    out_ref[...] = out.astype(BF16)
    for c in pending:
        c.wait_send()


def shards(
    queries, key_vectors, value_vectors, lengths, out_weight, residual, norm_gain, route_ids,
    route_logits, shared_gate_up, shared_down, expert_gate_up, expert_down, cache_blocks, block_table,
):
    any_, vmem = pl.BlockSpec(memory_space=pl.ANY), pl.BlockSpec(memory_space=pltpu.VMEM)
    dma = pltpu.SemaphoreType.DMA
    lens = jnp.pad(lengths.astype(F32), (0, 64)).reshape(1, 128)
    ow = jnp.pad(out_weight.T, ((0, 4), (0, 0)))
    sh = jnp.concatenate(
        [
            jnp.transpose(shared_gate_up, (1, 2, 0)).reshape(8, 1536),
            shared_down,
            jnp.zeros((4, 1536), BF16),
        ],
        axis=0,
    )
    wg = expert_gate_up.reshape(1536, 512)
    wd = expert_down.reshape(256, 1536)
    cache = cache_blocks.reshape(NY, NZ, NX, 8, 2, HD)
    sds = jax.ShapeDtypeStruct
    mixed, xall, rpall, shall, wgo, wdo, _, chand = pl.pallas_call(
        front_kernel,
        out_shape=(
            sds((32, 1536), F32),
            sds((NZ, 32, 1536), BF16),
            sds((NZ, 32, 128), F32),
            sds((NY, NX, 2, 16, 1536), BF16),
            sds((1536, 512), BF16),
            sds((256, 1536), BF16),
            sds((NZ, NY, NX, 8, 2, HD), BF16),
            sds((NY, NZ, NX, 8, 2, HD), BF16),
        ),
        in_specs=[vmem, any_, any_, vmem, any_, vmem, vmem, vmem, vmem, any_, any_, any_, any_],
        out_specs=(vmem, any_, any_, any_, any_, any_, any_, any_),
        scratch_shapes=[
            pltpu.VMEM((320, 256), BF16),
            pltpu.VMEM((320, 256), BF16),
            pltpu.VMEM((NZ, NX, 16, 768), BF16),
            pltpu.VMEM((384, 768), BF16),
            pltpu.VMEM((NY, 64, 768), BF16),
            pltpu.VMEM((NY, 2, 32, 384), F32),
            pltpu.VMEM((NY, 2, 32, 384), F32),
            pltpu.VMEM((32, 1536), BF16),
            pltpu.VMEM((32, 128), F32),
            dma((2, 4)), dma((2, 4)),
            dma((7,)), dma((7,)),
            dma((3,)), dma((3,)),
            dma((7,)), dma((7,)),
            dma((15,)), dma((15,)),
            dma((7,)), dma((7,)),
            dma((15,)), dma((15,)),
            dma((2,)), dma((2,)),
            dma((3,)), dma((3,)),
            dma((3,)), dma((3,)),
            dma((2, 4)), dma((2, 4)),
            dma((7,)), dma((7,)),
            dma((8,)),
        ],
        compiler_params=pltpu.CompilerParams(
            collective_id=0, has_side_effects=True, vmem_limit_bytes=40 << 20
        ),
        name="front",
    )(
        queries, key_vectors, value_vectors, lens, ow, residual, norm_gain.reshape(1, 1536),
        route_ids, route_logits, sh, wg, wd, cache,
    )
    cache_out = jnp.take(chand.reshape(128, 1, 8, 2, HD), block_table, axis=0)
    layer_out = pl.pallas_call(
        moe_kernel,
        out_shape=sds((32, 1536), BF16),
        in_specs=[any_, vmem, any_, any_, any_, any_, any_, vmem],
        out_specs=vmem,
        scratch_shapes=[
            pltpu.VMEM((NZ, 32, 1536), BF16),
            pltpu.VMEM((NY, NX, 2, 16, 1536), BF16),
            pltpu.VMEM((2, 1536, 512), BF16),
            pltpu.VMEM((2, 256, 1536), BF16),
            pltpu.VMEM((8, 48, 1536), BF16),
            pltpu.VMEM((8, 48, 1536), BF16),
            pltpu.VMEM((8, 48, 1536), BF16),
            pltpu.VMEM((8, 48, 1536), BF16),
            pltpu.VMEM((NZ, 32, 1536), BF16),
            pltpu.VMEM((NZ, 32, 1536), BF16),
            dma((7,)), dma((7,)),
            dma((7,)), dma((7,)),
            dma((7,)), dma((7,)),
            dma((6,)),
        ],
        compiler_params=pltpu.CompilerParams(
            collective_id=1, has_side_effects=True, vmem_limit_bytes=50 << 20
        ),
        name="moe",
    )(xall, rpall, shall, wg, wd, wgo, wdo, mixed)
    return layer_out, cache_out


def solution(mesh):
    in_specs = (
        P("seq", "head"),
        P("seq", "head"),
        P("seq", "head"),
        P(),
        P("head", "seq"),
        P(("seq", "head"), None),
        P(),
        P(("seq", "head"), None),
        P(("seq", "head"), None),
        P(None, None, ("seq", "head")),
        P(("seq", "head"), None),
        P("seq", None, None, None),
        P("seq", None, None),
        P("seq", None, None, "head", None),
        P(),
    )
    out_specs = (P(("seq", "head"), None), P(None, "seq", None, "head", None))
    return jax.shard_map(shards, mesh=mesh, in_specs=in_specs, out_specs=out_specs, check_vma=False)
```

```python
import functools
import math

import jax
import jax.numpy as jnp
from jax import lax
from jax.experimental import pallas as pl
from jax.experimental.pallas import tpu as pltpu
from jax.sharding import PartitionSpec as P

MESH = pl.DeviceIdType.MESH
HD = 128
NY, NZ, NX = 4, 8, 4
TOP = 6
CAP = 6
EXPERTS = 64
NEGATIVE = -1e30
EPSILON = 1e-05
F32 = jnp.float32
BF16 = jnp.bfloat16
ZORDER = (1, 7, 2, 6, 3, 5, 4)
OFF = (0, 1, 4, 3, 7, 6, 2, 5)
SLOT = {o: k for k, o in enumerate(OFF)}
ROWS = 24
COLS = 8 * ROWS
NT = (((1,), (1,)), ((), ()))


def place():
    s = lax.axis_index("seq")
    h = lax.axis_index("head")
    y = lax.div(s, NZ * NX)
    z = lax.rem(lax.div(s, NX), NZ)
    x = lax.rem(s, NX)
    return s, h, y, z, x


def seq_of(y, z, x):
    return y * (NZ * NX) + z * NX + x


def up(i, by, n):
    return lax.rem(i + by, n)


def rcopy(src, dst, ssem, rsem, dev):
    return pltpu.make_async_remote_copy(
        src_ref=src, dst_ref=dst, send_sem=ssem, recv_sem=rsem, device_id=dev, device_id_type=MESH
    )


def greet(peers):
    barrier = pltpu.get_barrier_semaphore()
    for dev in peers:
        pl.semaphore_signal(barrier, inc=1, device_id=dev, device_id_type=MESH)
    pl.semaphore_wait(barrier, len(peers))


def iota(shape, axis):
    return lax.broadcasted_iota(jnp.int32, shape, axis)


def silu(v):
    return v / (1.0 + jnp.exp(-v))


def routing_table(ids, logits):
    tok = ids.shape[0]
    lane = iota((tok, 128), 1)
    top = jnp.max(logits, axis=-1, keepdims=True)
    e = jnp.exp(logits - top)
    probs = e / jnp.sum(e, axis=-1, keepdims=True)
    named = jnp.zeros((tok, 128), F32)
    weight = jnp.zeros((tok, 128), F32)
    for r in range(TOP):
        idr = ids[:, r : r + 1]
        named = named + jnp.where(lane == idr, 1.0, 0.0)
        weight = weight + jnp.where(lane - EXPERTS == idr, probs[:, r : r + 1], 0.0)
    before = jnp.where(iota((tok, tok), 1) < iota((tok, tok), 0), 1.0, 0.0)
    rank = jnp.dot(before.astype(BF16), named.astype(BF16), preferred_element_type=F32)
    return jnp.where(lane < EXPERTS, jnp.where(named > 0.5, rank, -1.0), weight)


def layer_kernel(
    q_hbm, k_hbm, v_hbm, len_ref, ow_hbm, res_hbm, gain_ref, ids_ref, log_ref,
    sh_hbm, wg_hbm, wd_hbm, cache_hbm,
    out_ref, cmid_ref, chand_ref,
    qbuf, kwin, vwin, resbuf, owbuf, wc, hbuf, part, rbuf, xb, rpb, shb, wgb, wdb,
    dsend, drecv, rsend, rrecv, pz, racc,
    kv_s, kv_r, owz_s, owz_r, owx_s, owx_r, rp_s, rp_r, sh_s, sh_r, cz_s, cz_r, cp_s, cp_r,
    ex_s, ex_r, sib_s, sib_r, hy_s, hy_r, rs_s, rs_r, xz_s, xz_r, d_s, d_r, r_s, r_r, z_s, z_r, loc,
):
    s, h, y, z, x = place()
    seqs = NY * NZ * NX
    zdev = {d: (seq_of(y, up(z, d, NZ), x), h) for d in range(1, NZ)}
    plane = [
        (dy, dx) for dy in range(NY) for dx in range(NX) if (dy, dx) != (0, 0)
    ]
    pdev = {at: (seq_of(up(y, at[0], NY), z, up(x, at[1], NX)), h) for at in plane}
    sib = (s, 1 - h)
    cross = [(seq_of(up(y, dy, NY), z, x), 1 - h) for dy in (1, 2, 3)]
    ahead = [(lax.rem(s + by, seqs), h) for by in range(1, 5)]
    behind = [(lax.rem(s + seqs - by, seqs), h) for by in range(1, 5)]

    local = []

    def here(src, dst):
        copy = pltpu.make_async_copy(src, dst, loc.at[len(local)])
        copy.start()
        local.append(copy)
        return copy

    own_k = here(k_hbm, kwin.at[pl.ds(256, 64)])
    own_v = here(v_hbm, vwin.at[pl.ds(256, 64)])
    own_q = here(q_hbm, qbuf)
    own_ow = here(ow_hbm, owbuf.at[z, x])
    own_cache = here(cache_hbm.at[:, z], cmid_ref.at[z])
    own_res = here(res_hbm, resbuf)
    own_sh = here(sh_hbm, shb.at[y, x, h])
    own_wg = here(wg_hbm, wgb.at[0])
    own_wd = here(wd_hbm, wdb.at[0])
    greet(list(zdev.values()) + list(pdev.values()) + [sib] + cross + ahead + behind)

    pending = []

    def go(*args):
        copy = rcopy(*args)
        copy.start()
        pending.append(copy)
        return copy

    kv = []
    for by in range(1, 5):
        rows = pl.ds(64 * (4 - by), 64)
        kv.append(go(k_hbm, kwin.at[rows], kv_s.at[0, by - 1], kv_r.at[0, by - 1], ahead[by - 1]))
        kv.append(go(v_hbm, vwin.at[rows], kv_s.at[1, by - 1], kv_r.at[1, by - 1], ahead[by - 1]))
    owz = [go(ow_hbm, owbuf.at[z, x], owz_s.at[d], owz_r.at[d], zdev[d]) for d in ZORDER]
    with jax.named_scope("routing"):
        rpb[0] = routing_table(ids_ref[...], log_ref[...])
    rp = [
        go(rpb.at[0], rpb.at[SLOT[NZ - d]], rp_s.at[d], rp_r.at[d], zdev[d]) for d in ZORDER
    ]
    shp = [
        go(sh_hbm, shb.at[y, x, h], sh_s.at[i], sh_r.at[i], pdev[at]) for i, at in enumerate(plane)
    ]
    cz = [
        go(cache_hbm.at[:, up(z, d, NZ)], cmid_ref.at[z], cz_s.at[d], cz_r.at[d], zdev[d])
        for d in ZORDER
    ]
    pair = pdev[(2, 0)]
    rows_g, rows_d = pl.ds(h * 768, 768), pl.ds(h * 128, 128)
    ex = [
        go(wg_hbm.at[rows_g], wgb.at[1, rows_g], ex_s.at[0], ex_r.at[0], pair),
        go(wd_hbm.at[rows_d], wdb.at[1, rows_d], ex_s.at[1], ex_r.at[1], pair),
    ]

    with jax.named_scope("visible"):
        upper = jnp.where(iota((128, 128), 0) <= iota((128, 128), 1), 1.0, 0.0).astype(BF16)
        lens = jnp.broadcast_to(len_ref[...], (16, 128)).astype(BF16)
        ends = jnp.dot(lens, upper, preferred_element_type=F32)[0:1, :]
        qpos = (s * 64 + iota((64, 128), 0)).astype(F32)
        first = jnp.max(jnp.where(ends <= qpos, ends, 0.0), axis=-1, keepdims=True)
        kpos = (s * 64 - 256 + iota((64, 320), 1)).astype(F32)
        qcol = (s * 64 + iota((64, 320), 0)).astype(F32)
        seen = jnp.where((kpos >= first) & (kpos <= qcol), 0.0, NEGATIVE)
        seen3 = jnp.concatenate([seen, seen, seen], axis=0)

    with jax.named_scope("wait_keys"):
        own_k.wait()
        own_v.wait()
        own_q.wait()
        for c in kv:
            c.wait_recv()
    with jax.named_scope("attention"):
        for g in range(2):
            cols = slice(g * HD, (g + 1) * HD)
            qs = jnp.concatenate(
                [qbuf[:, (3 * g + i) * HD : (3 * g + i + 1) * HD] for i in range(3)], axis=0
            )
            sc = lax.dot_general(qs, kwin[:, cols], NT, preferred_element_type=F32)
            sc = jnp.where(seen3 < -1.0, NEGATIVE, sc * (1.0 / math.sqrt(HD)))
            w = jnp.exp(sc - jnp.max(sc, axis=-1, keepdims=True))
            total = jnp.sum(w, axis=-1, keepdims=True)
            o = jnp.dot(w.astype(BF16), vwin[:, cols], preferred_element_type=F32)
            o = (o / total).astype(BF16)
            for i in range(3):
                hbuf[y, :, (3 * g + i) * HD : (3 * g + i + 1) * HD] = o[i * 64 : (i + 1) * 64]
    hy = [
        go(hbuf.at[y], hbuf.at[y], hy_s.at[d], hy_r.at[d], pdev[(d, 0)]) for d in (1, 3, 2)
    ]

    with jax.named_scope("wait_columns"):
        own_ow.wait()
        for c in owz:
            c.wait_recv()
        owx = [
            go(owbuf.at[:, x], owbuf.at[:, x], owx_s.at[d], owx_r.at[d], pdev[(0, d)])
            for d in (1, 3, 2)
        ]
        for c in owx:
            c.wait_recv()
    with jax.named_scope("columns"):
        col, row = iota((384, 512), 0), iota((384, 512), 1)
        pick = jnp.where(row == lax.div(col, 12) * 16 + lax.rem(col, 12), 1.0, 0.0).astype(BF16)
        wc[...] = jnp.dot(
            pick, owbuf[...].reshape(512, 768), preferred_element_type=F32
        ).astype(BF16)

    with jax.named_scope("wait_heads"):
        for c in hy:
            c.wait_recv()
    with jax.named_scope("project"):
        po = lax.dot_general(hbuf[...].reshape(256, 768), wc[...], NT, preferred_element_type=F32)
        part[...] = po.reshape(4, 2, 32, 384)
    rs = []
    for d in (1, 3, 2):
        yd = up(y, d, NY)
        for i, hd in enumerate((h, 1 - h)):
            rs.append(
                go(part.at[yd, hd], rbuf.at[y, h], rs_s.at[i, d], rs_r.at[i, d], (seq_of(yd, z, x), hd))
            )
    rs.append(go(part.at[y, 1 - h], rbuf.at[y, h], rs_s.at[1, 0], rs_r.at[1, 0], sib))
    rbuf[y, h] = part[y, h]
    with jax.named_scope("cache_plane"):
        own_cache.wait()
        for c in cz:
            c.wait_recv()
        cp = [
            go(
                cmid_ref.at[:, up(y, at[0], NY), up(x, at[1], NX)], chand_ref.at[y, :, x],
                cp_s.at[i], cp_r.at[i], pdev[at],
            )
            for i, at in enumerate(plane)
        ]
        cp_own = here(cmid_ref.at[:, y, x], chand_ref.at[y, :, x])
    with jax.named_scope("wait_projected"):
        for c in rs:
            c.wait_recv()
    with jax.named_scope("norm"):
        own_res.wait()
        attn = [rbuf[j, 0] + rbuf[j, 1] for j in range(NY)]
        mixed = resbuf[...].astype(F32) + jnp.concatenate(attn, axis=1)
        ms = jnp.mean(mixed * mixed, axis=-1, keepdims=True)
        xb[0] = (mixed * lax.rsqrt(ms + EPSILON) * gain_ref[...]).astype(BF16)
    xz = {
        d: go(xb.at[0], xb.at[SLOT[NZ - d]], xz_s.at[d], xz_r.at[d], zdev[d])
        for d in [NZ - o for o in OFF[1:]]
    }

    with jax.named_scope("shared_weights"):
        own_sh.wait()
        for c in shp:
            c.wait_recv()
        sib_sh = go(shb.at[:, :, h], shb.at[:, :, h], sib_s.at[0], sib_r.at[0], sib)
        for c in rp:
            c.wait_recv()

    with jax.named_scope("choose"):
        lane = iota((128, COLS), 1)
        half = lax.div(lane, COLS // 2)
        expert = lax.rem(y + half, 2) * 32 + z * NX + lax.rem(lax.div(lane, ROWS), NX)
        row = iota((128, COLS), 0)
        of_rank = jnp.where(row == expert, 1.0, 0.0).astype(BF16)
        of_prob = jnp.where(row == expert + EXPERTS, 1.0, 0.0).astype(BF16)
        slot = lax.rem(iota((128, COLS), 1), ROWS)
        member = lax.div(row, 32) == lax.div(slot, CAP)
        number = lax.rem(slot, CAP).astype(F32)
        picks, weights = [], []
        for c in range(2):
            rpc = rpb[4 * c : 4 * c + 4].reshape(128, 128).astype(BF16)
            rank = jnp.dot(rpc, of_rank, preferred_element_type=F32)
            prob = jnp.dot(rpc, of_prob, preferred_element_type=F32)
            hit = member & (rank == number)
            picks.append(jnp.transpose(jnp.where(hit, 1.0, 0.0)).astype(BF16))
            weights.append(jnp.where(hit, prob, 0.0).astype(BF16))

    hops = [(p, d) for p in range(2) for d in (2, 1, 3, 0) if (p, d) != (0, 0)]
    sent = []
    for c in range(2):
        with jax.named_scope("wait_rows"):
            for o in OFF[4 * c : 4 * c + 4]:
                if o:
                    xz[NZ - o].wait_recv()
        with jax.named_scope("dispatch"):
            xc = xb[4 * c : 4 * c + 4].reshape(128, 1536)
            rows = jnp.dot(picks[c], xc, preferred_element_type=F32)
            for j in range(8):
                dsend[c, j] = rows[j * ROWS : (j + 1) * ROWS].astype(BF16)
            sent.append(
                [
                    go(
                        dsend.at[c, p * NX + up(x, d, NX)], drecv.at[c, p * NX + x],
                        d_s.at[c, i], d_r.at[c, i], pdev[(p, d)],
                    )
                    for i, (p, d) in enumerate(hops)
                ]
            )
            drecv[c, x] = dsend[c, x]

    with jax.named_scope("exchange_sibling"):
        for c in ex:
            c.wait_recv()
        sib_g = go(wgb.at[1, rows_g], wgb.at[1, rows_g], sib_s.at[1], sib_r.at[1], sib)
        sib_d = go(wdb.at[1, rows_d], wdb.at[1, rows_d], sib_s.at[2], sib_r.at[2], sib)
    with jax.named_scope("shared"):
        sib_sh.wait_recv()
        xs = xb[...].reshape(256, 1536)
        sh = shb[...].reshape(512, 1536)
        both = lax.dot_general(xs, sh, NT, preferred_element_type=F32)
        act = silu(pltpu.roll(both, 8, 1)) * pltpu.roll(both, 4, 1)
        live = lax.rem(lax.div(iota((256, 512), 1), 4), 4) == 2
        act = jnp.where(live, act, 0.0).astype(BF16)
        shared = jnp.dot(act, sh, preferred_element_type=F32)
    with jax.named_scope("wait_exchange"):
        own_wg.wait()
        own_wd.wait()
        sib_g.wait_recv()
        sib_d.wait_recv()

    back = []
    for c in range(2):
        with jax.named_scope("wait_dispatch"):
            for m in sent[c]:
                m.wait_recv()
        with jax.named_scope("experts"):
            rows = jnp.concatenate([drecv[c, j].astype(F32) for j in range(8)], axis=0).astype(BF16)
            acc = None
            for j in range(2):
                gu = jnp.dot(rows, wgb[j], preferred_element_type=F32)
                a = (silu(gu[:, :256]) * gu[:, 256:]).astype(BF16)
                o = jnp.dot(a, wdb[j], preferred_element_type=F32)
                acc = o if acc is None else acc + o
            for j in range(8):
                rsend[c, j] = acc[j * ROWS : (j + 1) * ROWS].astype(BF16)
            back.append(
                [
                    go(
                        rsend.at[c, p * NX + up(x, NX - d, NX)], rrecv.at[c, p * NX + x],
                        r_s.at[c, i], r_r.at[c, i],
                        pdev[((NY - p) % NY, (NX - d) % NX)],
                    )
                    for i, (p, d) in enumerate(hops)
                ]
            )
            rrecv[c, x] = rsend[c, x]
    red = []
    for c in range(2):
        with jax.named_scope("wait_return"):
            for m in back[c]:
                m.wait_recv()
        with jax.named_scope("combine"):
            rows = jnp.concatenate([rrecv[c, j].astype(F32) for j in range(8)], axis=0).astype(BF16)
            tot = shared[128 * c : 128 * c + 128] + jnp.dot(
                weights[c], rows, preferred_element_type=F32
            )
            pz[4 * c : 4 * c + 4] = tot.astype(BF16).reshape(4, 32, 1536)
            for o in OFF[4 * c : 4 * c + 4]:
                if o:
                    red.append(
                        go(pz.at[SLOT[o]], racc.at[SLOT[NZ - o]], z_s.at[o], z_r.at[o], zdev[o])
                    )
    racc[0] = pz[0]
    with jax.named_scope("wait_sum"):
        for c in red:
            c.wait_recv()
    out = mixed
    for j in range(NZ):
        out = out + racc[j].astype(F32)
    out_ref[...] = out.astype(BF16)
    with jax.named_scope("drain"):
        cp_own.wait()
        for c in cp:
            c.wait_recv()
        for c in pending:
            c.wait_send()


def shards(
    queries, key_vectors, value_vectors, lengths, out_weight, residual, norm_gain, route_ids,
    route_logits, shared_gate_up, shared_down, expert_gate_up, expert_down, cache_blocks, block_table,
):
    hbm, vmem = pl.BlockSpec(memory_space=pltpu.HBM), pl.BlockSpec(memory_space=pltpu.VMEM)
    dma = pltpu.SemaphoreType.DMA
    lens = jnp.pad(lengths.astype(F32), (0, 64)).reshape(1, 128)
    ow = jnp.pad(out_weight.T, ((0, 4), (0, 0)))
    sh = jnp.concatenate(
        [
            jnp.transpose(shared_gate_up, (1, 2, 0)).reshape(8, 1536),
            shared_down,
            jnp.zeros((4, 1536), BF16),
        ],
        axis=0,
    )
    wg = expert_gate_up.reshape(1536, 512)
    wd = expert_down.reshape(256, 1536)
    cache = cache_blocks.reshape(NY, NZ, NX, 8, 2, HD)
    sds = jax.ShapeDtypeStruct
    layer_out, _, chand = pl.pallas_call(
        layer_kernel,
        out_shape=(
            sds((32, 1536), BF16),
            sds((NZ, NY, NX, 8, 2, HD), BF16),
            sds((NY, NZ, NX, 8, 2, HD), BF16),
        ),
        in_specs=[hbm, hbm, hbm, vmem, hbm, hbm, vmem, vmem, vmem, hbm, hbm, hbm, hbm],
        out_specs=(vmem, hbm, hbm),
        scratch_shapes=[
            pltpu.VMEM((64, 768), BF16),
            pltpu.VMEM((320, 256), BF16),
            pltpu.VMEM((320, 256), BF16),
            pltpu.VMEM((32, 1536), BF16),
            pltpu.VMEM((NZ, NX, 16, 768), BF16),
            pltpu.VMEM((384, 768), BF16),
            pltpu.VMEM((NY, 64, 768), BF16),
            pltpu.VMEM((NY, 2, 32, 384), F32),
            pltpu.VMEM((NY, 2, 32, 384), F32),
            pltpu.VMEM((NZ, 32, 1536), BF16),
            pltpu.VMEM((NZ, 32, 128), F32),
            pltpu.VMEM((NY, NX, 2, 16, 1536), BF16),
            pltpu.VMEM((2, 1536, 512), BF16),
            pltpu.VMEM((2, 256, 1536), BF16),
            pltpu.VMEM((2, 8, ROWS, 1536), BF16),
            pltpu.VMEM((2, 8, ROWS, 1536), BF16),
            pltpu.VMEM((2, 8, ROWS, 1536), BF16),
            pltpu.VMEM((2, 8, ROWS, 1536), BF16),
            pltpu.VMEM((NZ, 32, 1536), BF16),
            pltpu.VMEM((NZ, 32, 1536), BF16),
            dma((2, 4)), dma((2, 4)),
            dma((8,)), dma((8,)),
            dma((4,)), dma((4,)),
            dma((8,)), dma((8,)),
            dma((15,)), dma((15,)),
            dma((8,)), dma((8,)),
            dma((15,)), dma((15,)),
            dma((2,)), dma((2,)),
            dma((3,)), dma((3,)),
            dma((4,)), dma((4,)),
            dma((2, 4)), dma((2, 4)),
            dma((8,)), dma((8,)),
            dma((2, 7)), dma((2, 7)),
            dma((2, 7)), dma((2, 7)),
            dma((8,)), dma((8,)),
            dma((10,)),
        ],
        compiler_params=pltpu.CompilerParams(
            collective_id=0, has_side_effects=True, vmem_limit_bytes=56 << 20
        ),
        name="layer",
    )(
        queries, key_vectors, value_vectors, lens, ow, residual, norm_gain.reshape(1, 1536),
        route_ids, route_logits, sh, wg, wd, cache,
    )
    cache_out = jnp.take(
        chand.reshape(128, 1, 8, 2, HD), block_table, axis=0, mode="clip"
    )
    return layer_out, cache_out


def solution(mesh):
    in_specs = (
        P("seq", "head"),
        P("seq", "head"),
        P("seq", "head"),
        P(),
        P("head", "seq"),
        P(("seq", "head"), None),
        P(),
        P(("seq", "head"), None),
        P(("seq", "head"), None),
        P(None, None, ("seq", "head")),
        P(("seq", "head"), None),
        P("seq", None, None, None),
        P("seq", None, None),
        P("seq", None, None, "head", None),
        P(),
    )
    out_specs = (P(("seq", "head"), None), P(None, "seq", None, "head", None))
    return jax.shard_map(shards, mesh=mesh, in_specs=in_specs, out_specs=out_specs, check_vma=False)
```

```python
import functools
import math

import jax
import jax.numpy as jnp
from jax import lax
from jax.experimental import pallas as pl
from jax.experimental.pallas import tpu as pltpu
from jax.sharding import PartitionSpec as P

MESH = pl.DeviceIdType.MESH
HD = 128
NY, NZ, NX = 4, 8, 4
TOP = 6
CAP = 6
EXPERTS = 64
NEGATIVE = -1e30
EPSILON = 1e-05
F32 = jnp.float32
BF16 = jnp.bfloat16
ZORDER = (1, 7, 2, 6, 3, 5, 4)
OFF = (0, 1, 4, 3, 7, 6, 2, 5)
SLOT = {o: k for k, o in enumerate(OFF)}
ROWS = 24
COLS = 8 * ROWS
NT = (((1,), (1,)), ((), ()))


def place():
    s = lax.axis_index("seq")
    h = lax.axis_index("head")
    y = lax.div(s, NZ * NX)
    z = lax.rem(lax.div(s, NX), NZ)
    x = lax.rem(s, NX)
    return s, h, y, z, x


def seq_of(y, z, x):
    return y * (NZ * NX) + z * NX + x


def up(i, by, n):
    return lax.rem(i + by, n)


def rcopy(src, dst, ssem, rsem, dev):
    return pltpu.make_async_remote_copy(
        src_ref=src, dst_ref=dst, send_sem=ssem, recv_sem=rsem, device_id=dev, device_id_type=MESH
    )


def iota(shape, axis):
    return lax.broadcasted_iota(jnp.int32, shape, axis)


def silu(v):
    return v / (1.0 + jnp.exp(-v))


def routing_table(ids, logits):
    top = jnp.max(logits, axis=0, keepdims=True)
    e = jnp.exp(logits - top)
    probs = e / jnp.sum(e, axis=0, keepdims=True)
    row = iota((128, 32), 0)
    named = jnp.zeros((128, 32), F32)
    weight = jnp.zeros((128, 32), F32)
    for r in range(TOP):
        idr = jnp.broadcast_to(ids[r : r + 1, :], (128, 32))
        named = named + jnp.where(row == idr, 1.0, 0.0)
        weight = weight + jnp.where(row - EXPERTS == idr, probs[r : r + 1, :], 0.0)
    before = jnp.where(iota((32, 32), 0) < iota((32, 32), 1), 1.0, 0.0)
    rank = jnp.dot(named.astype(BF16), before.astype(BF16), preferred_element_type=F32)
    table = jnp.where(row < EXPERTS, jnp.where(named > 0.5, rank, -1.0), weight)
    return jnp.transpose(table)


def layer_kernel(
    q_hbm, k_hbm, v_hbm, len_ref, ow_ref, res_hbm, gain_ref, ids_ref, log_ref,
    sgu_ref, sd_ref, wg_hbm, wd_hbm, cache_hbm,
    out_ref, cmid_ref, chand_ref,
    qbuf, kwin, vwin, resbuf, owpad, owbuf, wc, hbuf, part, rbuf, xb, rpb, shpad, shb, raw, wgb, wdb,
    relay_g, relay_d, dsend, drecv, rsend, rrecv, pz, racc,
    kv_s, kv_r, owz_s, owz_r, owx_s, owx_r, rp_s, rp_r, shy_s, shy_r, shx_s, shx_r, cz_s, cz_r, cp_s, cp_r,
    e1_s, e1_r, e2_s, e2_r, sib_s, sib_r, hy_s, hy_r, rs_s, rs_r, xz_s, xz_r, d_s, d_r, r_s, r_r, z_s, z_r, loc,
):
    s, h, y, z, x = place()
    seqs = NY * NZ * NX
    zdev = {d: (seq_of(y, up(z, d, NZ), x), h) for d in range(1, NZ)}
    plane = [
        (dy, dx) for dy in range(NY) for dx in range(NX) if (dy, dx) != (0, 0)
    ]
    pdev = {at: (seq_of(up(y, at[0], NY), z, up(x, at[1], NX)), h) for at in plane}
    sib = (s, 1 - h)
    cross = [(seq_of(up(y, dy, NY), z, x), 1 - h) for dy in (1, 2, 3)]
    ahead = [(lax.rem(s + by, seqs), h) for by in range(1, 5)]
    behind = [(lax.rem(s + seqs - by, seqs), h) for by in range(1, 5)]

    local = []

    def here(src, dst):
        copy = pltpu.make_async_copy(src, dst, loc.at[len(local)])
        copy.start()
        local.append(copy)
        return copy

    own_wg = here(wg_hbm, raw)
    own_k = here(k_hbm, kwin.at[pl.ds(256, 64)])
    own_v = here(v_hbm, vwin.at[pl.ds(256, 64)])
    own_q = here(q_hbm, qbuf)
    own_cache = here(cache_hbm.at[:, z], cmid_ref.at[z])
    own_res = here(res_hbm, resbuf)
    own_wd = here(wd_hbm, wdb.at[0])
    peers = list(zdev.values()) + list(pdev.values()) + [sib] + cross + ahead + behind
    barrier = pltpu.get_barrier_semaphore()
    for dev in peers:
        pl.semaphore_signal(barrier, inc=1, device_id=dev, device_id_type=MESH)

    with jax.named_scope("pack"):
        owpad[...] = jnp.concatenate(
            [ow_ref[...].astype(F32), jnp.zeros((4, 768), F32)], axis=0
        ).astype(BF16)
        owbuf[z, x] = owpad[...]
        shpad[...] = jnp.concatenate(
            [
                sgu_ref[...].astype(F32).reshape(8, 1536),
                sd_ref[...].astype(F32),
                jnp.zeros((4, 1536), F32),
            ],
            axis=0,
        ).astype(BF16)
        shb[y, x, h] = shpad[...]
    with jax.named_scope("routing"):
        rpb[0] = routing_table(ids_ref[...], log_ref[...])
    with jax.named_scope("gate_up"):
        own_wg.wait()
        wgb[0, :, 0:256] = raw[:, 0, :]
        wgb[0, :, 256:512] = raw[:, 1, :]
    with jax.named_scope("enter"):
        pl.semaphore_wait(barrier, len(peers))

    pending = []

    def go(*args):
        copy = rcopy(*args)
        copy.start()
        pending.append(copy)
        return copy

    kv = []
    for by in range(1, 5):
        rows = pl.ds(64 * (4 - by), 64)
        kv.append(go(k_hbm, kwin.at[rows], kv_s.at[0, by - 1], kv_r.at[0, by - 1], ahead[by - 1]))
        kv.append(go(v_hbm, vwin.at[rows], kv_s.at[1, by - 1], kv_r.at[1, by - 1], ahead[by - 1]))
    owz = [go(owpad, owbuf.at[z, x], owz_s.at[d], owz_r.at[d], zdev[d]) for d in ZORDER]
    rp = [
        go(rpb.at[0], rpb.at[SLOT[NZ - d]], rp_s.at[d], rp_r.at[d], zdev[d]) for d in ZORDER
    ]
    shy = [
        go(shpad, shb.at[y, x, h], shy_s.at[d], shy_r.at[d], pdev[(d, 0)]) for d in (1, 3, 2)
    ]
    sides = (pdev[(1, 0)], pdev[(3, 0)])
    rows_g, rows_d = pl.ds(h * 768, 768), pl.ds(h * 128, 128)

    def piece(i):
        if i < 4:
            return pl.ds(h * 768 + i * 192, 192)
        return pl.ds(h * 128 + (i - 4) * 64, 64)

    def first_hop(i):
        sem = e1_s.at[i], e1_r.at[i], sides[i % 2]
        if i < 4:
            return go(wgb.at[0, piece(i)], relay_g.at[i], *sem)
        return go(wd_hbm.at[piece(i)], relay_d.at[i - 4], *sem)

    def second_hop(i, arrived):
        arrived.wait_recv()
        sem = e2_s.at[i], e2_r.at[i], sides[i % 2]
        if i < 4:
            return go(relay_g.at[i], wgb.at[1, piece(i)], *sem)
        return go(relay_d.at[i - 4], wdb.at[1, piece(i)], *sem)

    ex1 = [first_hop(i) for i in range(4)]

    with jax.named_scope("visible"):
        upper = jnp.where(iota((64, 64), 0) <= iota((64, 64), 1), 1.0, 0.0).astype(BF16)
        lens = jnp.broadcast_to(len_ref[...].astype(F32).reshape(1, 64), (16, 64)).astype(BF16)
        ends = jnp.dot(lens, upper, preferred_element_type=F32)[0:1, :]
        qpos = (s * 64 + iota((64, 64), 0)).astype(F32)
        first = jnp.max(jnp.where(ends <= qpos, ends, 0.0), axis=-1, keepdims=True)
        kpos = (s * 64 - 256 + iota((64, 320), 1)).astype(F32)
        qcol = (s * 64 + iota((64, 320), 0)).astype(F32)
        seen = jnp.where((kpos >= first) & (kpos <= qcol), 0.0, NEGATIVE)
        seen3 = jnp.concatenate([seen, seen, seen], axis=0)

    with jax.named_scope("wait_keys"):
        own_k.wait()
        own_v.wait()
        own_q.wait()
        for c in kv:
            c.wait_recv()
        for c in owz:
            c.wait_recv()
    owx = [
        go(owbuf.at[:, x], owbuf.at[:, x], owx_s.at[d], owx_r.at[d], pdev[(0, d)])
        for d in (1, 3, 2)
    ]
    cz = [
        go(cache_hbm.at[:, up(z, d, NZ)], cmid_ref.at[z], cz_s.at[d], cz_r.at[d], zdev[d])
        for d in ZORDER
    ]
    with jax.named_scope("attention"):
        for g in range(2):
            cols = slice(g * HD, (g + 1) * HD)
            qs = jnp.concatenate(
                [qbuf[:, (3 * g + i) * HD : (3 * g + i + 1) * HD] for i in range(3)], axis=0
            )
            sc = lax.dot_general(qs, kwin[:, cols], NT, preferred_element_type=F32)
            sc = jnp.where(seen3 < -1.0, NEGATIVE, sc * (1.0 / math.sqrt(HD)))
            w = jnp.exp(sc - jnp.max(sc, axis=-1, keepdims=True))
            total = jnp.sum(w, axis=-1, keepdims=True)
            o = jnp.dot(w.astype(BF16), vwin[:, cols], preferred_element_type=F32)
            o = (o / total).astype(BF16)
            for i in range(3):
                hbuf[y, :, (3 * g + i) * HD : (3 * g + i + 1) * HD] = o[i * 64 : (i + 1) * 64]
    hy = [
        go(hbuf.at[y], hbuf.at[y], hy_s.at[d], hy_r.at[d], pdev[(d, 0)]) for d in (1, 3, 2)
    ]

    with jax.named_scope("wait_columns"):
        for c in owx:
            c.wait_recv()
        for c in shy:
            c.wait_recv()
    shx = [
        go(shb.at[:, x, h], shb.at[:, x, h], shx_s.at[d], shx_r.at[d], pdev[(0, d)])
        for d in (1, 3, 2)
    ]
    with jax.named_scope("columns"):
        col, row = iota((384, 512), 0), iota((384, 512), 1)
        pick = jnp.where(row == lax.div(col, 12) * 16 + lax.rem(col, 12), 1.0, 0.0).astype(BF16)
        wc[...] = jnp.dot(
            pick, owbuf[...].reshape(512, 768), preferred_element_type=F32
        ).astype(BF16)

    with jax.named_scope("wait_heads"):
        for c in hy:
            c.wait_recv()
    with jax.named_scope("project"):
        po = lax.dot_general(hbuf[...].reshape(256, 768), wc[...], NT, preferred_element_type=F32)
        part[...] = po.reshape(4, 2, 32, 384).astype(BF16)
    rs = []
    for d in (1, 3, 2):
        yd = up(y, d, NY)
        for i, hd in enumerate((h, 1 - h)):
            rs.append(
                go(part.at[yd, hd], rbuf.at[y, h], rs_s.at[i, d], rs_r.at[i, d], (seq_of(yd, z, x), hd))
            )
    rs.append(go(part.at[y, 1 - h], rbuf.at[y, h], rs_s.at[1, 0], rs_r.at[1, 0], sib))
    rbuf[y, h] = part[y, h]
    with jax.named_scope("wait_projected"):
        for c in rs:
            c.wait_recv()
    with jax.named_scope("norm"):
        own_res.wait()
        attn = [rbuf[j, 0].astype(F32) + rbuf[j, 1].astype(F32) for j in range(NY)]
        mixed = resbuf[...].astype(F32) + jnp.concatenate(attn, axis=1)
        ms = jnp.mean(mixed * mixed, axis=-1, keepdims=True)
        xb[0] = (mixed * lax.rsqrt(ms + EPSILON) * gain_ref[...].reshape(1, 1536)).astype(BF16)
    xz = {
        d: go(xb.at[0], xb.at[SLOT[NZ - d]], xz_s.at[d], xz_r.at[d], zdev[d])
        for d in [NZ - o for o in OFF[1:]]
    }

    with jax.named_scope("relay"):
        ex2 = [second_hop(i, ex1[i]) for i in range(4)]
        ex1 += [first_hop(i) for i in range(4, 6)]
    with jax.named_scope("shared_weights"):
        for c in shx:
            c.wait_recv()
        sib_sh = go(shb.at[:, :, h], shb.at[:, :, h], sib_s.at[0], sib_r.at[0], sib)
        for c in rp:
            c.wait_recv()

    with jax.named_scope("choose"):
        lane = iota((128, COLS), 1)
        half = lax.div(lane, COLS // 2)
        expert = lax.rem(y + half, 2) * 32 + z * NX + lax.rem(lax.div(lane, ROWS), NX)
        row = iota((128, COLS), 0)
        of_rank = jnp.where(row == expert, 1.0, 0.0).astype(BF16)
        of_prob = jnp.where(row == expert + EXPERTS, 1.0, 0.0).astype(BF16)
        slot = lax.rem(iota((128, COLS), 1), ROWS)
        member = lax.div(row, 32) == lax.div(slot, CAP)
        number = lax.rem(slot, CAP).astype(F32)
        picks, weights = [], []
        for c in range(2):
            rpc = rpb[4 * c : 4 * c + 4].reshape(128, 128).astype(BF16)
            rank = jnp.dot(rpc, of_rank, preferred_element_type=F32)
            prob = jnp.dot(rpc, of_prob, preferred_element_type=F32)
            hit = member & (rank == number)
            picks.append(jnp.transpose(jnp.where(hit, 1.0, 0.0)).astype(BF16))
            weights.append(jnp.where(hit, prob, 0.0).astype(BF16))

    turn = 1 + 2 * lax.rem(x, 2)

    def to_expert(p, d):
        return pdev[(0, d)] if p == 0 else (seq_of(up(y, turn, NY), z, up(x, d, NX)), h)

    def to_source(p, d):
        xs = up(x, NX - d, NX)
        if p == 0:
            return pdev[(0, NX - d)]
        return (seq_of(up(y, 3 - 2 * lax.rem(xs, 2), NY), z, xs), h)

    hops = [(p, d) for p in range(2) for d in (2, 1, 3, 0) if (p, d) != (0, 0)]
    sent = []
    for c in range(2):
        with jax.named_scope("wait_rows"):
            for o in OFF[4 * c : 4 * c + 4]:
                if o:
                    xz[NZ - o].wait_recv()
        with jax.named_scope("dispatch"):
            xc = xb[4 * c : 4 * c + 4].reshape(128, 1536)
            rows = jnp.dot(picks[c], xc, preferred_element_type=F32)
            for j in range(8):
                dsend[c, j] = rows[j * ROWS : (j + 1) * ROWS].astype(BF16)
            sent.append(
                [
                    go(
                        dsend.at[c, p * NX + up(x, d, NX)], drecv.at[c, p * NX + x],
                        d_s.at[c, i], d_r.at[c, i], to_expert(p, d),
                    )
                    for i, (p, d) in enumerate(hops)
                ]
            )
            drecv[c, x] = dsend[c, x]
        if c == 0:
            with jax.named_scope("relay_down"):
                ex2 += [second_hop(i, ex1[i]) for i in range(4, 6)]

    with jax.named_scope("exchange_sibling"):
        for c in ex2:
            c.wait_recv()
        sib_g = go(wgb.at[1, rows_g], wgb.at[1, rows_g], sib_s.at[1], sib_r.at[1], sib)
        sib_d = go(wdb.at[1, rows_d], wdb.at[1, rows_d], sib_s.at[2], sib_r.at[2], sib)
    with jax.named_scope("shared"):
        sib_sh.wait_recv()
        xs = xb[...].reshape(256, 1536)
        sh = shb[...].reshape(512, 1536)
        both = lax.dot_general(xs, sh, NT, preferred_element_type=F32)
        act = silu(pltpu.roll(both, 8, 1)) * pltpu.roll(both, 4, 1)
        live = lax.rem(lax.div(iota((256, 512), 1), 4), 4) == 2
        act = jnp.where(live, act, 0.0).astype(BF16)
        shared = jnp.dot(act, sh, preferred_element_type=F32)
    with jax.named_scope("wait_exchange"):
        own_wd.wait()
        sib_g.wait_recv()
        sib_d.wait_recv()

    back = []
    for c in range(2):
        with jax.named_scope("wait_dispatch"):
            for m in sent[c]:
                m.wait_recv()
        with jax.named_scope("experts"):
            rows = jnp.concatenate([drecv[c, j].astype(F32) for j in range(8)], axis=0).astype(BF16)
            acc = None
            for j in range(2):
                gu = jnp.dot(rows, wgb[j], preferred_element_type=F32)
                a = (silu(gu[:, :256]) * gu[:, 256:]).astype(BF16)
                o = jnp.dot(a, wdb[j], preferred_element_type=F32)
                acc = o if acc is None else acc + o
            for j in range(8):
                rsend[c, j] = acc[j * ROWS : (j + 1) * ROWS].astype(BF16)
            back.append(
                [
                    go(
                        rsend.at[c, p * NX + up(x, NX - d, NX)], rrecv.at[c, p * NX + x],
                        r_s.at[c, i], r_r.at[c, i], to_source(p, d),
                    )
                    for i, (p, d) in enumerate(hops)
                ]
            )
            rrecv[c, x] = rsend[c, x]
    red = []
    for c in range(2):
        with jax.named_scope("wait_return"):
            for m in back[c]:
                m.wait_recv()
        with jax.named_scope("combine"):
            rows = jnp.concatenate([rrecv[c, j].astype(F32) for j in range(8)], axis=0).astype(BF16)
            tot = shared[128 * c : 128 * c + 128] + jnp.dot(
                weights[c], rows, preferred_element_type=F32
            )
            pz[4 * c : 4 * c + 4] = tot.astype(BF16).reshape(4, 32, 1536)
            for o in OFF[4 * c : 4 * c + 4]:
                if o:
                    red.append(
                        go(pz.at[SLOT[o]], racc.at[SLOT[NZ - o]], z_s.at[o], z_r.at[o], zdev[o])
                    )
    racc[0] = pz[0]
    with jax.named_scope("cache_plane"):
        own_cache.wait()
        for c in cz:
            c.wait_recv()
        cp = [
            go(
                cmid_ref.at[:, up(y, at[0], NY), up(x, at[1], NX)], chand_ref.at[y, :, x],
                cp_s.at[i], cp_r.at[i], pdev[at],
            )
            for i, at in enumerate(plane)
        ]
        cp_own = here(cmid_ref.at[:, y, x], chand_ref.at[y, :, x])
    with jax.named_scope("wait_sum"):
        for c in red:
            c.wait_recv()
    out = mixed
    for j in range(NZ):
        out = out + racc[j].astype(F32)
    out_ref[...] = out.astype(BF16)
    with jax.named_scope("drain"):
        cp_own.wait()
        for c in cp:
            c.wait_recv()
        for c in pending:
            c.wait_send()


def shards(
    queries, key_vectors, value_vectors, lengths, out_weight, residual, norm_gain, route_ids,
    route_logits, shared_gate_up, shared_down, expert_gate_up, expert_down, cache_blocks, block_table,
):
    hbm, vmem = pl.BlockSpec(memory_space=pltpu.HBM), pl.BlockSpec(memory_space=pltpu.VMEM)
    dma = pltpu.SemaphoreType.DMA
    sgu = jnp.transpose(shared_gate_up, (1, 2, 0))
    wg = expert_gate_up.reshape(1536, 2, 256)
    wd = expert_down.reshape(256, 1536)
    cache = cache_blocks.reshape(NY, NZ, NX, 8, 2, HD)
    sds = jax.ShapeDtypeStruct
    layer_out, _, chand = pl.pallas_call(
        layer_kernel,
        out_shape=(
            sds((32, 1536), BF16),
            sds((NZ, NY, NX, 8, 2, HD), BF16),
            sds((NY, NZ, NX, 8, 2, HD), BF16),
        ),
        in_specs=[hbm, hbm, hbm, vmem, vmem, hbm, vmem, vmem, vmem, vmem, vmem, hbm, hbm, hbm],
        out_specs=(vmem, hbm, hbm),
        scratch_shapes=[
            pltpu.VMEM((64, 768), BF16),
            pltpu.VMEM((320, 256), BF16),
            pltpu.VMEM((320, 256), BF16),
            pltpu.VMEM((32, 1536), BF16),
            pltpu.VMEM((16, 768), BF16),
            pltpu.VMEM((NZ, NX, 16, 768), BF16),
            pltpu.VMEM((384, 768), BF16),
            pltpu.VMEM((NY, 64, 768), BF16),
            pltpu.VMEM((NY, 2, 32, 384), BF16),
            pltpu.VMEM((NY, 2, 32, 384), BF16),
            pltpu.VMEM((NZ, 32, 1536), BF16),
            pltpu.VMEM((NZ, 32, 128), F32),
            pltpu.VMEM((16, 1536), BF16),
            pltpu.VMEM((NY, NX, 2, 16, 1536), BF16),
            pltpu.VMEM((1536, 2, 256), BF16),
            pltpu.VMEM((2, 1536, 512), BF16),
            pltpu.VMEM((2, 256, 1536), BF16),
            pltpu.VMEM((4, 192, 512), BF16),
            pltpu.VMEM((2, 64, 1536), BF16),
            pltpu.VMEM((2, 8, ROWS, 1536), BF16),
            pltpu.VMEM((2, 8, ROWS, 1536), BF16),
            pltpu.VMEM((2, 8, ROWS, 1536), BF16),
            pltpu.VMEM((2, 8, ROWS, 1536), BF16),
            pltpu.VMEM((NZ, 32, 1536), BF16),
            pltpu.VMEM((NZ, 32, 1536), BF16),
            dma((2, 4)), dma((2, 4)),
            dma((8,)), dma((8,)),
            dma((4,)), dma((4,)),
            dma((8,)), dma((8,)),
            dma((4,)), dma((4,)),
            dma((4,)), dma((4,)),
            dma((8,)), dma((8,)),
            dma((15,)), dma((15,)),
            dma((6,)), dma((6,)),
            dma((6,)), dma((6,)),
            dma((3,)), dma((3,)),
            dma((4,)), dma((4,)),
            dma((2, 4)), dma((2, 4)),
            dma((8,)), dma((8,)),
            dma((2, 7)), dma((2, 7)),
            dma((2, 7)), dma((2, 7)),
            dma((8,)), dma((8,)),
            dma((8,)),
        ],
        compiler_params=pltpu.CompilerParams(
            collective_id=0, has_side_effects=True, vmem_limit_bytes=56 << 20
        ),
        name="layer",
    )(
        queries, key_vectors, value_vectors, lengths, out_weight.T, residual, norm_gain,
        route_ids.T, route_logits.T, sgu, shared_down, wg, wd, cache,
    )
    cache_out = jnp.take(
        chand.reshape(128, 1, 8, 2, HD), block_table, axis=0, mode="clip"
    )
    return layer_out, cache_out


def solution(mesh):
    in_specs = (
        P("seq", "head"),
        P("seq", "head"),
        P("seq", "head"),
        P(),
        P("head", "seq"),
        P(("seq", "head"), None),
        P(),
        P(("seq", "head"), None),
        P(("seq", "head"), None),
        P(None, None, ("seq", "head")),
        P(("seq", "head"), None),
        P("seq", None, None, None),
        P("seq", None, None),
        P("seq", None, None, "head", None),
        P(),
    )
    out_specs = (P(("seq", "head"), None), P(None, "seq", None, "head", None))
    return jax.shard_map(shards, mesh=mesh, in_specs=in_specs, out_specs=out_specs, check_vma=False)
```

```python
import functools
import math

import jax
import jax.numpy as jnp
from jax import lax
from jax.experimental import pallas as pl
from jax.experimental.pallas import tpu as pltpu
from jax.sharding import PartitionSpec as P

MESH = pl.DeviceIdType.MESH
HD = 128
NY, NZ, NX = 4, 8, 4
TOP = 6
CAP = 6
EXPERTS = 64
NEGATIVE = -1e30
EPSILON = 1e-05
F32 = jnp.float32
BF16 = jnp.bfloat16
ZORDER = (1, 7, 2, 6, 3, 5, 4)
OFF = (0, 1, 7, 4, 2, 6, 3, 5)
SLOT = {o: k for k, o in enumerate(OFF)}
ROWS = 24
COLS = 8 * ROWS
NT = (((1,), (1,)), ((), ()))


def place():
    s = lax.axis_index("seq")
    h = lax.axis_index("head")
    y = lax.div(s, NZ * NX)
    z = lax.rem(lax.div(s, NX), NZ)
    x = lax.rem(s, NX)
    return s, h, y, z, x


def seq_of(y, z, x):
    return y * (NZ * NX) + z * NX + x


def up(i, by, n):
    return lax.rem(i + by, n)


def rcopy(src, dst, ssem, rsem, dev):
    return pltpu.make_async_remote_copy(
        src_ref=src, dst_ref=dst, send_sem=ssem, recv_sem=rsem, device_id=dev, device_id_type=MESH
    )


def iota(shape, axis):
    return lax.broadcasted_iota(jnp.int32, shape, axis)


def silu(v):
    return v / (1.0 + jnp.exp(-v))


def routing_table(ids, logits):
    top = jnp.max(logits, axis=0, keepdims=True)
    e = jnp.exp(logits - top)
    probs = e / jnp.sum(e, axis=0, keepdims=True)
    row = iota((128, 32), 0)
    named = jnp.zeros((128, 32), F32)
    weight = jnp.zeros((128, 32), F32)
    for r in range(TOP):
        idr = jnp.broadcast_to(ids[r : r + 1, :], (128, 32))
        named = named + jnp.where(row == idr, 1.0, 0.0)
        weight = weight + jnp.where(row - EXPERTS == idr, probs[r : r + 1, :], 0.0)
    before = jnp.where(iota((32, 32), 0) < iota((32, 32), 1), 1.0, 0.0)
    rank = jnp.dot(named.astype(BF16), before.astype(BF16), preferred_element_type=F32)
    table = jnp.where(row < EXPERTS, jnp.where(named > 0.5, rank, -1.0), weight)
    return jnp.transpose(table)


def layer_kernel(
    q_hbm, k_hbm, v_hbm, len_ref, ow_ref, res_hbm, gain_ref, ids_ref, log_ref,
    sgu_ref, sd_ref, wg_hbm, wd_hbm, cache_hbm,
    out_ref, cmid_ref, chand_ref,
    qbuf, kwin, vwin, resbuf, owpad, owbuf, wc, hbuf, part, rbuf, xb, rpb, shpad, shb, raw, wgb, wdb,
    relay_g, relay_d, relay_z, dsend, drecv, rsend, rrecv, pz, racc,
    kv_s, kv_r, owz_s, owz_r, owx_s, owx_r, rp_s, rp_r, shy_s, shy_r, shx_s, shx_r, cz_s, cz_r, cp_s, cp_r,
    e1_s, e1_r, e2_s, e2_r, sib_s, sib_r, hy_s, hy_r, rs_s, rs_r, xz_s, xz_r, d_s, d_r, r_s, r_r, z_s, z_r, loc,
):
    s, h, y, z, x = place()
    seqs = NY * NZ * NX
    zdev = {d: (seq_of(y, up(z, d, NZ), x), h) for d in range(1, NZ)}
    plane = [
        (dy, dx) for dy in range(NY) for dx in range(NX) if (dy, dx) != (0, 0)
    ]
    pdev = {at: (seq_of(up(y, at[0], NY), z, up(x, at[1], NX)), h) for at in plane}
    sib = (s, 1 - h)
    cross = [(seq_of(up(y, dy, NY), z, x), 1 - h) for dy in (1, 2, 3)]
    ahead = [(lax.rem(s + by, seqs), h) for by in range(1, 5)]
    behind = [(lax.rem(s + seqs - by, seqs), h) for by in range(1, 5)]

    local = []

    def here(src, dst):
        copy = pltpu.make_async_copy(src, dst, loc.at[len(local)])
        copy.start()
        local.append(copy)
        return copy

    own_wg = here(wg_hbm, raw.at[0])
    own_k = here(k_hbm, kwin.at[pl.ds(256, 64)])
    own_v = here(v_hbm, vwin.at[pl.ds(256, 64)])
    own_q = here(q_hbm, qbuf)
    own_cache = here(cache_hbm.at[:, z], cmid_ref.at[z])
    own_res = here(res_hbm, resbuf)
    own_wd = here(wd_hbm, wdb.at[0])
    peers = list(zdev.values()) + list(pdev.values()) + [sib] + cross + ahead + behind
    barrier = pltpu.get_barrier_semaphore()
    for dev in peers:
        pl.semaphore_signal(barrier, inc=1, device_id=dev, device_id_type=MESH)

    with jax.named_scope("pack"):
        owpad[...] = jnp.concatenate(
            [ow_ref[...].astype(F32), jnp.zeros((4, 768), F32)], axis=0
        ).astype(BF16)
        owbuf[z, x] = owpad[...]
        shpad[...] = jnp.concatenate(
            [
                sgu_ref[...].astype(F32).reshape(8, 1536),
                sd_ref[...].astype(F32),
                jnp.zeros((4, 1536), F32),
            ],
            axis=0,
        ).astype(BF16)
        shb[y, x, h] = shpad[...]
    with jax.named_scope("routing"):
        rpb[0] = routing_table(ids_ref[...], log_ref[...])
    with jax.named_scope("enter"):
        pl.semaphore_wait(barrier, len(peers))

    pending = []

    def go(*args):
        copy = rcopy(*args)
        copy.start()
        pending.append(copy)
        return copy

    kv = []
    for by in range(1, 5):
        rows = pl.ds(64 * (4 - by), 64)
        kv.append(go(k_hbm, kwin.at[rows], kv_s.at[0, by - 1], kv_r.at[0, by - 1], ahead[by - 1]))
        kv.append(go(v_hbm, vwin.at[rows], kv_s.at[1, by - 1], kv_r.at[1, by - 1], ahead[by - 1]))
    owz = [go(owpad, owbuf.at[z, x], owz_s.at[d], owz_r.at[d], zdev[d]) for d in ZORDER]
    rp = [
        go(rpb.at[0], rpb.at[SLOT[NZ - d]], rp_s.at[d], rp_r.at[d], zdev[d]) for d in ZORDER
    ]
    shy = [
        go(shpad, shb.at[y, x, h], shy_s.at[d], shy_r.at[d], pdev[(d, 0)]) for d in (1, 3, 2)
    ]
    sides = (pdev[(1, 0)], pdev[(3, 0)])
    rows_g, rows_d = pl.ds(h * 768, 768), pl.ds(h * 128, 128)

    def piece(i):
        if i < 4:
            return pl.ds(h * 768 + i * 192, 192)
        return pl.ds(h * 128 + (i - 4) * 64, 64)

    def first_hop(i):
        sem = e1_s.at[i], e1_r.at[i], sides[i % 2]
        if i < 4:
            return go(wg_hbm.at[piece(i)], relay_g.at[i], *sem)
        return go(wd_hbm.at[piece(i)], relay_d.at[i - 4], *sem)

    def second_hop(i, arrived):
        arrived.wait_recv()
        sem = e2_s.at[i], e2_r.at[i], sides[i % 2]
        if i < 4:
            return go(relay_g.at[i], raw.at[1, piece(i)], *sem)
        return go(relay_d.at[i - 4], wdb.at[1, piece(i)], *sem)

    ex1 = [first_hop(i) for i in range(4)]

    with jax.named_scope("visible"):
        upper = jnp.where(iota((64, 64), 0) <= iota((64, 64), 1), 1.0, 0.0).astype(BF16)
        lens = jnp.broadcast_to(len_ref[...].astype(F32).reshape(1, 64), (16, 64)).astype(BF16)
        ends = jnp.dot(lens, upper, preferred_element_type=F32)[0:1, :]
        qpos = (s * 64 + iota((64, 64), 0)).astype(F32)
        first = jnp.max(jnp.where(ends <= qpos, ends, 0.0), axis=-1, keepdims=True)
        kpos = (s * 64 - 256 + iota((64, 320), 1)).astype(F32)
        qcol = (s * 64 + iota((64, 320), 0)).astype(F32)
        seen = jnp.where((kpos >= first) & (kpos <= qcol), 0.0, NEGATIVE)
        seen3 = jnp.concatenate([seen, seen, seen], axis=0)

    with jax.named_scope("wait_first_columns"):
        for c in owz:
            c.wait_recv()
    owx = {
        d: go(owbuf.at[:, x], owbuf.at[:, x], owx_s.at[d], owx_r.at[d], pdev[(0, d)])
        for d in (1, 3)
    }
    with jax.named_scope("wait_keys"):
        own_k.wait()
        own_v.wait()
        own_q.wait()
        for c in kv:
            c.wait_recv()
    with jax.named_scope("attention"):
        for g in range(2):
            cols = slice(g * HD, (g + 1) * HD)
            qs = jnp.concatenate(
                [qbuf[:, (3 * g + i) * HD : (3 * g + i + 1) * HD] for i in range(3)], axis=0
            )
            sc = lax.dot_general(qs, kwin[:, cols], NT, preferred_element_type=F32)
            sc = jnp.where(seen3 < -1.0, NEGATIVE, sc * (1.0 / math.sqrt(HD)))
            w = jnp.exp(sc - jnp.max(sc, axis=-1, keepdims=True))
            total = jnp.sum(w, axis=-1, keepdims=True)
            o = jnp.dot(w.astype(BF16), vwin[:, cols], preferred_element_type=F32)
            o = (o / total).astype(BF16)
            for i in range(3):
                hbuf[y, :, (3 * g + i) * HD : (3 * g + i + 1) * HD] = o[i * 64 : (i + 1) * 64]
    hy = [
        go(hbuf.at[y], hbuf.at[y], hy_s.at[d], hy_r.at[d], pdev[(d, 0)]) for d in (1, 3, 2)
    ]

    with jax.named_scope("gate_up"):
        own_wg.wait()
        wgb[0, 0:768, 0:256] = raw[0, 0:768, 0, :]
        wgb[0, 0:768, 256:512] = raw[0, 0:768, 1, :]
    with jax.named_scope("wait_columns"):
        left, right = up(x, 3, NX), up(x, 1, NX)
        owx[1].wait_recv()
        lower = owbuf.at[0:4, left]
        fwd = [go(lower, lower, owx_s.at[0], owx_r.at[0], pdev[(0, 1)])]
        owx[3].wait_recv()
        higher = owbuf.at[4:8, right]
        fwd.append(go(higher, higher, owx_s.at[2], owx_r.at[2], pdev[(0, 3)]))
        for c in shy:
            c.wait_recv()
    with jax.named_scope("relay_gate"):
        ex2 = [second_hop(i, ex1[i]) for i in range(2)]
    with jax.named_scope("wait_far_columns"):
        for c in fwd:
            c.wait_recv()
    shx = [
        go(shb.at[:, x, h], shb.at[:, x, h], shx_s.at[d], shx_r.at[d], pdev[(0, d)])
        for d in (1, 3, 2)
    ]
    with jax.named_scope("columns"):
        col, row = iota((384, 512), 0), iota((384, 512), 1)
        pick = jnp.where(row == lax.div(col, 12) * 16 + lax.rem(col, 12), 1.0, 0.0).astype(BF16)
        wc[...] = jnp.dot(
            pick, owbuf[...].reshape(512, 768), preferred_element_type=F32
        ).astype(BF16)

    with jax.named_scope("wait_heads"):
        for c in hy:
            c.wait_recv()
    with jax.named_scope("project"):
        po = lax.dot_general(hbuf[...].reshape(256, 768), wc[...], NT, preferred_element_type=F32)
        part[...] = po.reshape(4, 2, 32, 384).astype(BF16)
    rs = []
    for d in (1, 3, 2):
        yd = up(y, d, NY)
        for i, hd in enumerate((h, 1 - h)):
            rs.append(
                go(part.at[yd, hd], rbuf.at[y, h], rs_s.at[i, d], rs_r.at[i, d], (seq_of(yd, z, x), hd))
            )
    rs.append(go(part.at[y, 1 - h], rbuf.at[y, h], rs_s.at[1, 0], rs_r.at[1, 0], sib))
    rbuf[y, h] = part[y, h]
    with jax.named_scope("gate_up_rest"):
        wgb[0, 768:1536, 0:256] = raw[0, 768:1536, 0, :]
        wgb[0, 768:1536, 256:512] = raw[0, 768:1536, 1, :]
    with jax.named_scope("wait_projected"):
        for c in rs:
            c.wait_recv()
    with jax.named_scope("norm"):
        own_res.wait()
        attn = [rbuf[j, 0].astype(F32) + rbuf[j, 1].astype(F32) for j in range(NY)]
        mixed = resbuf[...].astype(F32) + jnp.concatenate(attn, axis=1)
        ms = jnp.mean(mixed * mixed, axis=-1, keepdims=True)
        xb[0] = (mixed * lax.rsqrt(ms + EPSILON) * gain_ref[...].reshape(1, 1536)).astype(BF16)
    xz = {
        d: go(xb.at[0], xb.at[SLOT[NZ - d]], xz_s.at[d], xz_r.at[d], zdev[d]) for d in (2, 6, 1, 7)
    }
    with jax.named_scope("relay"):
        ex2 += [second_hop(i, ex1[i]) for i in range(2, 4)]
        ex1 += [first_hop(i) for i in range(4, 6)]
    with jax.named_scope("choose"):
        for c in rp:
            c.wait_recv()
        lane = iota((128, COLS), 1)
        half = lax.div(lane, COLS // 2)
        expert = lax.rem(y + half, 2) * 32 + z * NX + lax.rem(lax.div(lane, ROWS), NX)
        row = iota((128, COLS), 0)
        of_rank = jnp.where(row == expert, 1.0, 0.0).astype(BF16)
        of_prob = jnp.where(row == expert + EXPERTS, 1.0, 0.0).astype(BF16)
        slot = lax.rem(iota((128, COLS), 1), ROWS)
        member = lax.div(row, 32) == lax.div(slot, CAP)
        number = lax.rem(slot, CAP).astype(F32)
        picks, weights = [], []
        for c in range(2):
            rpc = rpb[4 * c : 4 * c + 4].reshape(128, 128).astype(BF16)
            rank = jnp.dot(rpc, of_rank, preferred_element_type=F32)
            prob = jnp.dot(rpc, of_prob, preferred_element_type=F32)
            hit = member & (rank == number)
            picks.append(jnp.transpose(jnp.where(hit, 1.0, 0.0)).astype(BF16))
            weights.append(jnp.where(hit, prob, 0.0).astype(BF16))

    with jax.named_scope("wait_near_rows"):
        xz[2].wait_recv()
        low = pl.ds(0, 16)
        xz[4] = go(
            xb.at[SLOT[6], low], xb.at[SLOT[4], low], xz_s.at[4], xz_r.at[4], zdev[2]
        )
        xz[3] = go(xb.at[SLOT[6]], xb.at[SLOT[5]], xz_s.at[3], xz_r.at[3], zdev[1])
        xz[6].wait_recv()
        high = pl.ds(16, 16)
        xz[0] = go(
            xb.at[SLOT[2], high], xb.at[SLOT[4], high], xz_s.at[0], xz_r.at[0], zdev[6]
        )
        xz[5] = go(xb.at[SLOT[2]], xb.at[SLOT[3]], xz_s.at[5], xz_r.at[5], zdev[7])

    turn = 1 + 2 * lax.rem(x, 2)

    def to_expert(p, d):
        return pdev[(0, d)] if p == 0 else (seq_of(up(y, turn, NY), z, up(x, d, NX)), h)

    def to_source(p, d):
        xs = up(x, NX - d, NX)
        if p == 0:
            return pdev[(0, NX - d)]
        return (seq_of(up(y, 3 - 2 * lax.rem(xs, 2), NY), z, xs), h)

    hops = [(p, d) for p in range(2) for d in (2, 1, 3, 0) if (p, d) != (0, 0)]
    sent = []
    for c in range(2):
        with jax.named_scope("wait_rows"):
            for d in ((1, 7, 4, 0), (3, 5))[c]:
                xz[d].wait_recv()
        with jax.named_scope("dispatch"):
            xc = xb[4 * c : 4 * c + 4].reshape(128, 1536)
            rows = jnp.dot(picks[c], xc, preferred_element_type=F32)
            for j in range(8):
                dsend[c, j] = rows[j * ROWS : (j + 1) * ROWS].astype(BF16)
            sent.append(
                [
                    go(
                        dsend.at[c, p * NX + up(x, d, NX)], drecv.at[c, p * NX + x],
                        d_s.at[c, i], d_r.at[c, i], to_expert(p, d),
                    )
                    for i, (p, d) in enumerate(hops)
                ]
            )
            drecv[c, x] = dsend[c, x]
        if c == 0:
            with jax.named_scope("relay_down"):
                ex2 += [second_hop(i, ex1[i]) for i in range(4, 6)]
            with jax.named_scope("shared_weights"):
                for m in shx:
                    m.wait_recv()
                sib_sh = go(shb.at[:, :, h], shb.at[:, :, h], sib_s.at[0], sib_r.at[0], sib)

    cz = [
        go(cache_hbm.at[:, up(z, d, NZ)], cmid_ref.at[z], cz_s.at[d], cz_r.at[d], zdev[d])
        for d in ZORDER
    ]
    with jax.named_scope("exchange_sibling"):
        for c in ex2[:4]:
            c.wait_recv()
        sib_g = go(raw.at[1, rows_g], raw.at[1, rows_g], sib_s.at[1], sib_r.at[1], sib)
        for c in ex2[4:]:
            c.wait_recv()
        sib_d = go(wdb.at[1, rows_d], wdb.at[1, rows_d], sib_s.at[2], sib_r.at[2], sib)
    with jax.named_scope("shared"):
        sib_sh.wait_recv()
        xs = xb[...].reshape(256, 1536)
        sh = shb[...].reshape(512, 1536)
        both = lax.dot_general(xs, sh, NT, preferred_element_type=F32)
        act = silu(pltpu.roll(both, 8, 1)) * pltpu.roll(both, 4, 1)
        live = lax.rem(lax.div(iota((256, 512), 1), 4), 4) == 2
        act = jnp.where(live, act, 0.0).astype(BF16)
        shared = jnp.dot(act, sh, preferred_element_type=F32)
    with jax.named_scope("wait_exchange"):
        own_wd.wait()
        sib_g.wait_recv()
        wgb[1, :, 0:256] = raw[1, :, 0, :]
        wgb[1, :, 256:512] = raw[1, :, 1, :]
        sib_d.wait_recv()

    back = []
    for c in range(2):
        with jax.named_scope("wait_dispatch"):
            for m in sent[c]:
                m.wait_recv()
        with jax.named_scope("experts"):
            rows = jnp.concatenate([drecv[c, j].astype(F32) for j in range(8)], axis=0).astype(BF16)
            acc = None
            for j in range(2):
                gu = jnp.dot(rows, wgb[j], preferred_element_type=F32)
                a = (silu(gu[:, :256]) * gu[:, 256:]).astype(BF16)
                o = jnp.dot(a, wdb[j], preferred_element_type=F32)
                acc = o if acc is None else acc + o
            for j in range(8):
                rsend[c, j] = acc[j * ROWS : (j + 1) * ROWS].astype(BF16)
            back.append(
                [
                    go(
                        rsend.at[c, p * NX + up(x, NX - d, NX)], rrecv.at[c, p * NX + x],
                        r_s.at[c, i], r_r.at[c, i], to_source(p, d),
                    )
                    for i, (p, d) in enumerate(hops)
                ]
            )
            rrecv[c, x] = rsend[c, x]
    red = []
    for c in range(2):
        with jax.named_scope("wait_return"):
            for m in back[c]:
                m.wait_recv()
        with jax.named_scope("combine"):
            rows = jnp.concatenate([rrecv[c, j].astype(F32) for j in range(8)], axis=0).astype(BF16)
            tot = shared[128 * c : 128 * c + 128] + jnp.dot(
                weights[c], rows, preferred_element_type=F32
            )
            pz[4 * c : 4 * c + 4] = tot.astype(BF16).reshape(4, 32, 1536)
            for o in ((1, 7), (3, 5, 2, 6))[c]:
                red.append(
                    go(pz.at[SLOT[o]], racc.at[SLOT[NZ - o]], z_s.at[o], z_r.at[o], zdev[o])
                )
            if c == 0:
                by = go(pz.at[SLOT[4], high], relay_z, z_s.at[8], z_r.at[8], zdev[6])
                red.append(
                    go(pz.at[SLOT[4], low], racc.at[SLOT[4], low], z_s.at[4], z_r.at[4], zdev[4])
                )
        if c == 0:
            with jax.named_scope("relay_sum"):
                by.wait_recv()
                red.append(
                    go(relay_z, racc.at[SLOT[4], high], z_s.at[0], z_r.at[0], zdev[6])
                )
    racc[0] = pz[0]
    with jax.named_scope("cache_plane"):
        own_cache.wait()
        for c in cz:
            c.wait_recv()
        cp = [
            go(
                cmid_ref.at[:, up(y, at[0], NY), up(x, at[1], NX)], chand_ref.at[y, :, x],
                cp_s.at[i], cp_r.at[i], pdev[at],
            )
            for i, at in enumerate(plane)
        ]
        cp_own = here(cmid_ref.at[:, y, x], chand_ref.at[y, :, x])
    with jax.named_scope("wait_sum"):
        for c in red:
            c.wait_recv()
    out = mixed
    for j in range(NZ):
        out = out + racc[j].astype(F32)
    out_ref[...] = out.astype(BF16)
    with jax.named_scope("drain"):
        cp_own.wait()
        for c in cp:
            c.wait_recv()
        for c in pending:
            c.wait_send()


def shards(
    queries, key_vectors, value_vectors, lengths, out_weight, residual, norm_gain, route_ids,
    route_logits, shared_gate_up, shared_down, expert_gate_up, expert_down, cache_blocks, block_table,
):
    hbm, vmem = pl.BlockSpec(memory_space=pltpu.HBM), pl.BlockSpec(memory_space=pltpu.VMEM)
    dma = pltpu.SemaphoreType.DMA
    sgu = jnp.transpose(shared_gate_up, (1, 2, 0))
    wg = expert_gate_up.reshape(1536, 2, 256)
    wd = expert_down.reshape(256, 1536)
    cache = cache_blocks.reshape(NY, NZ, NX, 8, 2, HD)
    sds = jax.ShapeDtypeStruct
    layer_out, _, chand = pl.pallas_call(
        layer_kernel,
        out_shape=(
            sds((32, 1536), BF16),
            sds((NZ, NY, NX, 8, 2, HD), BF16),
            sds((NY, NZ, NX, 8, 2, HD), BF16),
        ),
        in_specs=[hbm, hbm, hbm, vmem, vmem, hbm, vmem, vmem, vmem, vmem, vmem, hbm, hbm, hbm],
        out_specs=(vmem, hbm, vmem),
        scratch_shapes=[
            pltpu.VMEM((64, 768), BF16),
            pltpu.VMEM((320, 256), BF16),
            pltpu.VMEM((320, 256), BF16),
            pltpu.VMEM((32, 1536), BF16),
            pltpu.VMEM((16, 768), BF16),
            pltpu.VMEM((NZ, NX, 16, 768), BF16),
            pltpu.VMEM((384, 768), BF16),
            pltpu.VMEM((NY, 64, 768), BF16),
            pltpu.VMEM((NY, 2, 32, 384), BF16),
            pltpu.VMEM((NY, 2, 32, 384), BF16),
            pltpu.VMEM((NZ, 32, 1536), BF16),
            pltpu.VMEM((NZ, 32, 128), F32),
            pltpu.VMEM((16, 1536), BF16),
            pltpu.VMEM((NY, NX, 2, 16, 1536), BF16),
            pltpu.VMEM((2, 1536, 2, 256), BF16),
            pltpu.VMEM((2, 1536, 512), BF16),
            pltpu.VMEM((2, 256, 1536), BF16),
            pltpu.VMEM((4, 192, 2, 256), BF16),
            pltpu.VMEM((2, 64, 1536), BF16),
            pltpu.VMEM((16, 1536), BF16),
            pltpu.VMEM((2, 8, ROWS, 1536), BF16),
            pltpu.VMEM((2, 8, ROWS, 1536), BF16),
            pltpu.VMEM((2, 8, ROWS, 1536), BF16),
            pltpu.VMEM((2, 8, ROWS, 1536), BF16),
            pltpu.VMEM((NZ, 32, 1536), BF16),
            pltpu.VMEM((NZ, 32, 1536), BF16),
            dma((2, 4)), dma((2, 4)),
            dma((8,)), dma((8,)),
            dma((4,)), dma((4,)),
            dma((8,)), dma((8,)),
            dma((4,)), dma((4,)),
            dma((4,)), dma((4,)),
            dma((8,)), dma((8,)),
            dma((15,)), dma((15,)),
            dma((6,)), dma((6,)),
            dma((6,)), dma((6,)),
            dma((3,)), dma((3,)),
            dma((4,)), dma((4,)),
            dma((2, 4)), dma((2, 4)),
            dma((8,)), dma((8,)),
            dma((2, 7)), dma((2, 7)),
            dma((2, 7)), dma((2, 7)),
            dma((9,)), dma((9,)),
            dma((8,)),
        ],
        compiler_params=pltpu.CompilerParams(
            collective_id=0, has_side_effects=True, vmem_limit_bytes=56 << 20
        ),
        name="layer",
    )(
        queries, key_vectors, value_vectors, lengths, out_weight.T, residual, norm_gain,
        route_ids.T, route_logits.T, sgu, shared_down, wg, wd, cache,
    )
    cache_out = jnp.take(
        chand.reshape(128, 1, 8, 2, HD), block_table, axis=0, mode="clip"
    )
    return layer_out, cache_out


def solution(mesh):
    in_specs = (
        P("seq", "head"),
        P("seq", "head"),
        P("seq", "head"),
        P(),
        P("head", "seq"),
        P(("seq", "head"), None),
        P(),
        P(("seq", "head"), None),
        P(("seq", "head"), None),
        P(None, None, ("seq", "head")),
        P(("seq", "head"), None),
        P("seq", None, None, None),
        P("seq", None, None),
        P("seq", None, None, "head", None),
        P(),
    )
    out_specs = (P(("seq", "head"), None), P(None, "seq", None, "head", None))
    return jax.shard_map(shards, mesh=mesh, in_specs=in_specs, out_specs=out_specs, check_vma=False)
```

```python
import functools
import math

import jax
import jax.numpy as jnp
from jax import lax
from jax.experimental import pallas as pl
from jax.experimental.pallas import tpu as pltpu
from jax.sharding import PartitionSpec as P

MESH = pl.DeviceIdType.MESH
HD = 128
NY, NZ, NX = 4, 8, 4
TOP = 6
CAP = 6
EXPERTS = 64
NEGATIVE = -1e30
EPSILON = 1e-05
F32 = jnp.float32
BF16 = jnp.bfloat16
ZORDER = (1, 7, 2, 6, 3, 5, 4)
OFF = (0, 3, 5, 4, 1, 7, 2, 6)
SLOT = {o: k for k, o in enumerate(OFF)}
ROWS = 24
COLS = 8 * ROWS
NT = (((1,), (1,)), ((), ()))


def place():
    s = lax.axis_index("seq")
    h = lax.axis_index("head")
    y = lax.div(s, NZ * NX)
    z = lax.rem(lax.div(s, NX), NZ)
    x = lax.rem(s, NX)
    return s, h, y, z, x


def seq_of(y, z, x):
    return y * (NZ * NX) + z * NX + x


def up(i, by, n):
    return lax.rem(i + by, n)


def rcopy(src, dst, ssem, rsem, dev):
    return pltpu.make_async_remote_copy(
        src_ref=src, dst_ref=dst, send_sem=ssem, recv_sem=rsem, device_id=dev, device_id_type=MESH
    )


def iota(shape, axis):
    return lax.broadcasted_iota(jnp.int32, shape, axis)


def silu(v):
    return v / (1.0 + jnp.exp(-v))


def routing_table(ids, logits):
    top = jnp.max(logits, axis=0, keepdims=True)
    e = jnp.exp(logits - top)
    probs = e / jnp.sum(e, axis=0, keepdims=True)
    row = iota((128, 32), 0)
    named = jnp.zeros((128, 32), F32)
    weight = jnp.zeros((128, 32), F32)
    for r in range(TOP):
        idr = jnp.broadcast_to(ids[r : r + 1, :], (128, 32))
        named = named + jnp.where(row == idr, 1.0, 0.0)
        weight = weight + jnp.where(row - EXPERTS == idr, probs[r : r + 1, :], 0.0)
    before = jnp.where(iota((32, 32), 0) < iota((32, 32), 1), 1.0, 0.0)
    rank = jnp.dot(named.astype(BF16), before.astype(BF16), preferred_element_type=F32)
    table = jnp.where(row < EXPERTS, jnp.where(named > 0.5, rank, -1.0), weight)
    return jnp.transpose(table)


def layer_kernel(
    q_hbm, k_hbm, v_hbm, len_ref, ow_ref, res_hbm, gain_ref, ids_ref, log_ref,
    sgu_ref, sd_ref, wg_hbm, wd_hbm, cache_hbm,
    out_ref, cmid_ref, chand_ref,
    qbuf, kwin, vwin, resbuf, owpad, owbuf, wc, hbuf, part, rbuf, xb, rpb, shpad, shb, raw, wgb, wdb,
    relay_g, relay_d, relay_x, relay_b, relay_3, relay_4, dsend, drecv, rsend, rrecv, pz, racc,
    kv_s, kv_r, owz_s, owz_r, owx_s, owx_r, rp_s, rp_r, shy_s, shy_r, shx_s, shx_r, cz_s, cz_r, cp_s, cp_r,
    e1_s, e1_r, e2_s, e2_r, sib_s, sib_r, hy_s, hy_r, rs_s, rs_r, xz_s, xz_r, d_s, d_r, q_s, q_r, r_s, r_r, z_s, z_r, loc,
):
    s, h, y, z, x = place()
    seqs = NY * NZ * NX
    zdev = {d: (seq_of(y, up(z, d, NZ), x), h) for d in range(1, NZ)}
    plane = [
        (dy, dx) for dy in range(NY) for dx in range(NX) if (dy, dx) != (0, 0)
    ]
    pdev = {at: (seq_of(up(y, at[0], NY), z, up(x, at[1], NX)), h) for at in plane}
    sib = (s, 1 - h)
    cross = [(seq_of(up(y, dy, NY), z, x), 1 - h) for dy in (1, 2, 3)]
    ahead = [(lax.rem(s + by, seqs), h) for by in range(1, 5)]
    behind = [(lax.rem(s + seqs - by, seqs), h) for by in range(1, 5)]

    local = []

    def here(src, dst):
        copy = pltpu.make_async_copy(src, dst, loc.at[len(local)])
        copy.start()
        local.append(copy)
        return copy

    own_wg = here(wg_hbm, raw.at[0])
    own_k = here(k_hbm, kwin.at[pl.ds(256, 64)])
    own_v = here(v_hbm, vwin.at[pl.ds(256, 64)])
    own_q = here(q_hbm, qbuf)
    own_cache = here(cache_hbm.at[:, z], cmid_ref.at[z])
    own_res = here(res_hbm, resbuf)
    own_wd = here(wd_hbm, wdb.at[0])
    peers = list(zdev.values()) + list(pdev.values()) + [sib] + cross + ahead + behind
    barrier = pltpu.get_barrier_semaphore()
    for dev in peers:
        pl.semaphore_signal(barrier, inc=1, device_id=dev, device_id_type=MESH)

    with jax.named_scope("pack"):
        owpad[...] = jnp.concatenate(
            [ow_ref[...].astype(F32), jnp.zeros((4, 768), F32)], axis=0
        ).astype(BF16)
        owbuf[z, x] = owpad[...]
        shpad[...] = jnp.concatenate(
            [
                sgu_ref[...].astype(F32).reshape(8, 1536),
                sd_ref[...].astype(F32),
                jnp.zeros((4, 1536), F32),
            ],
            axis=0,
        ).astype(BF16)
        shb[y, x, h] = shpad[...]
    with jax.named_scope("routing"):
        rpb[0] = routing_table(ids_ref[...], log_ref[...])
    with jax.named_scope("enter"):
        pl.semaphore_wait(barrier, len(peers))

    pending = []

    def go(*args):
        copy = rcopy(*args)
        copy.start()
        pending.append(copy)
        return copy

    kv = []
    for by in range(1, 5):
        rows = pl.ds(64 * (4 - by), 64)
        kv.append(go(k_hbm, kwin.at[rows], kv_s.at[0, by - 1], kv_r.at[0, by - 1], ahead[by - 1]))
        kv.append(go(v_hbm, vwin.at[rows], kv_s.at[1, by - 1], kv_r.at[1, by - 1], ahead[by - 1]))
    owz = [go(owpad, owbuf.at[z, x], owz_s.at[d], owz_r.at[d], zdev[d]) for d in ZORDER]
    shy = [
        go(shpad, shb.at[y, x, h], shy_s.at[d], shy_r.at[d], pdev[(d, 0)]) for d in (1, 3, 2)
    ]
    sides = (pdev[(1, 0)], pdev[(3, 0)])
    rows_g, rows_d = pl.ds(h * 768, 768), pl.ds(h * 128, 128)

    def piece(i):
        if i < 4:
            return pl.ds(h * 768 + i * 192, 192)
        return pl.ds(h * 128 + (i - 4) * 64, 64)

    def first_hop(i):
        sem = e1_s.at[i], e1_r.at[i], sides[i % 2]
        if i < 4:
            return go(wg_hbm.at[piece(i)], relay_g.at[i], *sem)
        return go(wd_hbm.at[piece(i)], relay_d.at[i - 4], *sem)

    def second_hop(i, arrived):
        arrived.wait_recv()
        sem = e2_s.at[i], e2_r.at[i], sides[i % 2]
        if i < 4:
            return go(relay_g.at[i], raw.at[1, piece(i)], *sem)
        return go(relay_d.at[i - 4], wdb.at[1, piece(i)], *sem)

    ex1 = [first_hop(i) for i in range(4)]

    with jax.named_scope("visible"):
        upper = jnp.where(iota((64, 64), 0) <= iota((64, 64), 1), 1.0, 0.0).astype(BF16)
        lens = jnp.broadcast_to(len_ref[...].astype(F32).reshape(1, 64), (16, 64)).astype(BF16)
        ends = jnp.dot(lens, upper, preferred_element_type=F32)[0:1, :]
        qpos = (s * 64 + iota((64, 64), 0)).astype(F32)
        first = jnp.max(jnp.where(ends <= qpos, ends, 0.0), axis=-1, keepdims=True)
        kpos = (s * 64 - 256 + iota((64, 320), 1)).astype(F32)
        qcol = (s * 64 + iota((64, 320), 0)).astype(F32)
        seen = jnp.where((kpos >= first) & (kpos <= qcol), 0.0, NEGATIVE)
        seen3 = jnp.concatenate([seen, seen, seen], axis=0)

    with jax.named_scope("wait_first_columns"):
        for c in owz:
            c.wait_recv()
    owx = {
        d: go(owbuf.at[:, x], owbuf.at[:, x], owx_s.at[d], owx_r.at[d], pdev[(0, d)])
        for d in (1, 3)
    }
    rp = [
        go(rpb.at[0], rpb.at[SLOT[NZ - d]], rp_s.at[d], rp_r.at[d], zdev[d]) for d in ZORDER
    ]
    with jax.named_scope("wait_keys"):
        own_k.wait()
        own_v.wait()
        own_q.wait()
        for c in kv:
            c.wait_recv()
    with jax.named_scope("attention"):
        for g in range(2):
            cols = slice(g * HD, (g + 1) * HD)
            qs = jnp.concatenate(
                [qbuf[:, (3 * g + i) * HD : (3 * g + i + 1) * HD] for i in range(3)], axis=0
            )
            sc = lax.dot_general(qs, kwin[:, cols], NT, preferred_element_type=F32)
            sc = jnp.where(seen3 < -1.0, NEGATIVE, sc * (1.0 / math.sqrt(HD)))
            w = jnp.exp(sc - jnp.max(sc, axis=-1, keepdims=True))
            total = jnp.sum(w, axis=-1, keepdims=True)
            o = jnp.dot(w.astype(BF16), vwin[:, cols], preferred_element_type=F32)
            o = (o / total).astype(BF16)
            for i in range(3):
                hbuf[y, :, (3 * g + i) * HD : (3 * g + i + 1) * HD] = o[i * 64 : (i + 1) * 64]
    hy = [
        go(hbuf.at[y], hbuf.at[y], hy_s.at[d], hy_r.at[d], pdev[(d, 0)]) for d in (1, 3, 2)
    ]

    with jax.named_scope("relay_gate"):
        ex2 = [second_hop(i, ex1[i]) for i in range(4)]
    with jax.named_scope("gate_up"):
        own_wg.wait()
        wgb[0, 0:768, 0:256] = raw[0, 0:768, 0, :]
        wgb[0, 0:768, 256:512] = raw[0, 0:768, 1, :]
    with jax.named_scope("wait_columns"):
        left, right = up(x, 3, NX), up(x, 1, NX)
        owx[1].wait_recv()
        lower = owbuf.at[0:4, left]
        fwd = [go(lower, lower, owx_s.at[0], owx_r.at[0], pdev[(0, 1)])]
        owx[3].wait_recv()
        higher = owbuf.at[4:8, right]
        fwd.append(go(higher, higher, owx_s.at[2], owx_r.at[2], pdev[(0, 3)]))
        for c in shy:
            c.wait_recv()
    with jax.named_scope("wait_far_columns"):
        for c in fwd:
            c.wait_recv()
    shx = [
        go(shb.at[:, x, h], shb.at[:, x, h], shx_s.at[d], shx_r.at[d], pdev[(0, d)])
        for d in (1, 3, 2)
    ]
    with jax.named_scope("columns"):
        col, row = iota((384, 512), 0), iota((384, 512), 1)
        pick = jnp.where(row == lax.div(col, 12) * 16 + lax.rem(col, 12), 1.0, 0.0).astype(BF16)
        wc[...] = jnp.dot(
            pick, owbuf[...].reshape(512, 768), preferred_element_type=F32
        ).astype(BF16)

    with jax.named_scope("wait_heads"):
        for c in hy:
            c.wait_recv()
    with jax.named_scope("project"):
        po = lax.dot_general(hbuf[...].reshape(256, 768), wc[...], NT, preferred_element_type=F32)
        part[...] = po.reshape(4, 2, 32, 384).astype(BF16)
    rs = []
    for d in (1, 3, 2):
        yd = up(y, d, NY)
        for i, hd in enumerate((h, 1 - h)):
            rs.append(
                go(part.at[yd, hd], rbuf.at[y, h], rs_s.at[i, d], rs_r.at[i, d], (seq_of(yd, z, x), hd))
            )
    rs.append(go(part.at[y, 1 - h], rbuf.at[y, h], rs_s.at[1, 0], rs_r.at[1, 0], sib))
    rbuf[y, h] = part[y, h]
    ex1 += [first_hop(i) for i in range(4, 6)]
    with jax.named_scope("gate_up_rest"):
        wgb[0, 768:1536, 0:256] = raw[0, 768:1536, 0, :]
        wgb[0, 768:1536, 256:512] = raw[0, 768:1536, 1, :]
    with jax.named_scope("wait_projected"):
        for c in rs:
            c.wait_recv()
    with jax.named_scope("norm"):
        own_res.wait()
        attn = [rbuf[j, 0].astype(F32) + rbuf[j, 1].astype(F32) for j in range(NY)]
        mixed = resbuf[...].astype(F32) + jnp.concatenate(attn, axis=1)
        ms = jnp.mean(mixed * mixed, axis=-1, keepdims=True)
        xb[0] = (mixed * lax.rsqrt(ms + EPSILON) * gain_ref[...].reshape(1, 1536)).astype(BF16)
    xz = {
        d: go(xb.at[0], xb.at[SLOT[NZ - d]], xz_s.at[d], xz_r.at[d], zdev[d]) for d in (2, 6, 1, 7)
    }
    with jax.named_scope("gate_sibling"):
        for c in ex2:
            c.wait_recv()
        sib_g = go(raw.at[1, rows_g], raw.at[1, rows_g], sib_s.at[1], sib_r.at[1], sib)
    with jax.named_scope("choose"):
        for c in rp:
            c.wait_recv()
        lane = iota((128, COLS), 1)
        half = lax.div(lane, COLS // 2)
        expert = lax.rem(y + half, 2) * 32 + z * NX + lax.rem(lax.div(lane, ROWS), NX)
        row = iota((128, COLS), 0)
        of_rank = jnp.where(row == expert, 1.0, 0.0).astype(BF16)
        of_prob = jnp.where(row == expert + EXPERTS, 1.0, 0.0).astype(BF16)
        slot = lax.rem(iota((128, COLS), 1), ROWS)
        member = lax.div(row, 32) == lax.div(slot, CAP)
        number = lax.rem(slot, CAP).astype(F32)
        picks, weights = [], []
        for c in range(2):
            rpc = rpb[4 * c : 4 * c + 4].reshape(128, 128).astype(BF16)
            rank = jnp.dot(rpc, of_rank, preferred_element_type=F32)
            prob = jnp.dot(rpc, of_prob, preferred_element_type=F32)
            hit = member & (rank == number)
            picks.append(jnp.transpose(jnp.where(hit, 1.0, 0.0)).astype(BF16))
            weights.append(jnp.where(hit, prob, 0.0).astype(BF16))

    with jax.named_scope("wait_near_rows"):
        xz[2].wait_recv()
        low = pl.ds(0, 16)
        xz[4] = go(
            xb.at[SLOT[6], low], xb.at[SLOT[4], low], xz_s.at[4], xz_r.at[4], zdev[2]
        )
        xz[3] = go(xb.at[SLOT[6]], xb.at[SLOT[5]], xz_s.at[3], xz_r.at[3], zdev[1])
        xz[6].wait_recv()
        high = pl.ds(16, 16)
        xz[0] = go(
            xb.at[SLOT[2], high], xb.at[SLOT[4], high], xz_s.at[0], xz_r.at[0], zdev[6]
        )
        xz[5] = go(xb.at[SLOT[2]], xb.at[SLOT[3]], xz_s.at[5], xz_r.at[5], zdev[7])
        xz[1].wait_recv()
        xz[7].wait_recv()

    turn = 1 + 2 * lax.rem(x, 2)

    def to_expert(p, d):
        return pdev[(0, d)] if p == 0 else (seq_of(up(y, turn, NY), z, up(x, d, NX)), h)

    def to_source(p, d):
        xs = up(x, NX - d, NX)
        if p == 0:
            return pdev[(0, NX - d)]
        return (seq_of(up(y, 3 - 2 * lax.rem(xs, 2), NY), z, xs), h)

    hops = [(p, d) for p in range(2) for d in (2, 1, 3, 0) if (p, d) != (0, 0)]
    before = pdev[(0, 3)]

    def dispatch(c):
        xc = xb[4 * c : 4 * c + 4].reshape(128, 1536)
        rows = jnp.dot(picks[c], xc, preferred_element_type=F32)
        for j in range(8):
            dsend[c, j] = rows[j * ROWS : (j + 1) * ROWS].astype(BF16)
        copies = [go(dsend.at[c, up(x, 2, NX)], relay_x.at[c], q_s.at[c], q_r.at[c], before)]
        for i, (p, d) in enumerate(hops[1:], 1):
            copies.append(
                go(
                    dsend.at[c, p * NX + up(x, d, NX)], drecv.at[c, p * NX + x],
                    d_s.at[c, i], d_r.at[c, i], to_expert(p, d),
                )
            )
        drecv[c, x] = dsend[c, x]
        return copies

    def pass_on(c, copies):
        copies[0].wait_recv()
        copies[0] = go(
            relay_x.at[c], drecv.at[c, up(x, 1, NX)], d_s.at[c, 0], d_r.at[c, 0], before
        )

    sent = {}
    with jax.named_scope("dispatch"):
        sent[1] = dispatch(1)
    with jax.named_scope("relay_down"):
        ex2 = [second_hop(i, ex1[i]) for i in range(4, 6)]
    with jax.named_scope("gate_up_other"):
        sib_g.wait_recv()
        wgb[1, :, 0:256] = raw[1, :, 0, :]
        wgb[1, :, 256:512] = raw[1, :, 1, :]
    with jax.named_scope("pass_on"):
        pass_on(1, sent[1])
    with jax.named_scope("wait_rows"):
        for d in (3, 5, 4, 0):
            xz[d].wait_recv()
    with jax.named_scope("dispatch"):
        sent[0] = dispatch(0)
    with jax.named_scope("shared_weights"):
        for m in shx:
            m.wait_recv()
        sib_sh = go(shb.at[:, :, h], shb.at[:, :, h], sib_s.at[0], sib_r.at[0], sib)
    cz = [
        go(cache_hbm.at[:, up(z, d, NZ)], cmid_ref.at[z], cz_s.at[d], cz_r.at[d], zdev[d])
        for d in ZORDER
    ]
    with jax.named_scope("pass_on"):
        pass_on(0, sent[0])
    with jax.named_scope("down_sibling"):
        for c in ex2:
            c.wait_recv()
        sib_d = go(wdb.at[1, rows_d], wdb.at[1, rows_d], sib_s.at[2], sib_r.at[2], sib)
    with jax.named_scope("shared"):
        sib_sh.wait_recv()
        xs = xb[...].reshape(256, 1536)
        sh = shb[...].reshape(512, 1536)
        both = lax.dot_general(xs, sh, NT, preferred_element_type=F32)
        act = silu(pltpu.roll(both, 8, 1)) * pltpu.roll(both, 4, 1)
        live = lax.rem(lax.div(iota((256, 512), 1), 4), 4) == 2
        act = jnp.where(live, act, 0.0).astype(BF16)
        shared = jnp.dot(act, sh, preferred_element_type=F32)
    with jax.named_scope("wait_exchange"):
        own_wd.wait()
        sib_d.wait_recv()

    back = []
    for c in range(2):
        with jax.named_scope("wait_dispatch"):
            for m in sent[c]:
                m.wait_recv()
        with jax.named_scope("experts"):
            rows = jnp.concatenate([drecv[c, j].astype(F32) for j in range(8)], axis=0).astype(BF16)
            acc = None
            for j in range(2):
                gu = jnp.dot(rows, wgb[j], preferred_element_type=F32)
                a = (silu(gu[:, :256]) * gu[:, 256:]).astype(BF16)
                o = jnp.dot(a, wdb[j], preferred_element_type=F32)
                acc = o if acc is None else acc + o
            for j in range(8):
                rsend[c, j] = acc[j * ROWS : (j + 1) * ROWS].astype(BF16)
            copies = [
                go(rsend.at[c, up(x, 2, NX)], relay_b.at[c], q_s.at[2 + c], q_r.at[2 + c], before)
            ]
            for i, (p, d) in enumerate(hops[1:], 1):
                copies.append(
                    go(
                        rsend.at[c, p * NX + up(x, NX - d, NX)], rrecv.at[c, p * NX + x],
                        r_s.at[c, i], r_r.at[c, i], to_source(p, d),
                    )
                )
            back.append(copies)
            rrecv[c, x] = rsend[c, x]
    with jax.named_scope("pass_back"):
        for c in range(2):
            back[c][0].wait_recv()
            back[c][0] = go(
                relay_b.at[c], rrecv.at[c, up(x, 1, NX)], r_s.at[c, 0], r_r.at[c, 0], before
            )

    def combined(c):
        for m in back[c]:
            m.wait_recv()
        rows = jnp.concatenate([rrecv[c, j].astype(F32) for j in range(8)], axis=0).astype(BF16)
        return shared[128 * c : 128 * c + 128] + jnp.dot(
            weights[c], rows, preferred_element_type=F32
        )

    with jax.named_scope("combine_far"):
        pz[0:4] = combined(0).astype(BF16).reshape(4, 32, 1536)
        far = [
            go(pz.at[SLOT[3]], relay_3.at[0], z_s.at[0], z_r.at[0], zdev[1]),
            go(pz.at[SLOT[5]], relay_3.at[1], z_s.at[1], z_r.at[1], zdev[7]),
            go(pz.at[SLOT[4], low], relay_4.at[0], z_s.at[2], z_r.at[2], zdev[2]),
            go(pz.at[SLOT[4], high], relay_4.at[1], z_s.at[3], z_r.at[3], zdev[6]),
        ]
    with jax.named_scope("combine_near"):
        tot = combined(1)
    with jax.named_scope("wait_far"):
        for m in far:
            m.wait_recv()
    with jax.named_scope("add_far"):
        none = jnp.zeros((16, 1536), F32)
        plus = (
            tot[64:96] + relay_3[0].astype(F32)
            + jnp.concatenate([relay_4[0].astype(F32), none], axis=0)
        )
        minus = (
            tot[96:128] + relay_3[1].astype(F32)
            + jnp.concatenate([none, relay_4[1].astype(F32)], axis=0)
        )
        pz[SLOT[2]] = plus.astype(BF16)
        pz[SLOT[6]] = minus.astype(BF16)
        pz[4:6] = tot[0:64].astype(BF16).reshape(2, 32, 1536)
        red = [
            go(pz.at[SLOT[o]], racc.at[SLOT[NZ - o] - 3], z_s.at[SLOT[o]], z_r.at[SLOT[o]], zdev[o])
            for o in (2, 6, 1, 7)
        ]
    racc[0] = pz[0]
    with jax.named_scope("cache_plane"):
        own_cache.wait()
        for c in cz:
            c.wait_recv()
        cp = [
            go(
                cmid_ref.at[:, up(y, at[0], NY), up(x, at[1], NX)], chand_ref.at[y, :, x],
                cp_s.at[i], cp_r.at[i], pdev[at],
            )
            for i, at in enumerate(plane)
        ]
        cp_own = here(cmid_ref.at[:, y, x], chand_ref.at[y, :, x])
    with jax.named_scope("wait_sum"):
        for c in red:
            c.wait_recv()
    out = mixed
    for j in range(5):
        out = out + racc[j].astype(F32)
    out_ref[...] = out.astype(BF16)
    with jax.named_scope("drain"):
        cp_own.wait()
        for c in cp:
            c.wait_recv()
        for c in pending:
            c.wait_send()


def shards(
    queries, key_vectors, value_vectors, lengths, out_weight, residual, norm_gain, route_ids,
    route_logits, shared_gate_up, shared_down, expert_gate_up, expert_down, cache_blocks, block_table,
):
    hbm, vmem = pl.BlockSpec(memory_space=pltpu.HBM), pl.BlockSpec(memory_space=pltpu.VMEM)
    dma = pltpu.SemaphoreType.DMA
    sgu = jnp.transpose(shared_gate_up, (1, 2, 0))
    wg = expert_gate_up.reshape(1536, 2, 256)
    wd = expert_down.reshape(256, 1536)
    cache = cache_blocks.reshape(NY, NZ, NX, 8, 2, HD)
    sds = jax.ShapeDtypeStruct
    layer_out, _, chand = pl.pallas_call(
        layer_kernel,
        out_shape=(
            sds((32, 1536), BF16),
            sds((NZ, NY, NX, 8, 2, HD), BF16),
            sds((NY, NZ, NX, 8, 2, HD), BF16),
        ),
        in_specs=[hbm, hbm, hbm, vmem, vmem, hbm, vmem, vmem, vmem, vmem, vmem, hbm, hbm, hbm],
        out_specs=(vmem, hbm, hbm),
        scratch_shapes=[
            pltpu.VMEM((64, 768), BF16),
            pltpu.VMEM((320, 256), BF16),
            pltpu.VMEM((320, 256), BF16),
            pltpu.VMEM((32, 1536), BF16),
            pltpu.VMEM((16, 768), BF16),
            pltpu.VMEM((NZ, NX, 16, 768), BF16),
            pltpu.VMEM((384, 768), BF16),
            pltpu.VMEM((NY, 64, 768), BF16),
            pltpu.VMEM((NY, 2, 32, 384), BF16),
            pltpu.VMEM((NY, 2, 32, 384), BF16),
            pltpu.VMEM((NZ, 32, 1536), BF16),
            pltpu.VMEM((NZ, 32, 128), F32),
            pltpu.VMEM((16, 1536), BF16),
            pltpu.VMEM((NY, NX, 2, 16, 1536), BF16),
            pltpu.VMEM((2, 1536, 2, 256), BF16),
            pltpu.VMEM((2, 1536, 512), BF16),
            pltpu.VMEM((2, 256, 1536), BF16),
            pltpu.VMEM((4, 192, 2, 256), BF16),
            pltpu.VMEM((2, 64, 1536), BF16),
            pltpu.VMEM((2, ROWS, 1536), BF16),
            pltpu.VMEM((2, ROWS, 1536), BF16),
            pltpu.VMEM((2, 32, 1536), BF16),
            pltpu.VMEM((2, 16, 1536), BF16),
            pltpu.VMEM((2, 8, ROWS, 1536), BF16),
            pltpu.VMEM((2, 8, ROWS, 1536), BF16),
            pltpu.VMEM((2, 8, ROWS, 1536), BF16),
            pltpu.VMEM((2, 8, ROWS, 1536), BF16),
            pltpu.VMEM((NZ, 32, 1536), BF16),
            pltpu.VMEM((5, 32, 1536), BF16),
            dma((2, 4)), dma((2, 4)),
            dma((8,)), dma((8,)),
            dma((4,)), dma((4,)),
            dma((8,)), dma((8,)),
            dma((4,)), dma((4,)),
            dma((4,)), dma((4,)),
            dma((8,)), dma((8,)),
            dma((15,)), dma((15,)),
            dma((6,)), dma((6,)),
            dma((6,)), dma((6,)),
            dma((3,)), dma((3,)),
            dma((4,)), dma((4,)),
            dma((2, 4)), dma((2, 4)),
            dma((8,)), dma((8,)),
            dma((2, 7)), dma((2, 7)),
            dma((4,)), dma((4,)),
            dma((2, 7)), dma((2, 7)),
            dma((9,)), dma((9,)),
            dma((8,)),
        ],
        compiler_params=pltpu.CompilerParams(
            collective_id=0, has_side_effects=True, vmem_limit_bytes=56 << 20
        ),
        name="layer",
    )(
        queries, key_vectors, value_vectors, lengths, out_weight.T, residual, norm_gain,
        route_ids.T, route_logits.T, sgu, shared_down, wg, wd, cache,
    )
    cache_out = jnp.take(
        chand.reshape(128, 1, 8, 2, HD), block_table, axis=0, mode="clip"
    )
    return layer_out, cache_out


def solution(mesh):
    in_specs = (
        P("seq", "head"),
        P("seq", "head"),
        P("seq", "head"),
        P(),
        P("head", "seq"),
        P(("seq", "head"), None),
        P(),
        P(("seq", "head"), None),
        P(("seq", "head"), None),
        P(None, None, ("seq", "head")),
        P(("seq", "head"), None),
        P("seq", None, None, None),
        P("seq", None, None),
        P("seq", None, None, "head", None),
        P(),
    )
    out_specs = (P(("seq", "head"), None), P(None, "seq", None, "head", None))
    return jax.shard_map(shards, mesh=mesh, in_specs=in_specs, out_specs=out_specs, check_vma=False)
```

```python
import functools
import math

import jax
import jax.numpy as jnp
from jax import lax
from jax.experimental import pallas as pl
from jax.experimental.pallas import tpu as pltpu
from jax.sharding import PartitionSpec as P

MESH = pl.DeviceIdType.MESH
HD = 128
NY, NZ, NX = 4, 8, 4
TOP = 6
CAP = 6
EXPERTS = 64
NEGATIVE = -1e30
EPSILON = 1e-05
F32 = jnp.float32
BF16 = jnp.bfloat16
ZORDER = (1, 7, 2, 6, 3, 5, 4)
OFF = (0, 3, 5, 4, 1, 7, 2, 6)
SLOT = {o: k for k, o in enumerate(OFF)}
ROWS = 24
COLS = 8 * ROWS
NT = (((1,), (1,)), ((), ()))


def place():
    s = lax.axis_index("seq")
    h = lax.axis_index("head")
    y = lax.div(s, NZ * NX)
    z = lax.rem(lax.div(s, NX), NZ)
    x = lax.rem(s, NX)
    return s, h, y, z, x


def seq_of(y, z, x):
    return y * (NZ * NX) + z * NX + x


def up(i, by, n):
    return lax.rem(i + by, n)


def rcopy(src, dst, ssem, rsem, dev):
    return pltpu.make_async_remote_copy(
        src_ref=src, dst_ref=dst, send_sem=ssem, recv_sem=rsem, device_id=dev, device_id_type=MESH
    )


def iota(shape, axis):
    return lax.broadcasted_iota(jnp.int32, shape, axis)


def silu(v):
    return v / (1.0 + jnp.exp(-v))


def routing_table(ids, logits):
    top = jnp.max(logits, axis=0, keepdims=True)
    e = jnp.exp(logits - top)
    probs = e / jnp.sum(e, axis=0, keepdims=True)
    row = iota((128, 32), 0)
    named = jnp.zeros((128, 32), F32)
    weight = jnp.zeros((128, 32), F32)
    for r in range(TOP):
        idr = jnp.broadcast_to(ids[r : r + 1, :], (128, 32))
        named = named + jnp.where(row == idr, 1.0, 0.0)
        weight = weight + jnp.where(row - EXPERTS == idr, probs[r : r + 1, :], 0.0)
    before = jnp.where(iota((32, 32), 0) < iota((32, 32), 1), 1.0, 0.0)
    rank = jnp.dot(named.astype(BF16), before.astype(BF16), preferred_element_type=F32)
    table = jnp.where(row < EXPERTS, jnp.where(named > 0.5, rank, -1.0), weight)
    return jnp.transpose(table)


def layer_kernel(
    q_hbm, k_hbm, v_hbm, len_ref, ow_ref, res_hbm, gain_ref, ids_ref, log_ref,
    sgu_ref, sd_ref, wg_hbm, wd_hbm, cache_hbm,
    out_ref, cmid_ref, chand_ref,
    qbuf, kwin, vwin, resbuf, owpad, owbuf, wc, hbuf, part, rbuf, xb, rpb, shpad, shb, raw, wgb, wdb,
    relay_g, relay_d, relay_x, relay_b, relay_3, relay_4, dsend, drecv, rsend, rrecv, pz, racc,
    kv_s, kv_r, owz_s, owz_r, owx_s, owx_r, rp_s, rp_r, shy_s, shy_r, shx_s, shx_r, cz_s, cz_r, cp_s, cp_r,
    e1_s, e1_r, e2_s, e2_r, sib_s, sib_r, hy_s, hy_r, rs_s, rs_r, xz_s, xz_r, d_s, d_r, q_s, q_r, r_s, r_r, z_s, z_r, loc,
):
    s, h, y, z, x = place()
    seqs = NY * NZ * NX
    zdev = {d: (seq_of(y, up(z, d, NZ), x), h) for d in range(1, NZ)}
    plane = [
        (dy, dx) for dy in range(NY) for dx in range(NX) if (dy, dx) != (0, 0)
    ]
    pdev = {at: (seq_of(up(y, at[0], NY), z, up(x, at[1], NX)), h) for at in plane}
    sib = (s, 1 - h)
    cross = [(seq_of(up(y, dy, NY), z, x), 1 - h) for dy in (1, 2, 3)]
    ahead = [(lax.rem(s + by, seqs), h) for by in range(1, 5)]
    behind = [(lax.rem(s + seqs - by, seqs), h) for by in range(1, 5)]

    local = []

    def here(src, dst):
        copy = pltpu.make_async_copy(src, dst, loc.at[len(local)])
        copy.start()
        local.append(copy)
        return copy

    own_wg = here(wg_hbm, raw.at[0])
    own_k = here(k_hbm, kwin.at[pl.ds(256, 64)])
    own_v = here(v_hbm, vwin.at[pl.ds(256, 64)])
    own_q = here(q_hbm, qbuf)
    own_cache = here(cache_hbm.at[:, z], cmid_ref.at[z])
    own_res = here(res_hbm, resbuf)
    own_wd = here(wd_hbm, wdb.at[0])
    peers = list(zdev.values()) + list(pdev.values()) + [sib] + cross + ahead + behind
    barrier = pltpu.get_barrier_semaphore()
    for dev in peers:
        pl.semaphore_signal(barrier, inc=1, device_id=dev, device_id_type=MESH)

    with jax.named_scope("pack"):
        owpad[...] = jnp.concatenate(
            [ow_ref[...].astype(F32), jnp.zeros((4, 768), F32)], axis=0
        ).astype(BF16)
        owbuf[z, x] = owpad[...]
        shpad[...] = jnp.concatenate(
            [
                sgu_ref[...].astype(F32).reshape(8, 1536),
                sd_ref[...].astype(F32),
                jnp.zeros((4, 1536), F32),
            ],
            axis=0,
        ).astype(BF16)
        shb[y, x, h] = shpad[...]
    with jax.named_scope("routing"):
        rpb[0] = routing_table(ids_ref[...], log_ref[...])
    with jax.named_scope("enter"):
        pl.semaphore_wait(barrier, len(peers))

    pending = []

    def go(*args):
        copy = rcopy(*args)
        copy.start()
        pending.append(copy)
        return copy

    owz = [go(owpad, owbuf.at[z, x], owz_s.at[d], owz_r.at[d], zdev[d]) for d in ZORDER]
    kv = []
    for by in range(1, 5):
        rows = pl.ds(64 * (4 - by), 64)
        kv.append(go(k_hbm, kwin.at[rows], kv_s.at[0, by - 1], kv_r.at[0, by - 1], ahead[by - 1]))
        kv.append(go(v_hbm, vwin.at[rows], kv_s.at[1, by - 1], kv_r.at[1, by - 1], ahead[by - 1]))
    shy = [
        go(shpad, shb.at[y, x, h], shy_s.at[d], shy_r.at[d], pdev[(d, 0)]) for d in (1, 3, 2)
    ]
    sides = (pdev[(1, 0)], pdev[(3, 0)])
    rows_g, rows_d = pl.ds(h * 768, 768), pl.ds(h * 128, 128)

    def piece(i):
        if i < 4:
            return pl.ds(h * 768 + i * 192, 192)
        return pl.ds(h * 128 + (i - 4) * 64, 64)

    def first_hop(i):
        sem = e1_s.at[i], e1_r.at[i], sides[i % 2]
        if i < 4:
            return go(wg_hbm.at[piece(i)], relay_g.at[i], *sem)
        return go(wd_hbm.at[piece(i)], relay_d.at[i - 4], *sem)

    def second_hop(i, arrived):
        arrived.wait_recv()
        sem = e2_s.at[i], e2_r.at[i], sides[i % 2]
        if i < 4:
            return go(relay_g.at[i], raw.at[1, piece(i)], *sem)
        return go(relay_d.at[i - 4], wdb.at[1, piece(i)], *sem)

    ex1 = [first_hop(i) for i in range(4)]

    with jax.named_scope("visible"):
        upper = jnp.where(iota((64, 64), 0) <= iota((64, 64), 1), 1.0, 0.0).astype(BF16)
        lens = jnp.broadcast_to(len_ref[...].astype(F32).reshape(1, 64), (16, 64)).astype(BF16)
        ends = jnp.dot(lens, upper, preferred_element_type=F32)[0:1, :]
        qpos = (s * 64 + iota((64, 64), 0)).astype(F32)
        first = jnp.max(jnp.where(ends <= qpos, ends, 0.0), axis=-1, keepdims=True)
        kpos = (s * 64 - 256 + iota((64, 320), 1)).astype(F32)
        qcol = (s * 64 + iota((64, 320), 0)).astype(F32)
        seen = jnp.where((kpos >= first) & (kpos <= qcol), 0.0, NEGATIVE)
        seen3 = jnp.concatenate([seen, seen, seen], axis=0)

    with jax.named_scope("wait_first_columns"):
        for c in owz:
            c.wait_recv()
    owx = {
        d: go(owbuf.at[:, x], owbuf.at[:, x], owx_s.at[d], owx_r.at[d], pdev[(0, d)])
        for d in (1, 3)
    }
    with jax.named_scope("wait_keys"):
        own_k.wait()
        own_v.wait()
        own_q.wait()
        for c in kv:
            c.wait_recv()
    with jax.named_scope("attention"):
        for g in range(2):
            cols = slice(g * HD, (g + 1) * HD)
            qs = jnp.concatenate(
                [qbuf[:, (3 * g + i) * HD : (3 * g + i + 1) * HD] for i in range(3)], axis=0
            )
            sc = lax.dot_general(qs, kwin[:, cols], NT, preferred_element_type=F32)
            sc = jnp.where(seen3 < -1.0, NEGATIVE, sc * (1.0 / math.sqrt(HD)))
            w = jnp.exp(sc - jnp.max(sc, axis=-1, keepdims=True))
            total = jnp.sum(w, axis=-1, keepdims=True)
            o = jnp.dot(w.astype(BF16), vwin[:, cols], preferred_element_type=F32)
            o = (o / total).astype(BF16)
            for i in range(3):
                hbuf[y, :, (3 * g + i) * HD : (3 * g + i + 1) * HD] = o[i * 64 : (i + 1) * 64]
    hy = [
        go(hbuf.at[y], hbuf.at[y], hy_s.at[d], hy_r.at[d], pdev[(d, 0)]) for d in (1, 3, 2)
    ]

    rp = [
        go(rpb.at[0], rpb.at[SLOT[NZ - d]], rp_s.at[d], rp_r.at[d], zdev[d]) for d in ZORDER
    ]
    with jax.named_scope("gate_up"):
        own_wg.wait()
        wgb[0, 0:768, 0:256] = raw[0, 0:768, 0, :]
        wgb[0, 0:768, 256:512] = raw[0, 0:768, 1, :]
    with jax.named_scope("wait_columns"):
        left, right = up(x, 3, NX), up(x, 1, NX)
        owx[1].wait_recv()
        lower = owbuf.at[0:4, left]
        fwd = [go(lower, lower, owx_s.at[0], owx_r.at[0], pdev[(0, 1)])]
        owx[3].wait_recv()
        higher = owbuf.at[4:8, right]
        fwd.append(go(higher, higher, owx_s.at[2], owx_r.at[2], pdev[(0, 3)]))
        for c in shy:
            c.wait_recv()
    with jax.named_scope("wait_far_columns"):
        for c in fwd:
            c.wait_recv()
    shx = [
        go(shb.at[:, x, h], shb.at[:, x, h], shx_s.at[d], shx_r.at[d], pdev[(0, d)])
        for d in (1, 3, 2)
    ]
    with jax.named_scope("relay_gate"):
        ex2 = [second_hop(i, ex1[i]) for i in range(2)]
    with jax.named_scope("columns"):
        col, row = iota((384, 512), 0), iota((384, 512), 1)
        pick = jnp.where(row == lax.div(col, 12) * 16 + lax.rem(col, 12), 1.0, 0.0).astype(BF16)
        wc[...] = jnp.dot(
            pick, owbuf[...].reshape(512, 768), preferred_element_type=F32
        ).astype(BF16)

    with jax.named_scope("wait_heads"):
        for c in hy:
            c.wait_recv()
    with jax.named_scope("project"):
        po = lax.dot_general(hbuf[...].reshape(256, 768), wc[...], NT, preferred_element_type=F32)
        part[...] = po.reshape(4, 2, 32, 384).astype(BF16)
    rs = []
    for d in (1, 3, 2):
        yd = up(y, d, NY)
        for i, hd in enumerate((h, 1 - h)):
            rs.append(
                go(part.at[yd, hd], rbuf.at[y, h], rs_s.at[i, d], rs_r.at[i, d], (seq_of(yd, z, x), hd))
            )
    rs.append(go(part.at[y, 1 - h], rbuf.at[y, h], rs_s.at[1, 0], rs_r.at[1, 0], sib))
    rbuf[y, h] = part[y, h]
    with jax.named_scope("relay_gate_rest"):
        ex2 += [second_hop(i, ex1[i]) for i in range(2, 4)]
        ex1 += [first_hop(i) for i in range(4, 6)]
    with jax.named_scope("gate_up_rest"):
        wgb[0, 768:1536, 0:256] = raw[0, 768:1536, 0, :]
        wgb[0, 768:1536, 256:512] = raw[0, 768:1536, 1, :]
    with jax.named_scope("wait_projected"):
        for c in rs:
            c.wait_recv()
    with jax.named_scope("norm"):
        own_res.wait()
        attn = [rbuf[j, 0].astype(F32) + rbuf[j, 1].astype(F32) for j in range(NY)]
        mixed = resbuf[...].astype(F32) + jnp.concatenate(attn, axis=1)
        ms = jnp.mean(mixed * mixed, axis=-1, keepdims=True)
        xb[0] = (mixed * lax.rsqrt(ms + EPSILON) * gain_ref[...].reshape(1, 1536)).astype(BF16)
    xz = {
        d: go(xb.at[0], xb.at[SLOT[NZ - d]], xz_s.at[d], xz_r.at[d], zdev[d]) for d in (2, 6, 1, 7)
    }
    with jax.named_scope("choose"):
        for c in rp:
            c.wait_recv()
        lane = iota((128, COLS), 1)
        half = lax.div(lane, COLS // 2)
        expert = lax.rem(y + half, 2) * 32 + z * NX + lax.rem(lax.div(lane, ROWS), NX)
        row = iota((128, COLS), 0)
        of_rank = jnp.where(row == expert, 1.0, 0.0).astype(BF16)
        of_prob = jnp.where(row == expert + EXPERTS, 1.0, 0.0).astype(BF16)
        slot = lax.rem(iota((128, COLS), 1), ROWS)
        member = lax.div(row, 32) == lax.div(slot, CAP)
        number = lax.rem(slot, CAP).astype(F32)
        picks, weights = [], []
        for c in range(2):
            rpc = rpb[4 * c : 4 * c + 4].reshape(128, 128).astype(BF16)
            rank = jnp.dot(rpc, of_rank, preferred_element_type=F32)
            prob = jnp.dot(rpc, of_prob, preferred_element_type=F32)
            hit = member & (rank == number)
            picks.append(jnp.transpose(jnp.where(hit, 1.0, 0.0)).astype(BF16))
            weights.append(jnp.where(hit, prob, 0.0).astype(BF16))

    with jax.named_scope("wait_near_rows"):
        xz[2].wait_recv()
        low = pl.ds(0, 16)
        xz[4] = go(
            xb.at[SLOT[6], low], xb.at[SLOT[4], low], xz_s.at[4], xz_r.at[4], zdev[2]
        )
        xz[3] = go(xb.at[SLOT[6]], xb.at[SLOT[5]], xz_s.at[3], xz_r.at[3], zdev[1])
        xz[6].wait_recv()
        high = pl.ds(16, 16)
        xz[0] = go(
            xb.at[SLOT[2], high], xb.at[SLOT[4], high], xz_s.at[0], xz_r.at[0], zdev[6]
        )
        xz[5] = go(xb.at[SLOT[2]], xb.at[SLOT[3]], xz_s.at[5], xz_r.at[5], zdev[7])
        xz[1].wait_recv()
        xz[7].wait_recv()

    turn = 1 + 2 * lax.rem(x, 2)

    def to_expert(p, d):
        return pdev[(0, d)] if p == 0 else (seq_of(up(y, turn, NY), z, up(x, d, NX)), h)

    def to_source(p, d):
        xs = up(x, NX - d, NX)
        if p == 0:
            return pdev[(0, NX - d)]
        return (seq_of(up(y, 3 - 2 * lax.rem(xs, 2), NY), z, xs), h)

    hops = [(p, d) for p in range(2) for d in (2, 1, 3, 0) if (p, d) != (0, 0)]
    before = pdev[(0, 3)]

    def dispatch(c):
        xc = xb[4 * c : 4 * c + 4].reshape(128, 1536)
        rows = jnp.dot(picks[c], xc, preferred_element_type=F32)
        for j in range(8):
            dsend[c, j] = rows[j * ROWS : (j + 1) * ROWS].astype(BF16)
        copies = [go(dsend.at[c, up(x, 2, NX)], relay_x.at[c], q_s.at[c], q_r.at[c], before)]
        for i, (p, d) in enumerate(hops[1:], 1):
            copies.append(
                go(
                    dsend.at[c, p * NX + up(x, d, NX)], drecv.at[c, p * NX + x],
                    d_s.at[c, i], d_r.at[c, i], to_expert(p, d),
                )
            )
        drecv[c, x] = dsend[c, x]
        return copies

    def pass_on(c, copies):
        copies[0].wait_recv()
        copies[0] = go(
            relay_x.at[c], drecv.at[c, up(x, 1, NX)], d_s.at[c, 0], d_r.at[c, 0], before
        )

    sent = {}
    with jax.named_scope("dispatch"):
        sent[1] = dispatch(1)
    ex2g = ex2
    with jax.named_scope("gate_sibling"):
        for c in ex2g:
            c.wait_recv()
        sib_g = go(raw.at[1, rows_g], raw.at[1, rows_g], sib_s.at[1], sib_r.at[1], sib)
    with jax.named_scope("relay_down"):
        ex2 = [second_hop(i, ex1[i]) for i in range(4, 6)]
    with jax.named_scope("pass_on"):
        pass_on(1, sent[1])
    with jax.named_scope("wait_rows"):
        for d in (3, 5, 4, 0):
            xz[d].wait_recv()
    with jax.named_scope("dispatch"):
        sent[0] = dispatch(0)
    with jax.named_scope("shared_weights"):
        for m in shx:
            m.wait_recv()
        sib_sh = go(shb.at[:, :, h], shb.at[:, :, h], sib_s.at[0], sib_r.at[0], sib)
    cz = [
        go(cache_hbm.at[:, up(z, d, NZ)], cmid_ref.at[z], cz_s.at[d], cz_r.at[d], zdev[d])
        for d in ZORDER
    ]
    with jax.named_scope("gate_up_other"):
        sib_g.wait_recv()
        wgb[1, :, 0:256] = raw[1, :, 0, :]
        wgb[1, :, 256:512] = raw[1, :, 1, :]
    with jax.named_scope("pass_on"):
        pass_on(0, sent[0])
    with jax.named_scope("down_sibling"):
        for c in ex2:
            c.wait_recv()
        sib_d = go(wdb.at[1, rows_d], wdb.at[1, rows_d], sib_s.at[2], sib_r.at[2], sib)
    with jax.named_scope("shared"):
        sib_sh.wait_recv()
        xs = xb[...].reshape(256, 1536)
        sh = shb[...].reshape(512, 1536)
        both = lax.dot_general(xs, sh, NT, preferred_element_type=F32)
        act = silu(pltpu.roll(both, 8, 1)) * pltpu.roll(both, 4, 1)
        live = lax.rem(lax.div(iota((256, 512), 1), 4), 4) == 2
        act = jnp.where(live, act, 0.0).astype(BF16)
        shared = jnp.dot(act, sh, preferred_element_type=F32)
    with jax.named_scope("wait_exchange"):
        own_wd.wait()
        sib_d.wait_recv()

    back = []
    for c in range(2):
        with jax.named_scope("wait_dispatch"):
            for m in sent[c]:
                m.wait_recv()
        with jax.named_scope("experts"):
            rows = jnp.concatenate([drecv[c, j].astype(F32) for j in range(8)], axis=0).astype(BF16)
            acc = None
            for j in range(2):
                gu = jnp.dot(rows, wgb[j], preferred_element_type=F32)
                a = (silu(gu[:, :256]) * gu[:, 256:]).astype(BF16)
                o = jnp.dot(a, wdb[j], preferred_element_type=F32)
                acc = o if acc is None else acc + o
            for j in range(8):
                rsend[c, j] = acc[j * ROWS : (j + 1) * ROWS].astype(BF16)
            copies = [
                go(rsend.at[c, up(x, 2, NX)], relay_b.at[c], q_s.at[2 + c], q_r.at[2 + c], before)
            ]
            for i, (p, d) in enumerate(hops[1:], 1):
                copies.append(
                    go(
                        rsend.at[c, p * NX + up(x, NX - d, NX)], rrecv.at[c, p * NX + x],
                        r_s.at[c, i], r_r.at[c, i], to_source(p, d),
                    )
                )
            back.append(copies)
            rrecv[c, x] = rsend[c, x]
    with jax.named_scope("pass_back"):
        for c in range(2):
            back[c][0].wait_recv()
            back[c][0] = go(
                relay_b.at[c], rrecv.at[c, up(x, 1, NX)], r_s.at[c, 0], r_r.at[c, 0], before
            )

    def combined(c):
        for m in back[c]:
            m.wait_recv()
        rows = jnp.concatenate([rrecv[c, j].astype(F32) for j in range(8)], axis=0).astype(BF16)
        return shared[128 * c : 128 * c + 128] + jnp.dot(
            weights[c], rows, preferred_element_type=F32
        )

    with jax.named_scope("combine_far"):
        pz[0:4] = combined(0).astype(BF16).reshape(4, 32, 1536)
        far = [
            go(pz.at[SLOT[3]], relay_3.at[0], z_s.at[0], z_r.at[0], zdev[1]),
            go(pz.at[SLOT[5]], relay_3.at[1], z_s.at[1], z_r.at[1], zdev[7]),
            go(pz.at[SLOT[4], low], relay_4.at[0], z_s.at[2], z_r.at[2], zdev[2]),
            go(pz.at[SLOT[4], high], relay_4.at[1], z_s.at[3], z_r.at[3], zdev[6]),
        ]
    with jax.named_scope("combine_near"):
        tot = combined(1)
        pz[4:6] = tot[0:64].astype(BF16).reshape(2, 32, 1536)

        def to_line(o):
            return go(
                pz.at[SLOT[o]], racc.at[SLOT[NZ - o] - 3], z_s.at[SLOT[o]], z_r.at[SLOT[o]], zdev[o]
            )

        red = [to_line(1), to_line(7)]
    with jax.named_scope("cache_plane"):
        own_cache.wait()
        for c in cz:
            c.wait_recv()
        cp = [
            go(
                cmid_ref.at[:, up(y, at[0], NY), up(x, at[1], NX)], chand_ref.at[y, :, x],
                cp_s.at[i], cp_r.at[i], pdev[at],
            )
            for i, at in enumerate(plane)
        ]
        cp_own = here(cmid_ref.at[:, y, x], chand_ref.at[y, :, x])
    with jax.named_scope("wait_far"):
        for m in far:
            m.wait_recv()
    with jax.named_scope("add_far"):
        none = jnp.zeros((16, 1536), F32)
        plus = (
            tot[64:96] + relay_3[0].astype(F32)
            + jnp.concatenate([relay_4[0].astype(F32), none], axis=0)
        )
        minus = (
            tot[96:128] + relay_3[1].astype(F32)
            + jnp.concatenate([none, relay_4[1].astype(F32)], axis=0)
        )
        pz[SLOT[2]] = plus.astype(BF16)
        pz[SLOT[6]] = minus.astype(BF16)
        red += [to_line(2), to_line(6)]
    racc[0] = pz[0]
    with jax.named_scope("wait_sum"):
        for c in red:
            c.wait_recv()
    out = mixed
    for j in range(5):
        out = out + racc[j].astype(F32)
    out_ref[...] = out.astype(BF16)
    with jax.named_scope("drain"):
        cp_own.wait()
        for c in cp:
            c.wait_recv()
        for c in pending:
            c.wait_send()


def shards(
    queries, key_vectors, value_vectors, lengths, out_weight, residual, norm_gain, route_ids,
    route_logits, shared_gate_up, shared_down, expert_gate_up, expert_down, cache_blocks, block_table,
):
    hbm, vmem = pl.BlockSpec(memory_space=pltpu.HBM), pl.BlockSpec(memory_space=pltpu.VMEM)
    dma = pltpu.SemaphoreType.DMA
    sgu = jnp.transpose(shared_gate_up, (1, 2, 0))
    wg = expert_gate_up.reshape(1536, 2, 256)
    wd = expert_down.reshape(256, 1536)
    cache = cache_blocks.reshape(NY, NZ, NX, 8, 2, HD)
    sds = jax.ShapeDtypeStruct
    layer_out, _, chand = pl.pallas_call(
        layer_kernel,
        out_shape=(
            sds((32, 1536), BF16),
            sds((NZ, NY, NX, 8, 2, HD), BF16),
            sds((NY, NZ, NX, 8, 2, HD), BF16),
        ),
        in_specs=[hbm, hbm, hbm, vmem, vmem, hbm, vmem, vmem, vmem, vmem, vmem, hbm, hbm, hbm],
        out_specs=(vmem, hbm, hbm),
        scratch_shapes=[
            pltpu.VMEM((64, 768), BF16),
            pltpu.VMEM((320, 256), BF16),
            pltpu.VMEM((320, 256), BF16),
            pltpu.VMEM((32, 1536), BF16),
            pltpu.VMEM((16, 768), BF16),
            pltpu.VMEM((NZ, NX, 16, 768), BF16),
            pltpu.VMEM((384, 768), BF16),
            pltpu.VMEM((NY, 64, 768), BF16),
            pltpu.VMEM((NY, 2, 32, 384), BF16),
            pltpu.VMEM((NY, 2, 32, 384), BF16),
            pltpu.VMEM((NZ, 32, 1536), BF16),
            pltpu.VMEM((NZ, 32, 128), F32),
            pltpu.VMEM((16, 1536), BF16),
            pltpu.VMEM((NY, NX, 2, 16, 1536), BF16),
            pltpu.VMEM((2, 1536, 2, 256), BF16),
            pltpu.VMEM((2, 1536, 512), BF16),
            pltpu.VMEM((2, 256, 1536), BF16),
            pltpu.VMEM((4, 192, 2, 256), BF16),
            pltpu.VMEM((2, 64, 1536), BF16),
            pltpu.VMEM((2, ROWS, 1536), BF16),
            pltpu.VMEM((2, ROWS, 1536), BF16),
            pltpu.VMEM((2, 32, 1536), BF16),
            pltpu.VMEM((2, 16, 1536), BF16),
            pltpu.VMEM((2, 8, ROWS, 1536), BF16),
            pltpu.VMEM((2, 8, ROWS, 1536), BF16),
            pltpu.VMEM((2, 8, ROWS, 1536), BF16),
            pltpu.VMEM((2, 8, ROWS, 1536), BF16),
            pltpu.VMEM((NZ, 32, 1536), BF16),
            pltpu.VMEM((5, 32, 1536), BF16),
            dma((2, 4)), dma((2, 4)),
            dma((8,)), dma((8,)),
            dma((4,)), dma((4,)),
            dma((8,)), dma((8,)),
            dma((4,)), dma((4,)),
            dma((4,)), dma((4,)),
            dma((8,)), dma((8,)),
            dma((15,)), dma((15,)),
            dma((6,)), dma((6,)),
            dma((6,)), dma((6,)),
            dma((3,)), dma((3,)),
            dma((4,)), dma((4,)),
            dma((2, 4)), dma((2, 4)),
            dma((8,)), dma((8,)),
            dma((2, 7)), dma((2, 7)),
            dma((4,)), dma((4,)),
            dma((2, 7)), dma((2, 7)),
            dma((9,)), dma((9,)),
            dma((8,)),
        ],
        compiler_params=pltpu.CompilerParams(
            collective_id=0, has_side_effects=True, vmem_limit_bytes=56 << 20
        ),
        name="layer",
    )(
        queries, key_vectors, value_vectors, lengths, out_weight.T, residual, norm_gain,
        route_ids.T, route_logits.T, sgu, shared_down, wg, wd, cache,
    )
    cache_out = jnp.take(
        chand.reshape(128, 1, 8, 2, HD), block_table, axis=0, mode="clip"
    )
    return layer_out, cache_out


def solution(mesh):
    in_specs = (
        P("seq", "head"),
        P("seq", "head"),
        P("seq", "head"),
        P(),
        P("head", "seq"),
        P(("seq", "head"), None),
        P(),
        P(("seq", "head"), None),
        P(("seq", "head"), None),
        P(None, None, ("seq", "head")),
        P(("seq", "head"), None),
        P("seq", None, None, None),
        P("seq", None, None),
        P("seq", None, None, "head", None),
        P(),
    )
    out_specs = (P(("seq", "head"), None), P(None, "seq", None, "head", None))
    return jax.shard_map(shards, mesh=mesh, in_specs=in_specs, out_specs=out_specs, check_vma=False)
```

```python
import functools
import math

import jax
import jax.numpy as jnp
from jax import lax
from jax.experimental import pallas as pl
from jax.experimental.pallas import tpu as pltpu
from jax.sharding import PartitionSpec as P

MESH = pl.DeviceIdType.MESH
HD = 128
NY, NZ, NX = 4, 8, 4
TOP = 6
CAP = 6
EXPERTS = 64
NEGATIVE = -1e30
EPSILON = 1e-05
F32 = jnp.float32
BF16 = jnp.bfloat16
ZORDER = (1, 7, 2, 6, 3, 5, 4)
OFF = (0, 3, 5, 4, 1, 7, 2, 6)
SLOT = {o: k for k, o in enumerate(OFF)}
ROWS = 24
POOL = 48
COLS = 8 * ROWS
NT = (((1,), (1,)), ((), ()))


def place():
    s = lax.axis_index("seq")
    h = lax.axis_index("head")
    y = lax.div(s, NZ * NX)
    z = lax.rem(lax.div(s, NX), NZ)
    x = lax.rem(s, NX)
    return s, h, y, z, x


def seq_of(y, z, x):
    return y * (NZ * NX) + z * NX + x


def up(i, by, n):
    return lax.rem(i + by, n)


def rcopy(src, dst, ssem, rsem, dev):
    return pltpu.make_async_remote_copy(
        src_ref=src, dst_ref=dst, send_sem=ssem, recv_sem=rsem, device_id=dev, device_id_type=MESH
    )


def iota(shape, axis):
    return lax.broadcasted_iota(jnp.int32, shape, axis)


def silu(v):
    return v / (1.0 + jnp.exp(-v))


def routing_table(ids, logits):
    top = jnp.max(logits, axis=0, keepdims=True)
    e = jnp.exp(logits - top)
    probs = e / jnp.sum(e, axis=0, keepdims=True)
    row = iota((128, 32), 0)
    named = jnp.zeros((128, 32), F32)
    weight = jnp.zeros((128, 32), F32)
    for r in range(TOP):
        idr = jnp.broadcast_to(ids[r : r + 1, :], (128, 32))
        named = named + jnp.where(row == idr, 1.0, 0.0)
        weight = weight + jnp.where(row - EXPERTS == idr, probs[r : r + 1, :], 0.0)
    before = jnp.where(iota((32, 32), 0) < iota((32, 32), 1), 1.0, 0.0)
    rank = jnp.dot(named.astype(BF16), before.astype(BF16), preferred_element_type=F32)
    table = jnp.where(row < EXPERTS, jnp.where(named > 0.5, rank, -1.0), weight)
    return jnp.transpose(table)


def layer_kernel(
    q_hbm, k_hbm, v_hbm, len_ref, ow_ref, res_hbm, gain_ref, ids_ref, log_ref,
    sgu_ref, sd_ref, wg_hbm, wd_hbm, cache_hbm,
    out_ref, cmid_ref, chand_ref,
    qbuf, kwin, vwin, resbuf, owpad, owbuf, wc, hbuf, part, rbuf, xb, rpb, shpad, shb, raw, wgb, wdb,
    relay_g, relay_d, relay_x, relay_b, relay_3, relay_4, dsend, drecv, rsend, rrecv, pz, racc,
    pool, kv_r, owz_r, owx_r, rp_r, shy_r, shx_r, cz_r, cp_r, e1_r, e2_r, sib_r, hy_r,
    rs_r, xz_r, d_r, q_r, r_r, z_r, loc,
):
    s, h, y, z, x = place()
    seqs = NY * NZ * NX
    zdev = {d: (seq_of(y, up(z, d, NZ), x), h) for d in range(1, NZ)}
    plane = [
        (dy, dx) for dy in range(NY) for dx in range(NX) if (dy, dx) != (0, 0)
    ]
    pdev = {at: (seq_of(up(y, at[0], NY), z, up(x, at[1], NX)), h) for at in plane}
    sib = (s, 1 - h)
    cross = [(seq_of(up(y, dy, NY), z, x), 1 - h) for dy in (1, 2, 3)]
    ahead = [(lax.rem(s + by, seqs), h) for by in range(1, 5)]
    behind = [(lax.rem(s + seqs - by, seqs), h) for by in range(1, 5)]

    local = []

    def here(src, dst):
        copy = pltpu.make_async_copy(src, dst, loc.at[len(local)])
        copy.start()
        local.append(copy)
        return copy

    own_wg = here(wg_hbm, raw.at[0])
    own_k = here(k_hbm, kwin.at[pl.ds(256, 64)])
    own_v = here(v_hbm, vwin.at[pl.ds(256, 64)])
    own_q = here(q_hbm, qbuf)
    own_cache = here(cache_hbm.at[:, z], cmid_ref.at[z])
    own_res = here(res_hbm, resbuf)
    own_wd = here(wd_hbm, wdb.at[0])
    peers = list(zdev.values()) + list(pdev.values()) + [sib] + cross + ahead + behind
    barrier = pltpu.get_barrier_semaphore()
    for dev in peers:
        pl.semaphore_signal(barrier, inc=1, device_id=dev, device_id_type=MESH)

    with jax.named_scope("pack"):
        owpad[...] = jnp.concatenate(
            [ow_ref[...].astype(F32), jnp.zeros((4, 768), F32)], axis=0
        ).astype(BF16)
        owbuf[z, x] = owpad[...]
        shpad[...] = jnp.concatenate(
            [
                sgu_ref[...].astype(F32).reshape(8, 1536),
                sd_ref[...].astype(F32),
                jnp.zeros((4, 1536), F32),
            ],
            axis=0,
        ).astype(BF16)
        shb[y, x, h] = shpad[...]
    with jax.named_scope("routing"):
        rpb[0] = routing_table(ids_ref[...], log_ref[...])
    with jax.named_scope("enter"):
        pl.semaphore_wait(barrier, len(peers))

    pending = []

    def go(src, dst, recv, dev):
        turn = len(pending)
        if turn >= POOL:
            pending[turn - POOL].wait_send()
        copy = rcopy(src, dst, pool.at[turn % POOL], recv, dev)
        copy.start()
        pending.append(copy)
        return copy

    owz = [go(owpad, owbuf.at[z, x], owz_r.at[d], zdev[d]) for d in ZORDER]
    kv = []
    for by in range(1, 5):
        rows = pl.ds(64 * (4 - by), 64)
        kv.append(go(k_hbm, kwin.at[rows], kv_r.at[0, by - 1], ahead[by - 1]))
        kv.append(go(v_hbm, vwin.at[rows], kv_r.at[1, by - 1], ahead[by - 1]))
    shy = [
        go(shpad, shb.at[y, x, h], shy_r.at[d], pdev[(d, 0)]) for d in (1, 3, 2)
    ]
    sides = (pdev[(1, 0)], pdev[(3, 0)])
    rows_g, rows_d = pl.ds(h * 768, 768), pl.ds(h * 128, 128)

    def piece(i):
        if i < 4:
            return pl.ds(h * 768 + i * 192, 192)
        return pl.ds(h * 128 + (i - 4) * 64, 64)

    def first_hop(i):
        sem = e1_r.at[i], sides[i % 2]
        if i < 4:
            return go(wg_hbm.at[piece(i)], relay_g.at[i], *sem)
        return go(wd_hbm.at[piece(i)], relay_d.at[i - 4], *sem)

    def second_hop(i, arrived):
        arrived.wait_recv()
        sem = e2_r.at[i], sides[i % 2]
        if i < 4:
            return go(relay_g.at[i], raw.at[1, piece(i)], *sem)
        return go(relay_d.at[i - 4], wdb.at[1, piece(i)], *sem)

    ex1 = [first_hop(i) for i in range(4)]

    with jax.named_scope("visible"):
        upper = jnp.where(iota((64, 64), 0) <= iota((64, 64), 1), 1.0, 0.0).astype(BF16)
        lens = jnp.broadcast_to(len_ref[...].astype(F32).reshape(1, 64), (16, 64)).astype(BF16)
        ends = jnp.dot(lens, upper, preferred_element_type=F32)[0:1, :]
        qpos = (s * 64 + iota((64, 64), 0)).astype(F32)
        first = jnp.max(jnp.where(ends <= qpos, ends, 0.0), axis=-1, keepdims=True)
        kpos = (s * 64 - 256 + iota((64, 320), 1)).astype(F32)
        qcol = (s * 64 + iota((64, 320), 0)).astype(F32)
        seen = jnp.where((kpos >= first) & (kpos <= qcol), 0.0, NEGATIVE)
        seen3 = jnp.concatenate([seen, seen, seen], axis=0)

    with jax.named_scope("wait_first_columns"):
        for c in owz:
            c.wait_recv()
    owx = {
        d: go(owbuf.at[:, x], owbuf.at[:, x], owx_r.at[d], pdev[(0, d)])
        for d in (1, 3)
    }
    with jax.named_scope("wait_keys"):
        own_k.wait()
        own_v.wait()
        own_q.wait()
        for c in kv:
            c.wait_recv()
    with jax.named_scope("attention"):
        for g in range(2):
            cols = slice(g * HD, (g + 1) * HD)
            qs = jnp.concatenate(
                [qbuf[:, (3 * g + i) * HD : (3 * g + i + 1) * HD] for i in range(3)], axis=0
            )
            sc = lax.dot_general(qs, kwin[:, cols], NT, preferred_element_type=F32)
            sc = jnp.where(seen3 < -1.0, NEGATIVE, sc * (1.0 / math.sqrt(HD)))
            w = jnp.exp(sc - jnp.max(sc, axis=-1, keepdims=True))
            total = jnp.sum(w, axis=-1, keepdims=True)
            o = jnp.dot(w.astype(BF16), vwin[:, cols], preferred_element_type=F32)
            o = (o / total).astype(BF16)
            for i in range(3):
                hbuf[y, :, (3 * g + i) * HD : (3 * g + i + 1) * HD] = o[i * 64 : (i + 1) * 64]
    hy = [
        go(hbuf.at[y], hbuf.at[y], hy_r.at[d], pdev[(d, 0)]) for d in (1, 3, 2)
    ]

    rp = [
        go(rpb.at[0], rpb.at[SLOT[NZ - d]], rp_r.at[d], zdev[d]) for d in ZORDER
    ]
    with jax.named_scope("gate_up"):
        own_wg.wait()
        wgb[0, 0:768, 0:256] = raw[0, 0:768, 0, :]
        wgb[0, 0:768, 256:512] = raw[0, 0:768, 1, :]
    with jax.named_scope("wait_columns"):
        left, right = up(x, 3, NX), up(x, 1, NX)
        owx[1].wait_recv()
        lower = owbuf.at[0:4, left]
        fwd = [go(lower, lower, owx_r.at[0], pdev[(0, 1)])]
        owx[3].wait_recv()
        higher = owbuf.at[4:8, right]
        fwd.append(go(higher, higher, owx_r.at[2], pdev[(0, 3)]))
        for c in shy:
            c.wait_recv()
    with jax.named_scope("wait_far_columns"):
        for c in fwd:
            c.wait_recv()
    shx = [
        go(shb.at[:, x, h], shb.at[:, x, h], shx_r.at[d], pdev[(0, d)])
        for d in (1, 3, 2)
    ]
    with jax.named_scope("relay_gate"):
        ex2 = [second_hop(i, ex1[i]) for i in range(2)]
    with jax.named_scope("columns"):
        col, row = iota((384, 512), 0), iota((384, 512), 1)
        pick = jnp.where(row == lax.div(col, 12) * 16 + lax.rem(col, 12), 1.0, 0.0).astype(BF16)
        wc[...] = jnp.dot(
            pick, owbuf[...].reshape(512, 768), preferred_element_type=F32
        ).astype(BF16)

    with jax.named_scope("wait_heads"):
        for c in hy:
            c.wait_recv()
    with jax.named_scope("project"):
        po = lax.dot_general(hbuf[...].reshape(256, 768), wc[...], NT, preferred_element_type=F32)
        part[...] = po.reshape(4, 2, 32, 384).astype(BF16)
    rs = []
    for d in (1, 3, 2):
        yd = up(y, d, NY)
        for i, hd in enumerate((h, 1 - h)):
            rs.append(
                go(part.at[yd, hd], rbuf.at[y, h], rs_r.at[i, d], (seq_of(yd, z, x), hd))
            )
    rs.append(go(part.at[y, 1 - h], rbuf.at[y, h], rs_r.at[1, 0], sib))
    rbuf[y, h] = part[y, h]
    with jax.named_scope("relay_gate_rest"):
        ex2 += [second_hop(i, ex1[i]) for i in range(2, 4)]
        ex1 += [first_hop(i) for i in range(4, 6)]
    with jax.named_scope("gate_up_rest"):
        wgb[0, 768:1536, 0:256] = raw[0, 768:1536, 0, :]
        wgb[0, 768:1536, 256:512] = raw[0, 768:1536, 1, :]
    with jax.named_scope("wait_projected"):
        for c in rs:
            c.wait_recv()
    with jax.named_scope("norm"):
        own_res.wait()
        attn = [rbuf[j, 0].astype(F32) + rbuf[j, 1].astype(F32) for j in range(NY)]
        mixed = resbuf[...].astype(F32) + jnp.concatenate(attn, axis=1)
        ms = jnp.mean(mixed * mixed, axis=-1, keepdims=True)
        xb[0] = (mixed * lax.rsqrt(ms + EPSILON) * gain_ref[...].reshape(1, 1536)).astype(BF16)
    xz = {
        d: go(xb.at[0], xb.at[SLOT[NZ - d]], xz_r.at[d], zdev[d]) for d in (2, 6, 1, 7)
    }
    ex2g = ex2
    with jax.named_scope("gate_sibling"):
        for c in ex2g:
            c.wait_recv()
        sib_g = go(raw.at[1, rows_g], raw.at[1, rows_g], sib_r.at[1], sib)
    with jax.named_scope("choose"):
        for c in rp:
            c.wait_recv()
        lane = iota((128, COLS), 1)
        half = lax.div(lane, COLS // 2)
        expert = lax.rem(y + half, 2) * 32 + z * NX + lax.rem(lax.div(lane, ROWS), NX)
        row = iota((128, COLS), 0)
        of_rank = jnp.where(row == expert, 1.0, 0.0).astype(BF16)
        of_prob = jnp.where(row == expert + EXPERTS, 1.0, 0.0).astype(BF16)
        slot = lax.rem(iota((128, COLS), 1), ROWS)
        member = lax.div(row, 32) == lax.div(slot, CAP)
        number = lax.rem(slot, CAP).astype(F32)
        picks, weights = [], []
        for c in range(2):
            rpc = rpb[4 * c : 4 * c + 4].reshape(128, 128).astype(BF16)
            rank = jnp.dot(rpc, of_rank, preferred_element_type=F32)
            prob = jnp.dot(rpc, of_prob, preferred_element_type=F32)
            hit = member & (rank == number)
            picks.append(jnp.transpose(jnp.where(hit, 1.0, 0.0)).astype(BF16))
            weights.append(jnp.where(hit, prob, 0.0).astype(BF16))

    with jax.named_scope("wait_near_rows"):
        xz[2].wait_recv()
        low = pl.ds(0, 16)
        xz[4] = go(
            xb.at[SLOT[6], low], xb.at[SLOT[4], low], xz_r.at[4], zdev[2]
        )
        xz[3] = go(xb.at[SLOT[6]], xb.at[SLOT[5]], xz_r.at[3], zdev[1])
        xz[6].wait_recv()
        high = pl.ds(16, 16)
        xz[0] = go(
            xb.at[SLOT[2], high], xb.at[SLOT[4], high], xz_r.at[0], zdev[6]
        )
        xz[5] = go(xb.at[SLOT[2]], xb.at[SLOT[3]], xz_r.at[5], zdev[7])
        xz[1].wait_recv()
        xz[7].wait_recv()

    turn = 1 + 2 * lax.rem(x, 2)

    def to_expert(p, d):
        return pdev[(0, d)] if p == 0 else (seq_of(up(y, turn, NY), z, up(x, d, NX)), h)

    def to_source(p, d):
        xs = up(x, NX - d, NX)
        if p == 0:
            return pdev[(0, NX - d)]
        return (seq_of(up(y, 3 - 2 * lax.rem(xs, 2), NY), z, xs), h)

    hops = [(p, d) for p in range(2) for d in (2, 1, 3, 0) if (p, d) != (0, 0)]
    before = pdev[(0, 3)]

    def dispatch(c):
        xc = xb[4 * c : 4 * c + 4].reshape(128, 1536)
        rows = jnp.dot(picks[c], xc, preferred_element_type=F32)
        for j in range(8):
            dsend[c, j] = rows[j * ROWS : (j + 1) * ROWS].astype(BF16)
        copies = [go(dsend.at[c, up(x, 2, NX)], relay_x.at[c], q_r.at[c], before)]
        for i, (p, d) in enumerate(hops[1:], 1):
            copies.append(
                go(
                    dsend.at[c, p * NX + up(x, d, NX)], drecv.at[c, p * NX + x],
                    d_r.at[c, i], to_expert(p, d),
                )
            )
        drecv[c, x] = dsend[c, x]
        return copies

    def pass_on(c, copies):
        copies[0].wait_recv()
        copies[0] = go(
            relay_x.at[c], drecv.at[c, up(x, 1, NX)], d_r.at[c, 0], before
        )

    sent = {}
    with jax.named_scope("dispatch"):
        sent[1] = dispatch(1)
    with jax.named_scope("relay_down"):
        ex2 = [second_hop(i, ex1[i]) for i in range(4, 6)]
    with jax.named_scope("gate_up_other"):
        sib_g.wait_recv()
        wgb[1, :, 0:256] = raw[1, :, 0, :]
        wgb[1, :, 256:512] = raw[1, :, 1, :]
    with jax.named_scope("pass_on"):
        pass_on(1, sent[1])
    with jax.named_scope("wait_rows"):
        for d in (3, 5, 4, 0):
            xz[d].wait_recv()
    with jax.named_scope("dispatch"):
        sent[0] = dispatch(0)
    with jax.named_scope("shared_weights"):
        for m in shx:
            m.wait_recv()
        sib_sh = go(shb.at[:, :, h], shb.at[:, :, h], sib_r.at[0], sib)
    cz = [
        go(cache_hbm.at[:, up(z, d, NZ)], cmid_ref.at[z], cz_r.at[d], zdev[d])
        for d in ZORDER
    ]
    with jax.named_scope("pass_on"):
        pass_on(0, sent[0])
    with jax.named_scope("down_sibling"):
        for c in ex2:
            c.wait_recv()
        sib_d = go(wdb.at[1, rows_d], wdb.at[1, rows_d], sib_r.at[2], sib)
    with jax.named_scope("shared"):
        sib_sh.wait_recv()
        xs = xb[...].reshape(256, 1536)
        sh = shb[...].reshape(512, 1536)
        both = lax.dot_general(xs, sh, NT, preferred_element_type=F32)
        act = silu(pltpu.roll(both, 8, 1)) * pltpu.roll(both, 4, 1)
        live = lax.rem(lax.div(iota((256, 512), 1), 4), 4) == 2
        act = jnp.where(live, act, 0.0).astype(BF16)
        shared = jnp.dot(act, sh, preferred_element_type=F32)
    with jax.named_scope("wait_exchange"):
        own_wd.wait()
        sib_d.wait_recv()

    back = {}
    for c in (1, 0):
        with jax.named_scope("wait_dispatch"):
            for m in sent[c]:
                m.wait_recv()
        with jax.named_scope("experts"):
            rows = jnp.concatenate([drecv[c, j].astype(F32) for j in range(8)], axis=0).astype(BF16)
            acc = None
            for j in range(2):
                gu = jnp.dot(rows, wgb[j], preferred_element_type=F32)
                a = (silu(gu[:, :256]) * gu[:, 256:]).astype(BF16)
                o = jnp.dot(a, wdb[j], preferred_element_type=F32)
                acc = o if acc is None else acc + o
            for j in range(8):
                rsend[c, j] = acc[j * ROWS : (j + 1) * ROWS].astype(BF16)
            copies = [
                go(rsend.at[c, up(x, 2, NX)], relay_b.at[c], q_r.at[2 + c], before)
            ]
            for i, (p, d) in enumerate(hops[1:], 1):
                copies.append(
                    go(
                        rsend.at[c, p * NX + up(x, NX - d, NX)], rrecv.at[c, p * NX + x],
                        r_r.at[c, i], to_source(p, d),
                    )
                )
            back[c] = copies
            rrecv[c, x] = rsend[c, x]
    with jax.named_scope("pass_back"):
        for c in (1, 0):
            back[c][0].wait_recv()
            back[c][0] = go(
                relay_b.at[c], rrecv.at[c, up(x, 1, NX)], r_r.at[c, 0], before
            )

    def combined(c):
        for m in back[c]:
            m.wait_recv()
        rows = jnp.concatenate([rrecv[c, j].astype(F32) for j in range(8)], axis=0).astype(BF16)
        return shared[128 * c : 128 * c + 128] + jnp.dot(
            weights[c], rows, preferred_element_type=F32
        )

    with jax.named_scope("combine_near"):
        tot = combined(1)
        pz[4:6] = tot[0:64].astype(BF16).reshape(2, 32, 1536)

        def to_line(o):
            return go(
                pz.at[SLOT[o]], racc.at[SLOT[NZ - o] - 3], z_r.at[SLOT[o]], zdev[o]
            )

        red = [to_line(1), to_line(7)]
    with jax.named_scope("combine_far"):
        pz[0:4] = combined(0).astype(BF16).reshape(4, 32, 1536)
        far = [
            go(pz.at[SLOT[3]], relay_3.at[0], z_r.at[0], zdev[1]),
            go(pz.at[SLOT[5]], relay_3.at[1], z_r.at[1], zdev[7]),
            go(pz.at[SLOT[4], low], relay_4.at[0], z_r.at[2], zdev[2]),
            go(pz.at[SLOT[4], high], relay_4.at[1], z_r.at[3], zdev[6]),
        ]
    with jax.named_scope("cache_plane"):
        own_cache.wait()
        for c in cz:
            c.wait_recv()
        cp = [
            go(
                cmid_ref.at[:, up(y, at[0], NY), up(x, at[1], NX)], chand_ref.at[y, :, x],
                cp_r.at[i], pdev[at],
            )
            for i, at in enumerate(plane)
        ]
        cp_own = here(cmid_ref.at[:, y, x], chand_ref.at[y, :, x])
    with jax.named_scope("wait_far"):
        for m in far:
            m.wait_recv()
    with jax.named_scope("add_far"):
        none = jnp.zeros((16, 1536), F32)
        plus = (
            tot[64:96] + relay_3[0].astype(F32)
            + jnp.concatenate([relay_4[0].astype(F32), none], axis=0)
        )
        minus = (
            tot[96:128] + relay_3[1].astype(F32)
            + jnp.concatenate([none, relay_4[1].astype(F32)], axis=0)
        )
        pz[SLOT[2]] = plus.astype(BF16)
        pz[SLOT[6]] = minus.astype(BF16)
        red += [to_line(2), to_line(6)]
    racc[0] = pz[0]
    with jax.named_scope("wait_sum"):
        for c in red:
            c.wait_recv()
    out = mixed
    for j in range(5):
        out = out + racc[j].astype(F32)
    out_ref[...] = out.astype(BF16)
    with jax.named_scope("drain"):
        cp_own.wait()
        for c in cp:
            c.wait_recv()
        for c in pending[-POOL:]:
            c.wait_send()


def shards(
    queries, key_vectors, value_vectors, lengths, out_weight, residual, norm_gain, route_ids,
    route_logits, shared_gate_up, shared_down, expert_gate_up, expert_down, cache_blocks, block_table,
):
    hbm, vmem = pl.BlockSpec(memory_space=pltpu.HBM), pl.BlockSpec(memory_space=pltpu.VMEM)
    dma = pltpu.SemaphoreType.DMA
    sgu = jnp.transpose(shared_gate_up, (1, 2, 0))
    wg = expert_gate_up.reshape(1536, 2, 256)
    wd = expert_down.reshape(256, 1536)
    cache = cache_blocks.reshape(NY, NZ, NX, 8, 2, HD)
    sds = jax.ShapeDtypeStruct
    layer_out, _, chand = pl.pallas_call(
        layer_kernel,
        out_shape=(
            sds((32, 1536), BF16),
            sds((NZ, NY, NX, 8, 2, HD), BF16),
            sds((NY, NZ, NX, 8, 2, HD), BF16),
        ),
        in_specs=[hbm, hbm, hbm, vmem, vmem, hbm, vmem, vmem, vmem, vmem, vmem, hbm, hbm, hbm],
        out_specs=(vmem, hbm, hbm),
        scratch_shapes=[
            pltpu.VMEM((64, 768), BF16),
            pltpu.VMEM((320, 256), BF16),
            pltpu.VMEM((320, 256), BF16),
            pltpu.VMEM((32, 1536), BF16),
            pltpu.VMEM((16, 768), BF16),
            pltpu.VMEM((NZ, NX, 16, 768), BF16),
            pltpu.VMEM((384, 768), BF16),
            pltpu.VMEM((NY, 64, 768), BF16),
            pltpu.VMEM((NY, 2, 32, 384), BF16),
            pltpu.VMEM((NY, 2, 32, 384), BF16),
            pltpu.VMEM((NZ, 32, 1536), BF16),
            pltpu.VMEM((NZ, 32, 128), F32),
            pltpu.VMEM((16, 1536), BF16),
            pltpu.VMEM((NY, NX, 2, 16, 1536), BF16),
            pltpu.VMEM((2, 1536, 2, 256), BF16),
            pltpu.VMEM((2, 1536, 512), BF16),
            pltpu.VMEM((2, 256, 1536), BF16),
            pltpu.VMEM((4, 192, 2, 256), BF16),
            pltpu.VMEM((2, 64, 1536), BF16),
            pltpu.VMEM((2, ROWS, 1536), BF16),
            pltpu.VMEM((2, ROWS, 1536), BF16),
            pltpu.VMEM((2, 32, 1536), BF16),
            pltpu.VMEM((2, 16, 1536), BF16),
            pltpu.VMEM((2, 8, ROWS, 1536), BF16),
            pltpu.VMEM((2, 8, ROWS, 1536), BF16),
            pltpu.VMEM((2, 8, ROWS, 1536), BF16),
            pltpu.VMEM((2, 8, ROWS, 1536), BF16),
            pltpu.VMEM((NZ, 32, 1536), BF16),
            pltpu.VMEM((5, 32, 1536), BF16),
            dma((POOL,)),
            dma((2, 4)),
            dma((8,)),
            dma((4,)),
            dma((8,)),
            dma((4,)),
            dma((4,)),
            dma((8,)),
            dma((15,)),
            dma((6,)),
            dma((6,)),
            dma((3,)),
            dma((4,)),
            dma((2, 4)),
            dma((8,)),
            dma((2, 7)),
            dma((4,)),
            dma((2, 7)),
            dma((9,)),
            dma((8,)),
        ],
        compiler_params=pltpu.CompilerParams(
            collective_id=0, has_side_effects=True, vmem_limit_bytes=56 << 20
        ),
        name="layer",
    )(
        queries, key_vectors, value_vectors, lengths, out_weight.T, residual, norm_gain,
        route_ids.T, route_logits.T, sgu, shared_down, wg, wd, cache,
    )
    cache_out = jnp.take(
        chand.reshape(128, 1, 8, 2, HD), block_table, axis=0, mode="clip"
    )
    return layer_out, cache_out


def solution(mesh):
    in_specs = (
        P("seq", "head"),
        P("seq", "head"),
        P("seq", "head"),
        P(),
        P("head", "seq"),
        P(("seq", "head"), None),
        P(),
        P(("seq", "head"), None),
        P(("seq", "head"), None),
        P(None, None, ("seq", "head")),
        P(("seq", "head"), None),
        P("seq", None, None, None),
        P("seq", None, None),
        P("seq", None, None, "head", None),
        P(),
    )
    out_specs = (P(("seq", "head"), None), P(None, "seq", None, "head", None))
    return jax.shard_map(shards, mesh=mesh, in_specs=in_specs, out_specs=out_specs, check_vma=False)
```

```python
import functools
import math

import jax
import jax.numpy as jnp
from jax import lax
from jax.experimental import pallas as pl
from jax.experimental.pallas import tpu as pltpu
from jax.sharding import PartitionSpec as P

MESH = pl.DeviceIdType.MESH
HD = 128
NY, NZ, NX = 4, 8, 4
TOP = 6
CAP = 6
EXPERTS = 64
NEGATIVE = -1e30
EPSILON = 1e-05
F32 = jnp.float32
BF16 = jnp.bfloat16
ZORDER = (1, 7, 2, 6, 3, 5, 4)
OFF = (0, 3, 5, 4, 1, 7, 2, 6)
SLOT = {o: k for k, o in enumerate(OFF)}
ROWS = 24
POOL = 48
COLS = 8 * ROWS
NT = (((1,), (1,)), ((), ()))


def place():
    s = lax.axis_index("seq")
    h = lax.axis_index("head")
    y = lax.div(s, NZ * NX)
    z = lax.rem(lax.div(s, NX), NZ)
    x = lax.rem(s, NX)
    return s, h, y, z, x


def seq_of(y, z, x):
    return y * (NZ * NX) + z * NX + x


def up(i, by, n):
    return lax.rem(i + by, n)


def rcopy(src, dst, ssem, rsem, dev):
    return pltpu.make_async_remote_copy(
        src_ref=src, dst_ref=dst, send_sem=ssem, recv_sem=rsem, device_id=dev, device_id_type=MESH
    )


def iota(shape, axis):
    return lax.broadcasted_iota(jnp.int32, shape, axis)


def silu(v):
    return v / (1.0 + jnp.exp(-v))


def routing_table(ids, logits):
    top = jnp.max(logits, axis=0, keepdims=True)
    e = jnp.exp(logits - top)
    probs = e / jnp.sum(e, axis=0, keepdims=True)
    row = iota((128, 32), 0)
    named = jnp.zeros((128, 32), F32)
    weight = jnp.zeros((128, 32), F32)
    for r in range(TOP):
        idr = jnp.broadcast_to(ids[r : r + 1, :], (128, 32))
        named = named + jnp.where(row == idr, 1.0, 0.0)
        weight = weight + jnp.where(row - EXPERTS == idr, probs[r : r + 1, :], 0.0)
    before = jnp.where(iota((32, 32), 0) < iota((32, 32), 1), 1.0, 0.0)
    rank = jnp.dot(named.astype(BF16), before.astype(BF16), preferred_element_type=F32)
    table = jnp.where(row < EXPERTS, jnp.where(named > 0.5, rank, -1.0), weight)
    return jnp.transpose(table)


def layer_kernel(
    q_hbm, k_hbm, v_hbm, len_ref, ow_ref, res_hbm, gain_ref, ids_ref, log_ref,
    sgu_ref, sd_ref, wg_hbm, wd_hbm, cache_hbm,
    out_ref, cmid_ref, chand_ref,
    qbuf, kwin, vwin, resbuf, owpad, owbuf, ocol, wc, hbuf, part, rbuf, xb, rpb, shpad, shb, raw, wgb, wdb,
    relay_g, relay_d, relay_x, relay_b, relay_3, relay_4, dsend, drecv, rsend, rrecv, pz, racc,
    pool, kv_r, owz_r, owx_r, rp_r, shy_r, shx_r, cz_r, cp_r, e1_r, e2_r, sib_r, hy_r,
    rs_r, xz_r, d_r, q_r, r_r, z_r, loc,
):
    s, h, y, z, x = place()
    seqs = NY * NZ * NX
    zdev = {d: (seq_of(y, up(z, d, NZ), x), h) for d in range(1, NZ)}
    plane = [
        (dy, dx) for dy in range(NY) for dx in range(NX) if (dy, dx) != (0, 0)
    ]
    pdev = {at: (seq_of(up(y, at[0], NY), z, up(x, at[1], NX)), h) for at in plane}
    sib = (s, 1 - h)
    cross = [(seq_of(up(y, dy, NY), z, x), 1 - h) for dy in (1, 2, 3)]
    ahead = [(lax.rem(s + by, seqs), h) for by in range(1, 5)]
    behind = [(lax.rem(s + seqs - by, seqs), h) for by in range(1, 5)]

    local = []

    def here(src, dst):
        copy = pltpu.make_async_copy(src, dst, loc.at[len(local)])
        copy.start()
        local.append(copy)
        return copy

    own_wg = here(wg_hbm, raw.at[0])
    own_k = here(k_hbm, kwin.at[pl.ds(256, 64)])
    own_v = here(v_hbm, vwin.at[pl.ds(256, 64)])
    own_q = here(q_hbm, qbuf)
    own_cache = here(cache_hbm.at[:, z], cmid_ref.at[z])
    own_res = here(res_hbm, resbuf)
    own_wd = here(wd_hbm, wdb.at[0])
    peers = list(zdev.values()) + list(pdev.values()) + [sib] + cross + ahead + behind
    barrier = pltpu.get_barrier_semaphore()
    for dev in peers:
        pl.semaphore_signal(barrier, inc=1, device_id=dev, device_id_type=MESH)

    with jax.named_scope("pack"):
        owpad[...] = jnp.concatenate(
            [ow_ref[...].astype(F32), jnp.zeros((4, 768), F32)], axis=0
        ).astype(BF16)
        owbuf[z] = owpad[...]
        shpad[...] = jnp.concatenate(
            [
                sgu_ref[...].astype(F32).reshape(8, 1536),
                sd_ref[...].astype(F32),
                jnp.zeros((4, 1536), F32),
            ],
            axis=0,
        ).astype(BF16)
        shb[y, x, h] = shpad[...]
    with jax.named_scope("routing"):
        rpb[0] = routing_table(ids_ref[...], log_ref[...])
    with jax.named_scope("enter"):
        pl.semaphore_wait(barrier, len(peers))

    pending = []

    def go(src, dst, recv, dev):
        turn = len(pending)
        if turn >= POOL:
            pending[turn - POOL].wait_send()
        copy = rcopy(src, dst, pool.at[turn % POOL], recv, dev)
        copy.start()
        pending.append(copy)
        return copy

    owz = [go(owpad, owbuf.at[z], owz_r.at[d], zdev[d]) for d in ZORDER]
    kv = []
    for by in range(1, 5):
        rows = pl.ds(64 * (4 - by), 64)
        kv.append(go(k_hbm, kwin.at[rows], kv_r.at[0, by - 1], ahead[by - 1]))
        kv.append(go(v_hbm, vwin.at[rows], kv_r.at[1, by - 1], ahead[by - 1]))
    shy = [
        go(shpad, shb.at[y, x, h], shy_r.at[d], pdev[(d, 0)]) for d in (1, 3, 2)
    ]
    sides = (pdev[(1, 0)], pdev[(3, 0)])
    rows_g, rows_d = pl.ds(h * 768, 768), pl.ds(h * 128, 128)

    def piece(i):
        if i < 4:
            return pl.ds(h * 768 + i * 192, 192)
        return pl.ds(h * 128 + (i - 4) * 64, 64)

    def first_hop(i):
        sem = e1_r.at[i], sides[i % 2]
        if i < 4:
            return go(wg_hbm.at[piece(i)], relay_g.at[i], *sem)
        return go(wd_hbm.at[piece(i)], relay_d.at[i - 4], *sem)

    def second_hop(i, arrived):
        arrived.wait_recv()
        sem = e2_r.at[i], sides[i % 2]
        if i < 4:
            return go(relay_g.at[i], raw.at[1, piece(i)], *sem)
        return go(relay_d.at[i - 4], wdb.at[1, piece(i)], *sem)

    ex1 = [first_hop(i) for i in range(4)]

    with jax.named_scope("visible"):
        upper = jnp.where(iota((64, 64), 0) <= iota((64, 64), 1), 1.0, 0.0).astype(BF16)
        lens = jnp.broadcast_to(len_ref[...].astype(F32).reshape(1, 64), (16, 64)).astype(BF16)
        ends = jnp.dot(lens, upper, preferred_element_type=F32)[0:1, :]
        qpos = (s * 64 + iota((64, 64), 0)).astype(F32)
        first = jnp.max(jnp.where(ends <= qpos, ends, 0.0), axis=-1, keepdims=True)
        kpos = (s * 64 - 256 + iota((64, 320), 1)).astype(F32)
        qcol = (s * 64 + iota((64, 320), 0)).astype(F32)
        seen = jnp.where((kpos >= first) & (kpos <= qcol), 0.0, NEGATIVE)
        seen3 = jnp.concatenate([seen, seen, seen], axis=0)

    col, row = iota((96, 128), 0), iota((96, 128), 1)
    pack = jnp.where(row == lax.div(col, 12) * 16 + lax.rem(col, 12), 1.0, 0.0).astype(BF16)
    with jax.named_scope("wait_first_columns"):
        for c in owz:
            c.wait_recv()
    ocol[x] = jnp.dot(
        pack, owbuf[...].reshape(128, 768), preferred_element_type=F32
    ).astype(BF16)
    owx = {
        d: go(ocol.at[x], ocol.at[x], owx_r.at[d], pdev[(0, d)])
        for d in (1, 3)
    }
    with jax.named_scope("wait_keys"):
        own_k.wait()
        own_v.wait()
        own_q.wait()
        for c in kv:
            c.wait_recv()
    with jax.named_scope("attention"):
        for g in range(2):
            cols = slice(g * HD, (g + 1) * HD)
            qs = jnp.concatenate(
                [qbuf[:, (3 * g + i) * HD : (3 * g + i + 1) * HD] for i in range(3)], axis=0
            )
            sc = lax.dot_general(qs, kwin[:, cols], NT, preferred_element_type=F32)
            sc = jnp.where(seen3 < -1.0, NEGATIVE, sc * (1.0 / math.sqrt(HD)))
            w = jnp.exp(sc - jnp.max(sc, axis=-1, keepdims=True))
            total = jnp.sum(w, axis=-1, keepdims=True)
            o = jnp.dot(w.astype(BF16), vwin[:, cols], preferred_element_type=F32)
            o = (o / total).astype(BF16)
            for i in range(3):
                hbuf[y, :, (3 * g + i) * HD : (3 * g + i + 1) * HD] = o[i * 64 : (i + 1) * 64]
    hy = [
        go(hbuf.at[y], hbuf.at[y], hy_r.at[d], pdev[(d, 0)]) for d in (1, 3, 2)
    ]

    rp = [
        go(rpb.at[0], rpb.at[SLOT[NZ - d]], rp_r.at[d], zdev[d]) for d in ZORDER
    ]
    with jax.named_scope("gate_up"):
        own_wg.wait()
        wgb[0, 0:768, 0:256] = raw[0, 0:768, 0, :]
        wgb[0, 0:768, 256:512] = raw[0, 0:768, 1, :]
    with jax.named_scope("wait_columns"):
        left, right = up(x, 3, NX), up(x, 1, NX)
        owx[1].wait_recv()
        lower = ocol.at[left, 0:48]
        fwd = [go(lower, lower, owx_r.at[0], pdev[(0, 1)])]
        owx[3].wait_recv()
        higher = ocol.at[right, 48:96]
        fwd.append(go(higher, higher, owx_r.at[2], pdev[(0, 3)]))
        for c in shy:
            c.wait_recv()
    with jax.named_scope("wait_far_columns"):
        for c in fwd:
            c.wait_recv()
    shx = [
        go(shb.at[:, x, h], shb.at[:, x, h], shx_r.at[d], pdev[(0, d)])
        for d in (1, 3, 2)
    ]
    with jax.named_scope("relay_gate"):
        ex2 = [second_hop(i, ex1[i]) for i in range(2)]
    with jax.named_scope("columns"):
        col, row = iota((384, 384), 0), iota((384, 384), 1)
        source = (
            lax.div(lax.rem(col, 48), 12) * 96 + lax.div(col, 48) * 12 + lax.rem(col, 12)
        )
        order = jnp.where(row == source, 1.0, 0.0).astype(BF16)
        wc[...] = jnp.dot(
            order, ocol[...].reshape(384, 768), preferred_element_type=F32
        ).astype(BF16)

    with jax.named_scope("wait_heads"):
        for c in hy:
            c.wait_recv()
    with jax.named_scope("project"):
        po = lax.dot_general(hbuf[...].reshape(256, 768), wc[...], NT, preferred_element_type=F32)
        part[...] = po.reshape(4, 2, 32, 384).astype(BF16)
    rs = []
    for d in (1, 3, 2):
        yd = up(y, d, NY)
        for i, hd in enumerate((h, 1 - h)):
            rs.append(
                go(part.at[yd, hd], rbuf.at[y, h], rs_r.at[i, d], (seq_of(yd, z, x), hd))
            )
    rs.append(go(part.at[y, 1 - h], rbuf.at[y, h], rs_r.at[1, 0], sib))
    rbuf[y, h] = part[y, h]
    with jax.named_scope("relay_gate_rest"):
        ex2 += [second_hop(i, ex1[i]) for i in range(2, 4)]
        ex1 += [first_hop(i) for i in range(4, 6)]
    with jax.named_scope("gate_up_rest"):
        wgb[0, 768:1536, 0:256] = raw[0, 768:1536, 0, :]
        wgb[0, 768:1536, 256:512] = raw[0, 768:1536, 1, :]
    with jax.named_scope("wait_projected"):
        for c in rs:
            c.wait_recv()
    with jax.named_scope("norm"):
        own_res.wait()
        attn = [rbuf[j, 0].astype(F32) + rbuf[j, 1].astype(F32) for j in range(NY)]
        mixed = resbuf[...].astype(F32) + jnp.concatenate(attn, axis=1)
        ms = jnp.mean(mixed * mixed, axis=-1, keepdims=True)
        xb[0] = (mixed * lax.rsqrt(ms + EPSILON) * gain_ref[...].reshape(1, 1536)).astype(BF16)
    xz = {
        d: go(xb.at[0], xb.at[SLOT[NZ - d]], xz_r.at[d], zdev[d]) for d in (2, 6, 1, 7)
    }
    ex2g = ex2
    with jax.named_scope("gate_sibling"):
        for c in ex2g:
            c.wait_recv()
        sib_g = go(raw.at[1, rows_g], raw.at[1, rows_g], sib_r.at[1], sib)
    with jax.named_scope("choose"):
        for c in rp:
            c.wait_recv()
        lane = iota((128, COLS), 1)
        half = lax.div(lane, COLS // 2)
        expert = lax.rem(y + half, 2) * 32 + z * NX + lax.rem(lax.div(lane, ROWS), NX)
        row = iota((128, COLS), 0)
        of_rank = jnp.where(row == expert, 1.0, 0.0).astype(BF16)
        of_prob = jnp.where(row == expert + EXPERTS, 1.0, 0.0).astype(BF16)
        slot = lax.rem(iota((128, COLS), 1), ROWS)
        member = lax.div(row, 32) == lax.div(slot, CAP)
        number = lax.rem(slot, CAP).astype(F32)
        picks, weights = [], []
        for c in range(2):
            rpc = rpb[4 * c : 4 * c + 4].reshape(128, 128).astype(BF16)
            rank = jnp.dot(rpc, of_rank, preferred_element_type=F32)
            prob = jnp.dot(rpc, of_prob, preferred_element_type=F32)
            hit = member & (rank == number)
            picks.append(jnp.transpose(jnp.where(hit, 1.0, 0.0)).astype(BF16))
            weights.append(jnp.where(hit, prob, 0.0).astype(BF16))

    with jax.named_scope("wait_near_rows"):
        xz[2].wait_recv()
        low = pl.ds(0, 16)
        xz[4] = go(
            xb.at[SLOT[6], low], xb.at[SLOT[4], low], xz_r.at[4], zdev[2]
        )
        xz[3] = go(xb.at[SLOT[6]], xb.at[SLOT[5]], xz_r.at[3], zdev[1])
        xz[6].wait_recv()
        high = pl.ds(16, 16)
        xz[0] = go(
            xb.at[SLOT[2], high], xb.at[SLOT[4], high], xz_r.at[0], zdev[6]
        )
        xz[5] = go(xb.at[SLOT[2]], xb.at[SLOT[3]], xz_r.at[5], zdev[7])
        xz[1].wait_recv()
        xz[7].wait_recv()

    turn = 1 + 2 * lax.rem(x, 2)

    def to_expert(p, d):
        return pdev[(0, d)] if p == 0 else (seq_of(up(y, turn, NY), z, up(x, d, NX)), h)

    def to_source(p, d):
        xs = up(x, NX - d, NX)
        if p == 0:
            return pdev[(0, NX - d)]
        return (seq_of(up(y, 3 - 2 * lax.rem(xs, 2), NY), z, xs), h)

    hops = [(p, d) for p in range(2) for d in (2, 1, 3, 0) if (p, d) != (0, 0)]
    before = pdev[(0, 3)]

    def dispatch(c):
        xc = xb[4 * c : 4 * c + 4].reshape(128, 1536)
        rows = jnp.dot(picks[c], xc, preferred_element_type=F32)
        for j in range(8):
            dsend[c, j] = rows[j * ROWS : (j + 1) * ROWS].astype(BF16)
        copies = [go(dsend.at[c, up(x, 2, NX)], relay_x.at[c], q_r.at[c], before)]
        for i, (p, d) in enumerate(hops[1:], 1):
            copies.append(
                go(
                    dsend.at[c, p * NX + up(x, d, NX)], drecv.at[c, p * NX + x],
                    d_r.at[c, i], to_expert(p, d),
                )
            )
        drecv[c, x] = dsend[c, x]
        return copies

    def pass_on(c, copies):
        copies[0].wait_recv()
        copies[0] = go(
            relay_x.at[c], drecv.at[c, up(x, 1, NX)], d_r.at[c, 0], before
        )

    sent = {}
    with jax.named_scope("dispatch"):
        sent[1] = dispatch(1)
    with jax.named_scope("relay_down"):
        ex2 = [second_hop(i, ex1[i]) for i in range(4, 6)]
    with jax.named_scope("gate_up_other"):
        sib_g.wait_recv()
        wgb[1, :, 0:256] = raw[1, :, 0, :]
        wgb[1, :, 256:512] = raw[1, :, 1, :]
    with jax.named_scope("pass_on"):
        pass_on(1, sent[1])
    with jax.named_scope("wait_rows"):
        for d in (3, 5, 4, 0):
            xz[d].wait_recv()
    with jax.named_scope("dispatch"):
        sent[0] = dispatch(0)
    with jax.named_scope("shared_weights"):
        for m in shx:
            m.wait_recv()
        sib_sh = go(shb.at[:, :, h], shb.at[:, :, h], sib_r.at[0], sib)
    cz = [
        go(cache_hbm.at[:, up(z, d, NZ)], cmid_ref.at[z], cz_r.at[d], zdev[d])
        for d in ZORDER
    ]
    with jax.named_scope("shared"):
        sib_sh.wait_recv()
        xs = xb[...].reshape(256, 1536)
        sh = shb[...].reshape(512, 1536)
        both = lax.dot_general(xs, sh, NT, preferred_element_type=F32)
        act = silu(pltpu.roll(both, 8, 1)) * pltpu.roll(both, 4, 1)
        live = lax.rem(lax.div(iota((256, 512), 1), 4), 4) == 2
        act = jnp.where(live, act, 0.0).astype(BF16)
        shared = jnp.dot(act, sh, preferred_element_type=F32)
    with jax.named_scope("down_sibling"):
        for c in ex2:
            c.wait_recv()
        sib_d = go(wdb.at[1, rows_d], wdb.at[1, rows_d], sib_r.at[2], sib)
    with jax.named_scope("wait_exchange"):
        own_wd.wait()
        sib_d.wait_recv()

    back = {}
    for c in (1, 0):
        if c == 0:
            with jax.named_scope("pass_on"):
                pass_on(0, sent[0])
        with jax.named_scope("wait_dispatch"):
            for m in sent[c]:
                m.wait_recv()
        with jax.named_scope("experts"):
            rows = jnp.concatenate([drecv[c, j].astype(F32) for j in range(8)], axis=0).astype(BF16)
            acc = None
            for j in range(2):
                gu = jnp.dot(rows, wgb[j], preferred_element_type=F32)
                a = (silu(gu[:, :256]) * gu[:, 256:]).astype(BF16)
                o = jnp.dot(a, wdb[j], preferred_element_type=F32)
                acc = o if acc is None else acc + o
            for j in range(8):
                rsend[c, j] = acc[j * ROWS : (j + 1) * ROWS].astype(BF16)
            copies = [
                go(rsend.at[c, up(x, 2, NX)], relay_b.at[c], q_r.at[2 + c], before)
            ]
            for i, (p, d) in enumerate(hops[1:], 1):
                copies.append(
                    go(
                        rsend.at[c, p * NX + up(x, NX - d, NX)], rrecv.at[c, p * NX + x],
                        r_r.at[c, i], to_source(p, d),
                    )
                )
            back[c] = copies
            rrecv[c, x] = rsend[c, x]
    with jax.named_scope("pass_back"):
        for c in (1, 0):
            back[c][0].wait_recv()
            back[c][0] = go(
                relay_b.at[c], rrecv.at[c, up(x, 1, NX)], r_r.at[c, 0], before
            )

    def combined(c):
        for m in back[c]:
            m.wait_recv()
        rows = jnp.concatenate([rrecv[c, j].astype(F32) for j in range(8)], axis=0).astype(BF16)
        return shared[128 * c : 128 * c + 128] + jnp.dot(
            weights[c], rows, preferred_element_type=F32
        )

    with jax.named_scope("combine_near"):
        tot = combined(1)
        pz[4:6] = tot[0:64].astype(BF16).reshape(2, 32, 1536)

        def to_line(o):
            return go(
                pz.at[SLOT[o]], racc.at[SLOT[NZ - o] - 3], z_r.at[SLOT[o]], zdev[o]
            )
    with jax.named_scope("combine_far"):
        pz[0:4] = combined(0).astype(BF16).reshape(4, 32, 1536)
        far = [
            go(pz.at[SLOT[3]], relay_3.at[0], z_r.at[0], zdev[1]),
            go(pz.at[SLOT[5]], relay_3.at[1], z_r.at[1], zdev[7]),
            go(pz.at[SLOT[4], low], relay_4.at[0], z_r.at[2], zdev[2]),
            go(pz.at[SLOT[4], high], relay_4.at[1], z_r.at[3], zdev[6]),
        ]
        red = [to_line(1), to_line(7)]
    with jax.named_scope("cache_plane"):
        own_cache.wait()
        for c in cz:
            c.wait_recv()
        cp = [
            go(
                cmid_ref.at[:, up(y, at[0], NY), up(x, at[1], NX)], chand_ref.at[y, :, x],
                cp_r.at[i], pdev[at],
            )
            for i, at in enumerate(plane)
        ]
        cp_own = here(cmid_ref.at[:, y, x], chand_ref.at[y, :, x])
    with jax.named_scope("wait_far"):
        for m in far:
            m.wait_recv()
    with jax.named_scope("add_far"):
        none = jnp.zeros((16, 1536), F32)
        plus = (
            tot[64:96] + relay_3[0].astype(F32)
            + jnp.concatenate([relay_4[0].astype(F32), none], axis=0)
        )
        minus = (
            tot[96:128] + relay_3[1].astype(F32)
            + jnp.concatenate([none, relay_4[1].astype(F32)], axis=0)
        )
        pz[SLOT[2]] = plus.astype(BF16)
        pz[SLOT[6]] = minus.astype(BF16)
        red += [to_line(2), to_line(6)]
    racc[0] = pz[0]
    with jax.named_scope("wait_sum"):
        for c in red:
            c.wait_recv()
    out = mixed
    for j in range(5):
        out = out + racc[j].astype(F32)
    out_ref[...] = out
    with jax.named_scope("drain"):
        cp_own.wait()
        for c in cp:
            c.wait_recv()
        for c in pending[-POOL:]:
            c.wait_send()


def shards(
    queries, key_vectors, value_vectors, lengths, out_weight, residual, norm_gain, route_ids,
    route_logits, shared_gate_up, shared_down, expert_gate_up, expert_down, cache_blocks, block_table,
):
    hbm, vmem = pl.BlockSpec(memory_space=pltpu.HBM), pl.BlockSpec(memory_space=pltpu.VMEM)
    dma = pltpu.SemaphoreType.DMA
    sgu = jnp.transpose(shared_gate_up, (1, 2, 0))
    wg = expert_gate_up.reshape(1536, 2, 256)
    wd = expert_down.reshape(256, 1536)
    cache = cache_blocks.reshape(NY, NZ, NX, 8, 2, HD)
    sds = jax.ShapeDtypeStruct
    layer_out, _, chand = pl.pallas_call(
        layer_kernel,
        out_shape=(
            sds((32, 1536), F32),
            sds((NZ, NY, NX, 8, 2, HD), BF16),
            sds((NY, NZ, NX, 8, 2, HD), BF16),
        ),
        in_specs=[hbm, hbm, hbm, vmem, vmem, hbm, vmem, vmem, vmem, vmem, vmem, hbm, hbm, hbm],
        out_specs=(vmem, hbm, hbm),
        scratch_shapes=[
            pltpu.VMEM((64, 768), BF16),
            pltpu.VMEM((320, 256), BF16),
            pltpu.VMEM((320, 256), BF16),
            pltpu.VMEM((32, 1536), BF16),
            pltpu.VMEM((16, 768), BF16),
            pltpu.VMEM((NZ, 16, 768), BF16),
            pltpu.VMEM((NX, 96, 768), BF16),
            pltpu.VMEM((384, 768), BF16),
            pltpu.VMEM((NY, 64, 768), BF16),
            pltpu.VMEM((NY, 2, 32, 384), BF16),
            pltpu.VMEM((NY, 2, 32, 384), BF16),
            pltpu.VMEM((NZ, 32, 1536), BF16),
            pltpu.VMEM((NZ, 32, 128), F32),
            pltpu.VMEM((16, 1536), BF16),
            pltpu.VMEM((NY, NX, 2, 16, 1536), BF16),
            pltpu.VMEM((2, 1536, 2, 256), BF16),
            pltpu.VMEM((2, 1536, 512), BF16),
            pltpu.VMEM((2, 256, 1536), BF16),
            pltpu.VMEM((4, 192, 2, 256), BF16),
            pltpu.VMEM((2, 64, 1536), BF16),
            pltpu.VMEM((2, ROWS, 1536), BF16),
            pltpu.VMEM((2, ROWS, 1536), BF16),
            pltpu.VMEM((2, 32, 1536), BF16),
            pltpu.VMEM((2, 16, 1536), BF16),
            pltpu.VMEM((2, 8, ROWS, 1536), BF16),
            pltpu.VMEM((2, 8, ROWS, 1536), BF16),
            pltpu.VMEM((2, 8, ROWS, 1536), BF16),
            pltpu.VMEM((2, 8, ROWS, 1536), BF16),
            pltpu.VMEM((NZ, 32, 1536), BF16),
            pltpu.VMEM((5, 32, 1536), BF16),
            dma((POOL,)),
            dma((2, 4)),
            dma((8,)),
            dma((4,)),
            dma((8,)),
            dma((4,)),
            dma((4,)),
            dma((8,)),
            dma((15,)),
            dma((6,)),
            dma((6,)),
            dma((3,)),
            dma((4,)),
            dma((2, 4)),
            dma((8,)),
            dma((2, 7)),
            dma((4,)),
            dma((2, 7)),
            dma((9,)),
            dma((8,)),
        ],
        compiler_params=pltpu.CompilerParams(
            collective_id=0, has_side_effects=True, vmem_limit_bytes=56 << 20
        ),
        name="layer",
    )(
        queries, key_vectors, value_vectors, lengths, out_weight.T, residual, norm_gain,
        route_ids.T, route_logits.T, sgu, shared_down, wg, wd, cache,
    )
    cache_out = jnp.take(
        chand.reshape(128, 1, 8, 2, HD), block_table, axis=0, mode="clip"
    )
    return layer_out.astype(BF16), cache_out


def solution(mesh):
    in_specs = (
        P("seq", "head"),
        P("seq", "head"),
        P("seq", "head"),
        P(),
        P("head", "seq"),
        P(("seq", "head"), None),
        P(),
        P(("seq", "head"), None),
        P(("seq", "head"), None),
        P(None, None, ("seq", "head")),
        P(("seq", "head"), None),
        P("seq", None, None, None),
        P("seq", None, None),
        P("seq", None, None, "head", None),
        P(),
    )
    out_specs = (P(("seq", "head"), None), P(None, "seq", None, "head", None))
    return jax.shard_map(shards, mesh=mesh, in_specs=in_specs, out_specs=out_specs, check_vma=False)
```

```python
import functools
import math

import jax
import jax.numpy as jnp
from jax import lax
from jax.experimental import pallas as pl
from jax.experimental.pallas import tpu as pltpu
from jax.sharding import PartitionSpec as P

MESH = pl.DeviceIdType.MESH
HD = 128
NY, NZ, NX = 4, 8, 4
TOP = 6
CAP = 6
EXPERTS = 64
NEGATIVE = -1e30
EPSILON = 1e-05
F32 = jnp.float32
BF16 = jnp.bfloat16
ZORDER = (1, 7, 2, 6, 3, 5, 4)
OFF = (0, 3, 5, 4, 1, 7, 2, 6)
SLOT = {o: k for k, o in enumerate(OFF)}
ROWS = 24
POOL = 48
COLS = 8 * ROWS
NT = (((1,), (1,)), ((), ()))


def place():
    s = lax.axis_index("seq")
    h = lax.axis_index("head")
    y = lax.div(s, NZ * NX)
    z = lax.rem(lax.div(s, NX), NZ)
    x = lax.rem(s, NX)
    return s, h, y, z, x


def seq_of(y, z, x):
    return y * (NZ * NX) + z * NX + x


def up(i, by, n):
    return lax.rem(i + by, n)


def rcopy(src, dst, ssem, rsem, dev):
    return pltpu.make_async_remote_copy(
        src_ref=src, dst_ref=dst, send_sem=ssem, recv_sem=rsem, device_id=dev, device_id_type=MESH
    )


def iota(shape, axis):
    return lax.broadcasted_iota(jnp.int32, shape, axis)


def silu(v):
    return v / (1.0 + jnp.exp(-v))


def routing_table(ids, logits):
    top = jnp.max(logits, axis=0, keepdims=True)
    e = jnp.exp(logits - top)
    probs = e / jnp.sum(e, axis=0, keepdims=True)
    row = iota((128, 32), 0)
    named = jnp.zeros((128, 32), F32)
    weight = jnp.zeros((128, 32), F32)
    for r in range(TOP):
        idr = jnp.broadcast_to(ids[r : r + 1, :], (128, 32))
        named = named + jnp.where(row == idr, 1.0, 0.0)
        weight = weight + jnp.where(row - EXPERTS == idr, probs[r : r + 1, :], 0.0)
    before = jnp.where(iota((32, 32), 0) < iota((32, 32), 1), 1.0, 0.0)
    rank = jnp.dot(named.astype(BF16), before.astype(BF16), preferred_element_type=F32)
    table = jnp.where(row < EXPERTS, jnp.where(named > 0.5, rank, -1.0), weight)
    return jnp.transpose(table)


def layer_kernel(
    q_hbm, k_hbm, v_hbm, len_ref, ow_ref, res_hbm, gain_ref, ids_ref, log_ref,
    sgu_ref, sd_ref, wg_hbm, wd_hbm, cache_hbm,
    out_ref, cmid_ref, chand_ref,
    qbuf, kwin, vwin, resbuf, owpad, owbuf, ocol, wc, hbuf, part, rbuf, xb, rpb, shpad, shb, raw, wgb, wdb,
    relay_g, relay_d, relay_x, relay_b, relay_3, relay_4, dsend, drecv, rsend, rrecv, pz, racc,
    pool, kv_r, owz_r, owx_r, rp_r, shy_r, shx_r, cz_r, cp_r, e1_r, e2_r, sib_r, hy_r,
    rs_r, xz_r, d_r, q_r, r_r, z_r, loc,
):
    s, h, y, z, x = place()
    seqs = NY * NZ * NX
    zdev = {d: (seq_of(y, up(z, d, NZ), x), h) for d in range(1, NZ)}
    plane = [
        (dy, dx) for dy in range(NY) for dx in range(NX) if (dy, dx) != (0, 0)
    ]
    pdev = {at: (seq_of(up(y, at[0], NY), z, up(x, at[1], NX)), h) for at in plane}
    sib = (s, 1 - h)
    cross = [(seq_of(up(y, dy, NY), z, x), 1 - h) for dy in (1, 2, 3)]
    ahead = [(lax.rem(s + by, seqs), h) for by in range(1, 5)]
    behind = [(lax.rem(s + seqs - by, seqs), h) for by in range(1, 5)]

    local = []

    def here(src, dst):
        copy = pltpu.make_async_copy(src, dst, loc.at[len(local)])
        copy.start()
        local.append(copy)
        return copy

    own_wg = here(wg_hbm, raw.at[0])
    own_k = here(k_hbm, kwin.at[pl.ds(256, 64)])
    own_v = here(v_hbm, vwin.at[pl.ds(256, 64)])
    own_q = here(q_hbm, qbuf)
    own_cache = here(cache_hbm.at[:, z], cmid_ref.at[z])
    own_res = here(res_hbm, resbuf)
    own_wd = here(wd_hbm, wdb.at[0])
    peers = list(zdev.values()) + list(pdev.values()) + [sib] + cross + ahead + behind
    barrier = pltpu.get_barrier_semaphore()
    for dev in peers:
        pl.semaphore_signal(barrier, inc=1, device_id=dev, device_id_type=MESH)

    with jax.named_scope("pack"):
        owpad[...] = jnp.concatenate(
            [ow_ref[...].astype(F32), jnp.zeros((4, 768), F32)], axis=0
        ).astype(BF16)
        owbuf[z] = owpad[...]
        shpad[...] = jnp.concatenate(
            [
                sgu_ref[...].astype(F32).reshape(8, 1536),
                sd_ref[...].astype(F32),
                jnp.zeros((4, 1536), F32),
            ],
            axis=0,
        ).astype(BF16)
        shb[y, x, h] = shpad[...]
    with jax.named_scope("routing"):
        rpb[0] = routing_table(ids_ref[...], log_ref[...])
    with jax.named_scope("enter"):
        pl.semaphore_wait(barrier, len(peers))

    pending = []

    def go(src, dst, recv, dev):
        turn = len(pending)
        if turn >= POOL:
            pending[turn - POOL].wait_send()
        copy = rcopy(src, dst, pool.at[turn % POOL], recv, dev)
        copy.start()
        pending.append(copy)
        return copy

    owz = [go(owpad, owbuf.at[z], owz_r.at[d], zdev[d]) for d in ZORDER]
    kv = []
    for by in range(1, 5):
        rows = pl.ds(64 * (4 - by), 64)
        kv.append(go(k_hbm, kwin.at[rows], kv_r.at[0, by - 1], ahead[by - 1]))
        kv.append(go(v_hbm, vwin.at[rows], kv_r.at[1, by - 1], ahead[by - 1]))
    shy = [
        go(shpad, shb.at[y, x, h], shy_r.at[d], pdev[(d, 0)]) for d in (1, 3, 2)
    ]
    sides = (pdev[(1, 0)], pdev[(3, 0)])
    rows_g, rows_d = pl.ds(h * 768, 768), pl.ds(h * 128, 128)

    def piece(i):
        if i < 4:
            return pl.ds(h * 768 + i * 192, 192)
        return pl.ds(h * 128 + (i - 4) * 64, 64)

    def first_hop(i):
        sem = e1_r.at[i], sides[i % 2]
        if i < 4:
            return go(wg_hbm.at[piece(i)], relay_g.at[i], *sem)
        return go(wd_hbm.at[piece(i)], relay_d.at[i - 4], *sem)

    def second_hop(i, arrived):
        arrived.wait_recv()
        sem = e2_r.at[i], sides[i % 2]
        if i < 4:
            return go(relay_g.at[i], raw.at[1, piece(i)], *sem)
        return go(relay_d.at[i - 4], wdb.at[1, piece(i)], *sem)

    ex1 = [first_hop(i) for i in range(4)]

    with jax.named_scope("visible"):
        upper = jnp.where(iota((64, 64), 0) <= iota((64, 64), 1), 1.0, 0.0).astype(BF16)
        lens = jnp.broadcast_to(len_ref[...].astype(F32).reshape(1, 64), (16, 64)).astype(BF16)
        ends = jnp.dot(lens, upper, preferred_element_type=F32)[0:1, :]
        qpos = (s * 64 + iota((64, 64), 0)).astype(F32)
        first = jnp.max(jnp.where(ends <= qpos, ends, 0.0), axis=-1, keepdims=True)
        kpos = (s * 64 - 256 + iota((64, 320), 1)).astype(F32)
        qcol = (s * 64 + iota((64, 320), 0)).astype(F32)
        seen = jnp.where((kpos >= first) & (kpos <= qcol), 0.0, NEGATIVE)
        seen3 = jnp.concatenate([seen, seen, seen], axis=0)

    col, row = iota((96, 128), 0), iota((96, 128), 1)
    pack = jnp.where(row == lax.div(col, 12) * 16 + lax.rem(col, 12), 1.0, 0.0).astype(BF16)
    with jax.named_scope("wait_first_columns"):
        for c in owz:
            c.wait_recv()
    ocol[x] = jnp.dot(
        pack, owbuf[...].reshape(128, 768), preferred_element_type=F32
    ).astype(BF16)
    owx = {
        d: go(ocol.at[x], ocol.at[x], owx_r.at[d], pdev[(0, d)])
        for d in (1, 3)
    }
    with jax.named_scope("wait_keys"):
        own_k.wait()
        own_v.wait()
        own_q.wait()
        for c in kv:
            c.wait_recv()
    with jax.named_scope("attention"):
        for g in range(2):
            cols = slice(g * HD, (g + 1) * HD)
            qs = jnp.concatenate(
                [qbuf[:, (3 * g + i) * HD : (3 * g + i + 1) * HD] for i in range(3)], axis=0
            )
            sc = lax.dot_general(qs, kwin[:, cols], NT, preferred_element_type=F32)
            sc = jnp.where(seen3 < -1.0, NEGATIVE, sc * (1.0 / math.sqrt(HD)))
            w = jnp.exp(sc - jnp.max(sc, axis=-1, keepdims=True))
            total = jnp.sum(w, axis=-1, keepdims=True)
            o = jnp.dot(w.astype(BF16), vwin[:, cols], preferred_element_type=F32)
            o = (o / total).astype(BF16)
            for i in range(3):
                hbuf[y, :, (3 * g + i) * HD : (3 * g + i + 1) * HD] = o[i * 64 : (i + 1) * 64]
    hy = [
        go(hbuf.at[y], hbuf.at[y], hy_r.at[d], pdev[(d, 0)]) for d in (1, 3, 2)
    ]

    rp = [
        go(rpb.at[0], rpb.at[SLOT[NZ - d]], rp_r.at[d], zdev[d]) for d in ZORDER
    ]
    cz = [
        go(cache_hbm.at[:, up(z, d, NZ)], cmid_ref.at[z], cz_r.at[d], zdev[d])
        for d in ZORDER
    ]
    with jax.named_scope("gate_up"):
        own_wg.wait()
        wgb[0, 0:768, 0:256] = raw[0, 0:768, 0, :]
        wgb[0, 0:768, 256:512] = raw[0, 0:768, 1, :]
    with jax.named_scope("wait_columns"):
        left, right = up(x, 3, NX), up(x, 1, NX)
        owx[1].wait_recv()
        lower = ocol.at[left, 0:48]
        fwd = [go(lower, lower, owx_r.at[0], pdev[(0, 1)])]
        owx[3].wait_recv()
        higher = ocol.at[right, 48:96]
        fwd.append(go(higher, higher, owx_r.at[2], pdev[(0, 3)]))
        for c in shy:
            c.wait_recv()
    with jax.named_scope("wait_far_columns"):
        for c in fwd:
            c.wait_recv()
    shx = [
        go(shb.at[:, x, h], shb.at[:, x, h], shx_r.at[d], pdev[(0, d)])
        for d in (1, 3, 2)
    ]
    with jax.named_scope("relay_gate"):
        ex2 = [second_hop(i, ex1[i]) for i in range(2)]
    with jax.named_scope("columns"):
        col, row = iota((384, 384), 0), iota((384, 384), 1)
        source = (
            lax.div(lax.rem(col, 48), 12) * 96 + lax.div(col, 48) * 12 + lax.rem(col, 12)
        )
        order = jnp.where(row == source, 1.0, 0.0).astype(BF16)
        wc[...] = jnp.dot(
            order, ocol[...].reshape(384, 768), preferred_element_type=F32
        ).astype(BF16)

    with jax.named_scope("wait_heads"):
        for c in hy:
            c.wait_recv()
    with jax.named_scope("project"):
        po = lax.dot_general(hbuf[...].reshape(256, 768), wc[...], NT, preferred_element_type=F32)
        part[...] = po.reshape(4, 2, 32, 384).astype(BF16)
    rs = []
    for d in (1, 3, 2):
        yd = up(y, d, NY)
        for i, hd in enumerate((h, 1 - h)):
            rs.append(
                go(part.at[yd, hd], rbuf.at[y, h], rs_r.at[i, d], (seq_of(yd, z, x), hd))
            )
    rs.append(go(part.at[y, 1 - h], rbuf.at[y, h], rs_r.at[1, 0], sib))
    rbuf[y, h] = part[y, h]
    with jax.named_scope("relay_gate_rest"):
        ex2 += [second_hop(i, ex1[i]) for i in range(2, 4)]
        ex1 += [first_hop(i) for i in range(4, 6)]
    with jax.named_scope("gate_up_rest"):
        wgb[0, 768:1536, 0:256] = raw[0, 768:1536, 0, :]
        wgb[0, 768:1536, 256:512] = raw[0, 768:1536, 1, :]
    with jax.named_scope("wait_projected"):
        for c in rs:
            c.wait_recv()
    with jax.named_scope("norm"):
        own_res.wait()
        attn = [rbuf[j, 0].astype(F32) + rbuf[j, 1].astype(F32) for j in range(NY)]
        mixed = resbuf[...].astype(F32) + jnp.concatenate(attn, axis=1)
        ms = jnp.mean(mixed * mixed, axis=-1, keepdims=True)
        xb[0] = (mixed * lax.rsqrt(ms + EPSILON) * gain_ref[...].reshape(1, 1536)).astype(BF16)
    xz = {
        d: go(xb.at[0], xb.at[SLOT[NZ - d]], xz_r.at[d], zdev[d]) for d in (2, 6, 1, 7)
    }
    ex2g = ex2
    with jax.named_scope("cache_plane"):
        own_cache.wait()
        for c in cz:
            c.wait_recv()
        cp = [
            go(
                cmid_ref.at[:, up(y, at[0], NY), up(x, at[1], NX)], chand_ref.at[y, :, x],
                cp_r.at[i], pdev[at],
            )
            for i, at in enumerate(plane)
        ]
        cp_own = here(cmid_ref.at[:, y, x], chand_ref.at[y, :, x])
    with jax.named_scope("gate_sibling"):
        for c in ex2g:
            c.wait_recv()
        sib_g = go(raw.at[1, rows_g], raw.at[1, rows_g], sib_r.at[1], sib)
    with jax.named_scope("choose"):
        for c in rp:
            c.wait_recv()
        lane = iota((128, COLS), 1)
        half = lax.div(lane, COLS // 2)
        expert = lax.rem(y + half, 2) * 32 + z * NX + lax.rem(lax.div(lane, ROWS), NX)
        row = iota((128, COLS), 0)
        of_rank = jnp.where(row == expert, 1.0, 0.0).astype(BF16)
        of_prob = jnp.where(row == expert + EXPERTS, 1.0, 0.0).astype(BF16)
        slot = lax.rem(iota((128, COLS), 1), ROWS)
        member = lax.div(row, 32) == lax.div(slot, CAP)
        number = lax.rem(slot, CAP).astype(F32)
        picks, weights = [], []
        for c in range(2):
            rpc = rpb[4 * c : 4 * c + 4].reshape(128, 128).astype(BF16)
            rank = jnp.dot(rpc, of_rank, preferred_element_type=F32)
            prob = jnp.dot(rpc, of_prob, preferred_element_type=F32)
            hit = member & (rank == number)
            picks.append(jnp.transpose(jnp.where(hit, 1.0, 0.0)).astype(BF16))
            weights.append(jnp.where(hit, prob, 0.0).astype(BF16))

    with jax.named_scope("wait_near_rows"):
        xz[2].wait_recv()
        low = pl.ds(0, 16)
        xz[4] = go(
            xb.at[SLOT[6], low], xb.at[SLOT[4], low], xz_r.at[4], zdev[2]
        )
        xz[3] = go(xb.at[SLOT[6]], xb.at[SLOT[5]], xz_r.at[3], zdev[1])
        xz[6].wait_recv()
        high = pl.ds(16, 16)
        xz[0] = go(
            xb.at[SLOT[2], high], xb.at[SLOT[4], high], xz_r.at[0], zdev[6]
        )
        xz[5] = go(xb.at[SLOT[2]], xb.at[SLOT[3]], xz_r.at[5], zdev[7])
        xz[1].wait_recv()
        xz[7].wait_recv()

    turn = 1 + 2 * lax.rem(x, 2)

    def to_expert(p, d):
        return pdev[(0, d)] if p == 0 else (seq_of(up(y, turn, NY), z, up(x, d, NX)), h)

    def to_source(p, d):
        xs = up(x, NX - d, NX)
        if p == 0:
            return pdev[(0, NX - d)]
        return (seq_of(up(y, 3 - 2 * lax.rem(xs, 2), NY), z, xs), h)

    hops = [(p, d) for p in range(2) for d in (2, 1, 3, 0) if (p, d) != (0, 0)]
    before = pdev[(0, 3)]

    def dispatch(c):
        xc = xb[4 * c : 4 * c + 4].reshape(128, 1536)
        rows = jnp.dot(picks[c], xc, preferred_element_type=F32)
        for j in range(8):
            dsend[c, j] = rows[j * ROWS : (j + 1) * ROWS].astype(BF16)
        copies = [go(dsend.at[c, up(x, 2, NX)], relay_x.at[c], q_r.at[c], before)]
        for i, (p, d) in enumerate(hops[1:], 1):
            copies.append(
                go(
                    dsend.at[c, p * NX + up(x, d, NX)], drecv.at[c, p * NX + x],
                    d_r.at[c, i], to_expert(p, d),
                )
            )
        drecv[c, x] = dsend[c, x]
        return copies

    def pass_on(c, copies):
        copies[0].wait_recv()
        copies[0] = go(
            relay_x.at[c], drecv.at[c, up(x, 1, NX)], d_r.at[c, 0], before
        )

    sent = {}
    with jax.named_scope("dispatch"):
        sent[1] = dispatch(1)
    with jax.named_scope("relay_down"):
        ex2 = [second_hop(i, ex1[i]) for i in range(4, 6)]
    with jax.named_scope("gate_up_other"):
        sib_g.wait_recv()
        wgb[1, :, 0:256] = raw[1, :, 0, :]
        wgb[1, :, 256:512] = raw[1, :, 1, :]
    with jax.named_scope("pass_on"):
        pass_on(1, sent[1])
    with jax.named_scope("wait_rows"):
        for d in (3, 5, 4, 0):
            xz[d].wait_recv()
    with jax.named_scope("dispatch"):
        sent[0] = dispatch(0)
    with jax.named_scope("shared_weights"):
        for m in shx:
            m.wait_recv()
        sib_sh = go(shb.at[:, :, h], shb.at[:, :, h], sib_r.at[0], sib)
    with jax.named_scope("shared"):
        sib_sh.wait_recv()
        xs = xb[...].reshape(256, 1536)
        sh = shb[...].reshape(512, 1536)
        both = lax.dot_general(xs, sh, NT, preferred_element_type=F32)
        act = silu(pltpu.roll(both, 8, 1)) * pltpu.roll(both, 4, 1)
        live = lax.rem(lax.div(iota((256, 512), 1), 4), 4) == 2
        act = jnp.where(live, act, 0.0).astype(BF16)
        shared = jnp.dot(act, sh, preferred_element_type=F32)
    with jax.named_scope("pass_on"):
        pass_on(0, sent[0])
    with jax.named_scope("down_sibling"):
        for c in ex2:
            c.wait_recv()
        sib_d = go(wdb.at[1, rows_d], wdb.at[1, rows_d], sib_r.at[2], sib)
    with jax.named_scope("wait_exchange"):
        own_wd.wait()
        sib_d.wait_recv()

    def experts(c):
        for m in sent[c]:
            m.wait_recv()
        rows = jnp.concatenate([drecv[c, j].astype(F32) for j in range(8)], axis=0).astype(BF16)
        acc = None
        for j in range(2):
            gu = jnp.dot(rows, wgb[j], preferred_element_type=F32)
            a = (silu(gu[:, :256]) * gu[:, 256:]).astype(BF16)
            o = jnp.dot(a, wdb[j], preferred_element_type=F32)
            acc = o if acc is None else acc + o
        for j in range(8):
            rsend[c, j] = acc[j * ROWS : (j + 1) * ROWS].astype(BF16)
        rrecv[c, x] = rsend[c, x]

    def give_back(c):
        copies = [go(rsend.at[c, up(x, 2, NX)], relay_b.at[c], q_r.at[2 + c], before)]
        for i, (p, d) in enumerate(hops[1:], 1):
            copies.append(
                go(
                    rsend.at[c, p * NX + up(x, NX - d, NX)], rrecv.at[c, p * NX + x],
                    r_r.at[c, i], to_source(p, d),
                )
            )
        return copies

    def pass_back(c, copies):
        copies[0].wait_recv()
        copies[0] = go(relay_b.at[c], rrecv.at[c, up(x, 1, NX)], r_r.at[c, 0], before)

    back = {}
    with jax.named_scope("experts_near"):
        experts(1)
    with jax.named_scope("experts_far"):
        experts(0)
        back[0] = give_back(0)
    with jax.named_scope("pass_back_far"):
        pass_back(0, back[0])
        back[1] = give_back(1)

    def combined(c):
        for m in back[c]:
            m.wait_recv()
        rows = jnp.concatenate([rrecv[c, j].astype(F32) for j in range(8)], axis=0).astype(BF16)
        return shared[128 * c : 128 * c + 128] + jnp.dot(
            weights[c], rows, preferred_element_type=F32
        )

    with jax.named_scope("combine_far"):
        pz[0:4] = combined(0).astype(BF16).reshape(4, 32, 1536)
        far = [
            go(pz.at[SLOT[3]], relay_3.at[0], z_r.at[0], zdev[1]),
            go(pz.at[SLOT[5]], relay_3.at[1], z_r.at[1], zdev[7]),
            go(pz.at[SLOT[4], low], relay_4.at[0], z_r.at[2], zdev[2]),
            go(pz.at[SLOT[4], high], relay_4.at[1], z_r.at[3], zdev[6]),
        ]
    with jax.named_scope("pass_back_near"):
        pass_back(1, back[1])
    with jax.named_scope("combine_near"):
        tot = combined(1)
        pz[4:6] = tot[0:64].astype(BF16).reshape(2, 32, 1536)

        def to_line(o):
            return go(
                pz.at[SLOT[o]], racc.at[SLOT[NZ - o] - 3], z_r.at[SLOT[o]], zdev[o]
            )
    with jax.named_scope("wait_far"):
        for m in far:
            m.wait_recv()
    with jax.named_scope("add_far"):
        none = jnp.zeros((16, 1536), F32)
        plus = (
            tot[64:96] + relay_3[0].astype(F32)
            + jnp.concatenate([relay_4[0].astype(F32), none], axis=0)
        )
        minus = (
            tot[96:128] + relay_3[1].astype(F32)
            + jnp.concatenate([none, relay_4[1].astype(F32)], axis=0)
        )
        pz[SLOT[2]] = plus.astype(BF16)
        pz[SLOT[6]] = minus.astype(BF16)
        red = [to_line(2), to_line(6), to_line(1), to_line(7)]
    racc[0] = pz[0]
    with jax.named_scope("wait_sum"):
        for c in red:
            c.wait_recv()
    out = mixed
    for j in range(5):
        out = out + racc[j].astype(F32)
    out_ref[...] = out.astype(BF16)
    with jax.named_scope("drain"):
        cp_own.wait()
        for c in cp:
            c.wait_recv()
        for c in pending[-POOL:]:
            c.wait_send()


def shards(
    queries, key_vectors, value_vectors, lengths, out_weight, residual, norm_gain, route_ids,
    route_logits, shared_gate_up, shared_down, expert_gate_up, expert_down, cache_blocks, block_table,
):
    hbm, vmem = pl.BlockSpec(memory_space=pltpu.HBM), pl.BlockSpec(memory_space=pltpu.VMEM)
    dma = pltpu.SemaphoreType.DMA
    sgu = jnp.transpose(shared_gate_up, (1, 2, 0))
    wg = expert_gate_up.reshape(1536, 2, 256)
    wd = expert_down.reshape(256, 1536)
    cache = cache_blocks.reshape(NY, NZ, NX, 8, 2, HD)
    sds = jax.ShapeDtypeStruct
    layer_out, _, chand = pl.pallas_call(
        layer_kernel,
        out_shape=(
            sds((32, 1536), BF16),
            sds((NZ, NY, NX, 8, 2, HD), BF16),
            sds((NY, NZ, NX, 8, 2, HD), BF16),
        ),
        in_specs=[hbm, hbm, hbm, vmem, vmem, hbm, vmem, vmem, vmem, vmem, vmem, hbm, hbm, hbm],
        out_specs=(vmem, hbm, hbm),
        scratch_shapes=[
            pltpu.VMEM((64, 768), BF16),
            pltpu.VMEM((320, 256), BF16),
            pltpu.VMEM((320, 256), BF16),
            pltpu.VMEM((32, 1536), BF16),
            pltpu.VMEM((16, 768), BF16),
            pltpu.VMEM((NZ, 16, 768), BF16),
            pltpu.VMEM((NX, 96, 768), BF16),
            pltpu.VMEM((384, 768), BF16),
            pltpu.VMEM((NY, 64, 768), BF16),
            pltpu.VMEM((NY, 2, 32, 384), BF16),
            pltpu.VMEM((NY, 2, 32, 384), BF16),
            pltpu.VMEM((NZ, 32, 1536), BF16),
            pltpu.VMEM((NZ, 32, 128), F32),
            pltpu.VMEM((16, 1536), BF16),
            pltpu.VMEM((NY, NX, 2, 16, 1536), BF16),
            pltpu.VMEM((2, 1536, 2, 256), BF16),
            pltpu.VMEM((2, 1536, 512), BF16),
            pltpu.VMEM((2, 256, 1536), BF16),
            pltpu.VMEM((4, 192, 2, 256), BF16),
            pltpu.VMEM((2, 64, 1536), BF16),
            pltpu.VMEM((2, ROWS, 1536), BF16),
            pltpu.VMEM((2, ROWS, 1536), BF16),
            pltpu.VMEM((2, 32, 1536), BF16),
            pltpu.VMEM((2, 16, 1536), BF16),
            pltpu.VMEM((2, 8, ROWS, 1536), BF16),
            pltpu.VMEM((2, 8, ROWS, 1536), BF16),
            pltpu.VMEM((2, 8, ROWS, 1536), BF16),
            pltpu.VMEM((2, 8, ROWS, 1536), BF16),
            pltpu.VMEM((NZ, 32, 1536), BF16),
            pltpu.VMEM((5, 32, 1536), BF16),
            dma((POOL,)),
            dma((2, 4)),
            dma((8,)),
            dma((4,)),
            dma((8,)),
            dma((4,)),
            dma((4,)),
            dma((8,)),
            dma((15,)),
            dma((6,)),
            dma((6,)),
            dma((3,)),
            dma((4,)),
            dma((2, 4)),
            dma((8,)),
            dma((2, 7)),
            dma((4,)),
            dma((2, 7)),
            dma((9,)),
            dma((8,)),
        ],
        compiler_params=pltpu.CompilerParams(
            collective_id=0, has_side_effects=True, vmem_limit_bytes=56 << 20
        ),
        name="layer",
    )(
        queries, key_vectors, value_vectors, lengths, out_weight.T, residual, norm_gain,
        route_ids.T, route_logits.T, sgu, shared_down, wg, wd, cache,
    )
    cache_out = jnp.take(
        chand.reshape(128, 1, 8, 2, HD), block_table, axis=0, mode="clip"
    )
    return layer_out, cache_out


def solution(mesh):
    in_specs = (
        P("seq", "head"),
        P("seq", "head"),
        P("seq", "head"),
        P(),
        P("head", "seq"),
        P(("seq", "head"), None),
        P(),
        P(("seq", "head"), None),
        P(("seq", "head"), None),
        P(None, None, ("seq", "head")),
        P(("seq", "head"), None),
        P("seq", None, None, None),
        P("seq", None, None),
        P("seq", None, None, "head", None),
        P(),
    )
    out_specs = (P(("seq", "head"), None), P(None, "seq", None, "head", None))
    return jax.shard_map(shards, mesh=mesh, in_specs=in_specs, out_specs=out_specs, check_vma=False)
```

```python
import functools
import math

import jax
import jax.numpy as jnp
from jax import lax
from jax.experimental import pallas as pl
from jax.experimental.pallas import tpu as pltpu
from jax.sharding import PartitionSpec as P

MESH = pl.DeviceIdType.MESH
HD = 128
NY, NZ, NX = 4, 8, 4
TOP = 6
CAP = 6
EXPERTS = 64
NEGATIVE = -1e30
EPSILON = 1e-05
F32 = jnp.float32
BF16 = jnp.bfloat16
ZORDER = (1, 7, 2, 6, 3, 5, 4)
OFF = (0, 3, 5, 4, 1, 7, 2, 6)
SLOT = {o: k for k, o in enumerate(OFF)}
ROWS = 24
POOL = 48
COLS = 8 * ROWS
NT = (((1,), (1,)), ((), ()))


def place():
    s = lax.axis_index("seq")
    h = lax.axis_index("head")
    y = lax.div(s, NZ * NX)
    z = lax.rem(lax.div(s, NX), NZ)
    x = lax.rem(s, NX)
    return s, h, y, z, x


def seq_of(y, z, x):
    return y * (NZ * NX) + z * NX + x


def up(i, by, n):
    return lax.rem(i + by, n)


def rcopy(src, dst, ssem, rsem, dev):
    return pltpu.make_async_remote_copy(
        src_ref=src, dst_ref=dst, send_sem=ssem, recv_sem=rsem, device_id=dev, device_id_type=MESH
    )


def iota(shape, axis):
    return lax.broadcasted_iota(jnp.int32, shape, axis)


def silu(v):
    return v / (1.0 + jnp.exp(-v))


def routing_table(ids, logits):
    top = jnp.max(logits, axis=0, keepdims=True)
    e = jnp.exp(logits - top)
    probs = e / jnp.sum(e, axis=0, keepdims=True)
    row = iota((128, 32), 0)
    named = jnp.zeros((128, 32), F32)
    weight = jnp.zeros((128, 32), F32)
    for r in range(TOP):
        idr = jnp.broadcast_to(ids[r : r + 1, :], (128, 32))
        named = named + jnp.where(row == idr, 1.0, 0.0)
        weight = weight + jnp.where(row - EXPERTS == idr, probs[r : r + 1, :], 0.0)
    before = jnp.where(iota((32, 32), 0) < iota((32, 32), 1), 1.0, 0.0)
    rank = jnp.dot(named.astype(BF16), before.astype(BF16), preferred_element_type=F32)
    table = jnp.where(row < EXPERTS, jnp.where(named > 0.5, rank, -1.0), weight)
    return jnp.transpose(table)


def layer_kernel(
    q_hbm, k_hbm, v_hbm, len_ref, ow_ref, res_hbm, gain_ref, ids_ref, log_ref,
    sgu_ref, sd_ref, wg_hbm, wd_hbm, cache_hbm, table_ref,
    out_ref, cmid_ref, cache_ref,
    qbuf, kwin, vwin, resbuf, owpad, owbuf, ocol, wc, hbuf, part, rbuf, xb, rpb, shpad, shb, raw, wgb, wdb,
    chand_ref, taken, relay_g, relay_d, relay_x, relay_b, relay_3, relay_4, dsend, drecv, rsend, rrecv, pz, racc,
    pool, kv_r, owz_r, owx_r, rp_r, shy_r, shx_r, cz_r, cp_r, e1_r, e2_r, sib_r, hy_r,
    rs_r, xz_r, d_r, q_r, r_r, z_r, loc,
):
    s, h, y, z, x = place()
    seqs = NY * NZ * NX
    zdev = {d: (seq_of(y, up(z, d, NZ), x), h) for d in range(1, NZ)}
    plane = [
        (dy, dx) for dy in range(NY) for dx in range(NX) if (dy, dx) != (0, 0)
    ]
    pdev = {at: (seq_of(up(y, at[0], NY), z, up(x, at[1], NX)), h) for at in plane}
    sib = (s, 1 - h)
    cross = [(seq_of(up(y, dy, NY), z, x), 1 - h) for dy in (1, 2, 3)]
    ahead = [(lax.rem(s + by, seqs), h) for by in range(1, 5)]
    behind = [(lax.rem(s + seqs - by, seqs), h) for by in range(1, 5)]

    local = []

    def here(src, dst):
        copy = pltpu.make_async_copy(src, dst, loc.at[len(local)])
        copy.start()
        local.append(copy)
        return copy

    own_wg = here(wg_hbm, raw.at[0])
    own_k = here(k_hbm, kwin.at[pl.ds(256, 64)])
    own_v = here(v_hbm, vwin.at[pl.ds(256, 64)])
    own_q = here(q_hbm, qbuf)
    own_cache = here(cache_hbm.at[:, z], cmid_ref.at[z])
    own_res = here(res_hbm, resbuf)
    own_wd = here(wd_hbm, wdb.at[0])
    peers = list(zdev.values()) + list(pdev.values()) + [sib] + cross + ahead + behind
    barrier = pltpu.get_barrier_semaphore()
    for dev in peers:
        pl.semaphore_signal(barrier, inc=1, device_id=dev, device_id_type=MESH)

    with jax.named_scope("pack"):
        owpad[...] = jnp.concatenate(
            [ow_ref[...].astype(F32), jnp.zeros((4, 768), F32)], axis=0
        ).astype(BF16)
        owbuf[z] = owpad[...]
        shpad[...] = jnp.concatenate(
            [
                sgu_ref[...].astype(F32).reshape(8, 1536),
                sd_ref[...].astype(F32),
                jnp.zeros((4, 1536), F32),
            ],
            axis=0,
        ).astype(BF16)
        shb[y, x, h] = shpad[...]
    with jax.named_scope("routing"):
        rpb[0] = routing_table(ids_ref[...], log_ref[...])
    with jax.named_scope("enter"):
        pl.semaphore_wait(barrier, len(peers))

    pending = []

    def go(src, dst, recv, dev):
        turn = len(pending)
        if turn >= POOL:
            pending[turn - POOL].wait_send()
        copy = rcopy(src, dst, pool.at[turn % POOL], recv, dev)
        copy.start()
        pending.append(copy)
        return copy

    owz = [go(owpad, owbuf.at[z], owz_r.at[d], zdev[d]) for d in ZORDER]
    kv = []
    for by in range(1, 5):
        rows = pl.ds(64 * (4 - by), 64)
        kv.append(go(k_hbm, kwin.at[rows], kv_r.at[0, by - 1], ahead[by - 1]))
        kv.append(go(v_hbm, vwin.at[rows], kv_r.at[1, by - 1], ahead[by - 1]))
    shy = [
        go(shpad, shb.at[y, x, h], shy_r.at[d], pdev[(d, 0)]) for d in (1, 3, 2)
    ]
    sides = (pdev[(1, 0)], pdev[(3, 0)])
    rows_g, rows_d = pl.ds(h * 768, 768), pl.ds(h * 128, 128)

    def piece(i):
        if i < 4:
            return pl.ds(h * 768 + i * 192, 192)
        return pl.ds(h * 128 + (i - 4) * 64, 64)

    def first_hop(i):
        sem = e1_r.at[i], sides[i % 2]
        if i < 4:
            return go(wg_hbm.at[piece(i)], relay_g.at[i], *sem)
        return go(wd_hbm.at[piece(i)], relay_d.at[i - 4], *sem)

    def second_hop(i, arrived):
        arrived.wait_recv()
        sem = e2_r.at[i], sides[i % 2]
        if i < 4:
            return go(relay_g.at[i], raw.at[1, piece(i)], *sem)
        return go(relay_d.at[i - 4], wdb.at[1, piece(i)], *sem)

    ex1 = [first_hop(i) for i in range(4)]

    with jax.named_scope("visible"):
        upper = jnp.where(iota((64, 64), 0) <= iota((64, 64), 1), 1.0, 0.0).astype(BF16)
        lens = jnp.broadcast_to(len_ref[...].astype(F32).reshape(1, 64), (16, 64)).astype(BF16)
        ends = jnp.dot(lens, upper, preferred_element_type=F32)[0:1, :]
        qpos = (s * 64 + iota((64, 64), 0)).astype(F32)
        first = jnp.max(jnp.where(ends <= qpos, ends, 0.0), axis=-1, keepdims=True)
        kpos = (s * 64 - 256 + iota((64, 320), 1)).astype(F32)
        qcol = (s * 64 + iota((64, 320), 0)).astype(F32)
        seen = jnp.where((kpos >= first) & (kpos <= qcol), 0.0, NEGATIVE)
        seen3 = jnp.concatenate([seen, seen, seen], axis=0)

    col, row = iota((96, 128), 0), iota((96, 128), 1)
    pack = jnp.where(row == lax.div(col, 12) * 16 + lax.rem(col, 12), 1.0, 0.0).astype(BF16)
    with jax.named_scope("wait_first_columns"):
        for c in owz:
            c.wait_recv()
    ocol[x] = jnp.dot(
        pack, owbuf[...].reshape(128, 768), preferred_element_type=F32
    ).astype(BF16)
    owx = {
        d: go(ocol.at[x], ocol.at[x], owx_r.at[d], pdev[(0, d)])
        for d in (1, 3)
    }
    with jax.named_scope("wait_keys"):
        own_k.wait()
        own_v.wait()
        own_q.wait()
        for c in kv:
            c.wait_recv()
    with jax.named_scope("attention"):
        for g in range(2):
            cols = slice(g * HD, (g + 1) * HD)
            qs = jnp.concatenate(
                [qbuf[:, (3 * g + i) * HD : (3 * g + i + 1) * HD] for i in range(3)], axis=0
            )
            sc = lax.dot_general(qs, kwin[:, cols], NT, preferred_element_type=F32)
            sc = jnp.where(seen3 < -1.0, NEGATIVE, sc * (1.0 / math.sqrt(HD)))
            w = jnp.exp(sc - jnp.max(sc, axis=-1, keepdims=True))
            total = jnp.sum(w, axis=-1, keepdims=True)
            o = jnp.dot(w.astype(BF16), vwin[:, cols], preferred_element_type=F32)
            o = (o / total).astype(BF16)
            for i in range(3):
                hbuf[y, :, (3 * g + i) * HD : (3 * g + i + 1) * HD] = o[i * 64 : (i + 1) * 64]
    hy = [
        go(hbuf.at[y], hbuf.at[y], hy_r.at[d], pdev[(d, 0)]) for d in (1, 3, 2)
    ]

    rp = [
        go(rpb.at[0], rpb.at[SLOT[NZ - d]], rp_r.at[d], zdev[d]) for d in ZORDER
    ]
    cz = [
        go(cache_hbm.at[:, up(z, d, NZ)], cmid_ref.at[z], cz_r.at[d], zdev[d])
        for d in ZORDER
    ]
    with jax.named_scope("gate_up"):
        own_wg.wait()
        wgb[0, 0:768, 0:256] = raw[0, 0:768, 0, :]
        wgb[0, 0:768, 256:512] = raw[0, 0:768, 1, :]
    with jax.named_scope("wait_columns"):
        left, right = up(x, 3, NX), up(x, 1, NX)
        owx[1].wait_recv()
        lower = ocol.at[left, 0:48]
        fwd = [go(lower, lower, owx_r.at[0], pdev[(0, 1)])]
        owx[3].wait_recv()
        higher = ocol.at[right, 48:96]
        fwd.append(go(higher, higher, owx_r.at[2], pdev[(0, 3)]))
        for c in shy:
            c.wait_recv()
    with jax.named_scope("wait_far_columns"):
        for c in fwd:
            c.wait_recv()
    shx = [
        go(shb.at[:, x, h], shb.at[:, x, h], shx_r.at[d], pdev[(0, d)])
        for d in (1, 3, 2)
    ]
    with jax.named_scope("relay_gate"):
        ex2 = [second_hop(i, ex1[i]) for i in range(2)]
    with jax.named_scope("columns"):
        col, row = iota((384, 384), 0), iota((384, 384), 1)
        source = (
            lax.div(lax.rem(col, 48), 12) * 96 + lax.div(col, 48) * 12 + lax.rem(col, 12)
        )
        order = jnp.where(row == source, 1.0, 0.0).astype(BF16)
        wc[...] = jnp.dot(
            order, ocol[...].reshape(384, 768), preferred_element_type=F32
        ).astype(BF16)

    with jax.named_scope("wait_heads"):
        for c in hy:
            c.wait_recv()
    with jax.named_scope("project"):
        po = lax.dot_general(hbuf[...].reshape(256, 768), wc[...], NT, preferred_element_type=F32)
        part[...] = po.reshape(4, 2, 32, 384).astype(BF16)
    rs = []
    for d in (1, 3, 2):
        yd = up(y, d, NY)
        for i, hd in enumerate((h, 1 - h)):
            rs.append(
                go(part.at[yd, hd], rbuf.at[y, h], rs_r.at[i, d], (seq_of(yd, z, x), hd))
            )
    rs.append(go(part.at[y, 1 - h], rbuf.at[y, h], rs_r.at[1, 0], sib))
    rbuf[y, h] = part[y, h]
    with jax.named_scope("relay_gate_rest"):
        ex2 += [second_hop(i, ex1[i]) for i in range(2, 4)]
        ex1 += [first_hop(i) for i in range(4, 6)]
    with jax.named_scope("gate_up_rest"):
        wgb[0, 768:1536, 0:256] = raw[0, 768:1536, 0, :]
        wgb[0, 768:1536, 256:512] = raw[0, 768:1536, 1, :]
    with jax.named_scope("wait_projected"):
        for c in rs:
            c.wait_recv()
    with jax.named_scope("norm"):
        own_res.wait()
        attn = [rbuf[j, 0].astype(F32) + rbuf[j, 1].astype(F32) for j in range(NY)]
        mixed = resbuf[...].astype(F32) + jnp.concatenate(attn, axis=1)
        ms = jnp.mean(mixed * mixed, axis=-1, keepdims=True)
        xb[0] = (mixed * lax.rsqrt(ms + EPSILON) * gain_ref[...].reshape(1, 1536)).astype(BF16)
    xz = {
        d: go(xb.at[0], xb.at[SLOT[NZ - d]], xz_r.at[d], zdev[d]) for d in (2, 6, 1, 7)
    }
    ex2g = ex2
    with jax.named_scope("cache_plane"):
        own_cache.wait()
        for c in cz:
            c.wait_recv()
        cp = [
            go(
                cmid_ref.at[:, up(y, at[0], NY), up(x, at[1], NX)], chand_ref.at[y, :, x],
                cp_r.at[i], pdev[at],
            )
            for i, at in enumerate(plane)
        ]
        cp_own = here(cmid_ref.at[:, y, x], chand_ref.at[y, :, x])
    with jax.named_scope("gate_sibling"):
        for c in ex2g:
            c.wait_recv()
        sib_g = go(raw.at[1, rows_g], raw.at[1, rows_g], sib_r.at[1], sib)
    with jax.named_scope("choose"):
        for c in rp:
            c.wait_recv()
        lane = iota((128, COLS), 1)
        half = lax.div(lane, COLS // 2)
        expert = lax.rem(y + half, 2) * 32 + z * NX + lax.rem(lax.div(lane, ROWS), NX)
        row = iota((128, COLS), 0)
        of_rank = jnp.where(row == expert, 1.0, 0.0).astype(BF16)
        of_prob = jnp.where(row == expert + EXPERTS, 1.0, 0.0).astype(BF16)
        slot = lax.rem(iota((128, COLS), 1), ROWS)
        member = lax.div(row, 32) == lax.div(slot, CAP)
        number = lax.rem(slot, CAP).astype(F32)
        picks, weights = [], []
        for c in range(2):
            rpc = rpb[4 * c : 4 * c + 4].reshape(128, 128).astype(BF16)
            rank = jnp.dot(rpc, of_rank, preferred_element_type=F32)
            prob = jnp.dot(rpc, of_prob, preferred_element_type=F32)
            hit = member & (rank == number)
            picks.append(jnp.transpose(jnp.where(hit, 1.0, 0.0)).astype(BF16))
            weights.append(jnp.where(hit, prob, 0.0).astype(BF16))

    with jax.named_scope("wait_near_rows"):
        xz[2].wait_recv()
        low = pl.ds(0, 16)
        xz[4] = go(
            xb.at[SLOT[6], low], xb.at[SLOT[4], low], xz_r.at[4], zdev[2]
        )
        xz[3] = go(xb.at[SLOT[6]], xb.at[SLOT[5]], xz_r.at[3], zdev[1])
        xz[6].wait_recv()
        high = pl.ds(16, 16)
        xz[0] = go(
            xb.at[SLOT[2], high], xb.at[SLOT[4], high], xz_r.at[0], zdev[6]
        )
        xz[5] = go(xb.at[SLOT[2]], xb.at[SLOT[3]], xz_r.at[5], zdev[7])
        xz[1].wait_recv()
        xz[7].wait_recv()

    turn = 1 + 2 * lax.rem(x, 2)

    def to_expert(p, d):
        return pdev[(0, d)] if p == 0 else (seq_of(up(y, turn, NY), z, up(x, d, NX)), h)

    def to_source(p, d):
        xs = up(x, NX - d, NX)
        if p == 0:
            return pdev[(0, NX - d)]
        return (seq_of(up(y, 3 - 2 * lax.rem(xs, 2), NY), z, xs), h)

    hops = [(p, d) for p in range(2) for d in (2, 1, 3, 0) if (p, d) != (0, 0)]
    before = pdev[(0, 3)]

    def dispatch(c):
        xc = xb[4 * c : 4 * c + 4].reshape(128, 1536)
        rows = jnp.dot(picks[c], xc, preferred_element_type=F32)
        for j in range(8):
            dsend[c, j] = rows[j * ROWS : (j + 1) * ROWS].astype(BF16)
        copies = [go(dsend.at[c, up(x, 2, NX)], relay_x.at[c], q_r.at[c], before)]
        for i, (p, d) in enumerate(hops[1:], 1):
            copies.append(
                go(
                    dsend.at[c, p * NX + up(x, d, NX)], drecv.at[c, p * NX + x],
                    d_r.at[c, i], to_expert(p, d),
                )
            )
        drecv[c, x] = dsend[c, x]
        return copies

    def pass_on(c, copies):
        copies[0].wait_recv()
        copies[0] = go(
            relay_x.at[c], drecv.at[c, up(x, 1, NX)], d_r.at[c, 0], before
        )

    sent = {}
    with jax.named_scope("dispatch"):
        sent[1] = dispatch(1)
    with jax.named_scope("gate_up_other"):
        sib_g.wait_recv()
        wgb[1, :, 0:256] = raw[1, :, 0, :]
        wgb[1, :, 256:512] = raw[1, :, 1, :]
    with jax.named_scope("relay_down"):
        ex2 = [second_hop(i, ex1[i]) for i in range(4, 6)]
    with jax.named_scope("pass_on"):
        pass_on(1, sent[1])
    with jax.named_scope("wait_rows"):
        for d in (3, 5, 4, 0):
            xz[d].wait_recv()
    with jax.named_scope("dispatch"):
        sent[0] = dispatch(0)
    with jax.named_scope("shared_weights"):
        for m in shx:
            m.wait_recv()
        sib_sh = go(shb.at[:, :, h], shb.at[:, :, h], sib_r.at[0], sib)
    with jax.named_scope("shared"):
        sib_sh.wait_recv()
        xs = xb[...].reshape(256, 1536)
        sh = shb[...].reshape(512, 1536)
        both = lax.dot_general(xs, sh, NT, preferred_element_type=F32)
        act = silu(pltpu.roll(both, 8, 1)) * pltpu.roll(both, 4, 1)
        live = lax.rem(lax.div(iota((256, 512), 1), 4), 4) == 2
        act = jnp.where(live, act, 0.0).astype(BF16)
        shared = jnp.dot(act, sh, preferred_element_type=F32)
    with jax.named_scope("pass_on"):
        pass_on(0, sent[0])
    with jax.named_scope("down_sibling"):
        for c in ex2:
            c.wait_recv()
        sib_d = go(wdb.at[1, rows_d], wdb.at[1, rows_d], sib_r.at[2], sib)
    with jax.named_scope("wait_exchange"):
        own_wd.wait()
        sib_d.wait_recv()

    def experts(c):
        for m in sent[c]:
            m.wait_recv()
        rows = jnp.concatenate([drecv[c, j].astype(F32) for j in range(8)], axis=0).astype(BF16)
        acc = None
        for j in range(2):
            gu = jnp.dot(rows, wgb[j], preferred_element_type=F32)
            a = (silu(gu[:, :256]) * gu[:, 256:]).astype(BF16)
            o = jnp.dot(a, wdb[j], preferred_element_type=F32)
            acc = o if acc is None else acc + o
        for j in range(8):
            rsend[c, j] = acc[j * ROWS : (j + 1) * ROWS].astype(BF16)
        rrecv[c, x] = rsend[c, x]

    def give_back(c):
        copies = [go(rsend.at[c, up(x, 2, NX)], relay_b.at[c], q_r.at[2 + c], before)]
        for i, (p, d) in enumerate(hops[1:], 1):
            copies.append(
                go(
                    rsend.at[c, p * NX + up(x, NX - d, NX)], rrecv.at[c, p * NX + x],
                    r_r.at[c, i], to_source(p, d),
                )
            )
        return copies

    def pass_back(c, copies):
        copies[0].wait_recv()
        copies[0] = go(relay_b.at[c], rrecv.at[c, up(x, 1, NX)], r_r.at[c, 0], before)

    back = {}
    with jax.named_scope("experts_near"):
        experts(1)
    with jax.named_scope("experts_far"):
        experts(0)
        back[0] = give_back(0)
    with jax.named_scope("pass_back_far"):
        pass_back(0, back[0])
        back[1] = give_back(1)

    with jax.named_scope("cache_order"):
        cp_own.wait()
        for c in cp:
            c.wait_recv()

        def take(b, carry):
            i = table_ref[b]
            taken[b] = chand_ref[lax.div(i, 32), lax.rem(lax.div(i, 4), 8), lax.rem(i, 4)]
            return carry

        lax.fori_loop(0, 128, take, 0)
        taken_out = here(taken, cache_ref)

    def combined(c):
        for m in back[c]:
            m.wait_recv()
        rows = jnp.concatenate([rrecv[c, j].astype(F32) for j in range(8)], axis=0).astype(BF16)
        return shared[128 * c : 128 * c + 128] + jnp.dot(
            weights[c], rows, preferred_element_type=F32
        )

    with jax.named_scope("combine_far"):
        pz[0:4] = combined(0).astype(BF16).reshape(4, 32, 1536)
        far = [
            go(pz.at[SLOT[3]], relay_3.at[0], z_r.at[0], zdev[1]),
            go(pz.at[SLOT[5]], relay_3.at[1], z_r.at[1], zdev[7]),
            go(pz.at[SLOT[4], low], relay_4.at[0], z_r.at[2], zdev[2]),
            go(pz.at[SLOT[4], high], relay_4.at[1], z_r.at[3], zdev[6]),
        ]
    with jax.named_scope("pass_back_near"):
        pass_back(1, back[1])
    with jax.named_scope("combine_near"):
        tot = combined(1)
        pz[4:6] = tot[0:64].astype(BF16).reshape(2, 32, 1536)

        def to_line(o):
            return go(
                pz.at[SLOT[o]], racc.at[SLOT[NZ - o] - 3], z_r.at[SLOT[o]], zdev[o]
            )
    with jax.named_scope("wait_far"):
        for m in far:
            m.wait_recv()
    with jax.named_scope("add_far"):
        none = jnp.zeros((16, 1536), F32)
        plus = (
            tot[64:96] + relay_3[0].astype(F32)
            + jnp.concatenate([relay_4[0].astype(F32), none], axis=0)
        )
        minus = (
            tot[96:128] + relay_3[1].astype(F32)
            + jnp.concatenate([none, relay_4[1].astype(F32)], axis=0)
        )
        pz[SLOT[2]] = plus.astype(BF16)
        pz[SLOT[6]] = minus.astype(BF16)
        red = [to_line(2), to_line(6), to_line(1), to_line(7)]
    racc[0] = pz[0]
    with jax.named_scope("wait_sum"):
        for c in red:
            c.wait_recv()
    out = mixed
    for j in range(5):
        out = out + racc[j].astype(F32)
    out_ref[...] = out.astype(BF16)
    with jax.named_scope("drain"):
        taken_out.wait()
        for c in pending[-POOL:]:
            c.wait_send()


def shards(
    queries, key_vectors, value_vectors, lengths, out_weight, residual, norm_gain, route_ids,
    route_logits, shared_gate_up, shared_down, expert_gate_up, expert_down, cache_blocks, block_table,
):
    hbm, vmem = pl.BlockSpec(memory_space=pltpu.HBM), pl.BlockSpec(memory_space=pltpu.VMEM)
    smem = pl.BlockSpec(memory_space=pltpu.SMEM)
    dma = pltpu.SemaphoreType.DMA
    sgu = jnp.transpose(shared_gate_up, (1, 2, 0))
    wg = expert_gate_up.reshape(1536, 2, 256)
    wd = expert_down.reshape(256, 1536)
    cache = cache_blocks.reshape(NY, NZ, NX, 8, 2, HD)
    sds = jax.ShapeDtypeStruct
    layer_out, _, taken = pl.pallas_call(
        layer_kernel,
        out_shape=(
            sds((32, 1536), BF16),
            sds((NZ, NY, NX, 8, 2, HD), BF16),
            sds((128, 8, 2, HD), BF16),
        ),
        in_specs=[hbm, hbm, hbm, vmem, vmem, hbm, vmem, vmem, vmem, vmem, vmem, hbm, hbm, hbm, smem],
        out_specs=(vmem, hbm, hbm),
        scratch_shapes=[
            pltpu.VMEM((64, 768), BF16),
            pltpu.VMEM((320, 256), BF16),
            pltpu.VMEM((320, 256), BF16),
            pltpu.VMEM((32, 1536), BF16),
            pltpu.VMEM((16, 768), BF16),
            pltpu.VMEM((NZ, 16, 768), BF16),
            pltpu.VMEM((NX, 96, 768), BF16),
            pltpu.VMEM((384, 768), BF16),
            pltpu.VMEM((NY, 64, 768), BF16),
            pltpu.VMEM((NY, 2, 32, 384), BF16),
            pltpu.VMEM((NY, 2, 32, 384), BF16),
            pltpu.VMEM((NZ, 32, 1536), BF16),
            pltpu.VMEM((NZ, 32, 128), F32),
            pltpu.VMEM((16, 1536), BF16),
            pltpu.VMEM((NY, NX, 2, 16, 1536), BF16),
            pltpu.VMEM((2, 1536, 2, 256), BF16),
            pltpu.VMEM((2, 1536, 512), BF16),
            pltpu.VMEM((2, 256, 1536), BF16),
            pltpu.VMEM((NY, NZ, NX, 8, 2, HD), BF16),
            pltpu.VMEM((128, 8, 2, HD), BF16),
            pltpu.VMEM((4, 192, 2, 256), BF16),
            pltpu.VMEM((2, 64, 1536), BF16),
            pltpu.VMEM((2, ROWS, 1536), BF16),
            pltpu.VMEM((2, ROWS, 1536), BF16),
            pltpu.VMEM((2, 32, 1536), BF16),
            pltpu.VMEM((2, 16, 1536), BF16),
            pltpu.VMEM((2, 8, ROWS, 1536), BF16),
            pltpu.VMEM((2, 8, ROWS, 1536), BF16),
            pltpu.VMEM((2, 8, ROWS, 1536), BF16),
            pltpu.VMEM((2, 8, ROWS, 1536), BF16),
            pltpu.VMEM((NZ, 32, 1536), BF16),
            pltpu.VMEM((5, 32, 1536), BF16),
            dma((POOL,)),
            dma((2, 4)),
            dma((8,)),
            dma((4,)),
            dma((8,)),
            dma((4,)),
            dma((4,)),
            dma((8,)),
            dma((15,)),
            dma((6,)),
            dma((6,)),
            dma((3,)),
            dma((4,)),
            dma((2, 4)),
            dma((8,)),
            dma((2, 7)),
            dma((4,)),
            dma((2, 7)),
            dma((9,)),
            dma((9,)),
        ],
        compiler_params=pltpu.CompilerParams(
            collective_id=0, has_side_effects=True, vmem_limit_bytes=56 << 20
        ),
        name="layer",
    )(
        queries, key_vectors, value_vectors, lengths, out_weight.T, residual, norm_gain,
        route_ids.T, route_logits.T, sgu, shared_down, wg, wd, cache, block_table,
    )
    cache_out = taken.reshape(128, 1, 8, 2, HD)
    return layer_out, cache_out


def solution(mesh):
    in_specs = (
        P("seq", "head"),
        P("seq", "head"),
        P("seq", "head"),
        P(),
        P("head", "seq"),
        P(("seq", "head"), None),
        P(),
        P(("seq", "head"), None),
        P(("seq", "head"), None),
        P(None, None, ("seq", "head")),
        P(("seq", "head"), None),
        P("seq", None, None, None),
        P("seq", None, None),
        P("seq", None, None, "head", None),
        P(),
    )
    out_specs = (P(("seq", "head"), None), P(None, "seq", None, "head", None))
    return jax.shard_map(shards, mesh=mesh, in_specs=in_specs, out_specs=out_specs, check_vma=False)
```

```python
import functools
import math

import jax
import jax.numpy as jnp
from jax import lax
from jax.experimental import pallas as pl
from jax.experimental.pallas import tpu as pltpu
from jax.sharding import PartitionSpec as P

MESH = pl.DeviceIdType.MESH
HD = 128
NY, NZ, NX = 4, 8, 4
TOP = 6
CAP = 6
EXPERTS = 64
NEGATIVE = -1e30
EPSILON = 1e-05
F32 = jnp.float32
BF16 = jnp.bfloat16
ZORDER = (1, 7, 2, 6, 3, 5, 4)
OFF = (0, 3, 5, 4, 1, 7, 2, 6)
SLOT = {o: k for k, o in enumerate(OFF)}
ROWS = 24
POOL = 48
COLS = 8 * ROWS
NT = (((1,), (1,)), ((), ()))


def place():
    s = lax.axis_index("seq")
    h = lax.axis_index("head")
    y = lax.div(s, NZ * NX)
    z = lax.rem(lax.div(s, NX), NZ)
    x = lax.rem(s, NX)
    return s, h, y, z, x


def seq_of(y, z, x):
    return y * (NZ * NX) + z * NX + x


def up(i, by, n):
    return lax.rem(i + by, n)


def rcopy(src, dst, ssem, rsem, dev):
    return pltpu.make_async_remote_copy(
        src_ref=src, dst_ref=dst, send_sem=ssem, recv_sem=rsem, device_id=dev, device_id_type=MESH
    )


def iota(shape, axis):
    return lax.broadcasted_iota(jnp.int32, shape, axis)


def silu(v):
    return v / (1.0 + jnp.exp(-v))


def routing_table(ids, logits):
    top = jnp.max(logits, axis=0, keepdims=True)
    e = jnp.exp(logits - top)
    probs = e / jnp.sum(e, axis=0, keepdims=True)
    row = iota((128, 32), 0)
    named = jnp.zeros((128, 32), F32)
    weight = jnp.zeros((128, 32), F32)
    for r in range(TOP):
        idr = jnp.broadcast_to(ids[r : r + 1, :], (128, 32))
        named = named + jnp.where(row == idr, 1.0, 0.0)
        weight = weight + jnp.where(row - EXPERTS == idr, probs[r : r + 1, :], 0.0)
    before = jnp.where(iota((32, 32), 0) < iota((32, 32), 1), 1.0, 0.0)
    rank = jnp.dot(named.astype(BF16), before.astype(BF16), preferred_element_type=F32)
    table = jnp.where(row < EXPERTS, jnp.where(named > 0.5, rank, -1.0), weight)
    return jnp.transpose(table)


def layer_kernel(
    q_hbm, k_hbm, v_hbm, len_ref, ow_ref, res_hbm, gain_ref, ids_ref, log_ref,
    sgu_ref, sd_ref, wg_hbm, wd_hbm, cache_hbm, table_ref,
    out_ref, cmid_ref, cache_ref,
    qbuf, kwin, vwin, resbuf, owpad, owbuf, ocol, wc, hbuf, part, rbuf, xb, rpb, shpad, shb, raw, wgb, wdb,
    chand_ref, taken, relay_g, relay_d, relay_x, relay_b, relay_3, relay_4, dsend, drecv, rsend, rrecv, pz, racc,
    pool, kv_r, owz_r, owx_r, rp_r, shy_r, shx_r, cz_r, cp_r, e1_r, e2_r, sib_r, hy_r,
    rs_r, xz_r, d_r, q_r, r_r, z_r, loc,
):
    s, h, y, z, x = place()
    seqs = NY * NZ * NX
    zdev = {d: (seq_of(y, up(z, d, NZ), x), h) for d in range(1, NZ)}
    plane = [
        (dy, dx) for dy in range(NY) for dx in range(NX) if (dy, dx) != (0, 0)
    ]
    pdev = {at: (seq_of(up(y, at[0], NY), z, up(x, at[1], NX)), h) for at in plane}
    sib = (s, 1 - h)
    cross = [(seq_of(up(y, dy, NY), z, x), 1 - h) for dy in (1, 2, 3)]
    ahead = [(lax.rem(s + by, seqs), h) for by in range(1, 5)]
    behind = [(lax.rem(s + seqs - by, seqs), h) for by in range(1, 5)]

    local = []

    def here(src, dst):
        copy = pltpu.make_async_copy(src, dst, loc.at[len(local)])
        copy.start()
        local.append(copy)
        return copy

    own_wg = here(wg_hbm, raw.at[0])
    own_k = here(k_hbm, kwin.at[pl.ds(256, 64)])
    own_v = here(v_hbm, vwin.at[pl.ds(256, 64)])
    own_q = here(q_hbm, qbuf)
    own_cache = here(cache_hbm.at[:, z], cmid_ref.at[z])
    own_res = here(res_hbm, resbuf)
    own_wd = here(wd_hbm, wdb.at[0])
    peers = list(zdev.values()) + list(pdev.values()) + [sib] + cross + ahead + behind
    barrier = pltpu.get_barrier_semaphore()
    for dev in peers:
        pl.semaphore_signal(barrier, inc=1, device_id=dev, device_id_type=MESH)

    with jax.named_scope("pack"):
        owpad[...] = jnp.concatenate(
            [ow_ref[...].astype(F32), jnp.zeros((4, 768), F32)], axis=0
        ).astype(BF16)
        owbuf[z] = owpad[...]
        shpad[...] = jnp.concatenate(
            [
                sgu_ref[...].astype(F32).reshape(8, 1536),
                sd_ref[...].astype(F32),
                jnp.zeros((4, 1536), F32),
            ],
            axis=0,
        ).astype(BF16)
        shb[y, x, h] = shpad[...]
    with jax.named_scope("routing"):
        rpb[0] = routing_table(ids_ref[...], log_ref[...])
    with jax.named_scope("enter"):
        pl.semaphore_wait(barrier, len(peers))

    pending = []

    def go(src, dst, recv, dev):
        turn = len(pending)
        if turn >= POOL:
            pending[turn - POOL].wait_send()
        copy = rcopy(src, dst, pool.at[turn % POOL], recv, dev)
        copy.start()
        pending.append(copy)
        return copy

    owz = [go(owpad, owbuf.at[z], owz_r.at[d], zdev[d]) for d in ZORDER]
    kv = []
    for by in range(1, 5):
        rows = pl.ds(64 * (4 - by), 64)
        kv.append(go(k_hbm, kwin.at[rows], kv_r.at[0, by - 1], ahead[by - 1]))
        kv.append(go(v_hbm, vwin.at[rows], kv_r.at[1, by - 1], ahead[by - 1]))
    shy = [
        go(shpad, shb.at[y, x, h], shy_r.at[d], pdev[(d, 0)]) for d in (1, 3, 2)
    ]
    sides = (pdev[(1, 0)], pdev[(3, 0)])
    rows_g, rows_d = pl.ds(h * 768, 768), pl.ds(h * 128, 128)

    def piece(i):
        if i < 4:
            return pl.ds(h * 768 + i * 192, 192)
        return pl.ds(h * 128 + (i - 4) * 64, 64)

    def first_hop(i):
        sem = e1_r.at[i], sides[i % 2]
        if i < 4:
            return go(wg_hbm.at[piece(i)], relay_g.at[i], *sem)
        return go(wd_hbm.at[piece(i)], relay_d.at[i - 4], *sem)

    def second_hop(i, arrived):
        arrived.wait_recv()
        sem = e2_r.at[i], sides[i % 2]
        if i < 4:
            return go(relay_g.at[i], raw.at[1, piece(i)], *sem)
        return go(relay_d.at[i - 4], wdb.at[1, piece(i)], *sem)

    ex1 = [first_hop(i) for i in range(4)]

    with jax.named_scope("visible"):
        upper = jnp.where(iota((64, 64), 0) <= iota((64, 64), 1), 1.0, 0.0).astype(BF16)
        lens = jnp.broadcast_to(len_ref[...].astype(F32).reshape(1, 64), (16, 64)).astype(BF16)
        ends = jnp.dot(lens, upper, preferred_element_type=F32)[0:1, :]
        qpos = (s * 64 + iota((64, 64), 0)).astype(F32)
        first = jnp.max(jnp.where(ends <= qpos, ends, 0.0), axis=-1, keepdims=True)
        kpos = (s * 64 - 256 + iota((64, 320), 1)).astype(F32)
        qcol = (s * 64 + iota((64, 320), 0)).astype(F32)
        seen = jnp.where((kpos >= first) & (kpos <= qcol), 0.0, NEGATIVE)
        seen3 = jnp.concatenate([seen, seen, seen], axis=0)

    col, row = iota((96, 128), 0), iota((96, 128), 1)
    pack = jnp.where(row == lax.div(col, 12) * 16 + lax.rem(col, 12), 1.0, 0.0).astype(BF16)
    with jax.named_scope("wait_first_columns"):
        for c in owz:
            c.wait_recv()
    ocol[x] = jnp.dot(
        pack, owbuf[...].reshape(128, 768), preferred_element_type=F32
    ).astype(BF16)
    owx = {
        d: go(ocol.at[x], ocol.at[x], owx_r.at[d], pdev[(0, d)])
        for d in (1, 3)
    }
    with jax.named_scope("wait_keys"):
        own_k.wait()
        own_v.wait()
        own_q.wait()
        for c in kv:
            c.wait_recv()
    with jax.named_scope("attention"):
        for g in range(2):
            cols = slice(g * HD, (g + 1) * HD)
            qs = jnp.concatenate(
                [qbuf[:, (3 * g + i) * HD : (3 * g + i + 1) * HD] for i in range(3)], axis=0
            )
            sc = lax.dot_general(qs, kwin[:, cols], NT, preferred_element_type=F32)
            sc = jnp.where(seen3 < -1.0, NEGATIVE, sc * (1.0 / math.sqrt(HD)))
            w = jnp.exp(sc - jnp.max(sc, axis=-1, keepdims=True))
            total = jnp.sum(w, axis=-1, keepdims=True)
            o = jnp.dot(w.astype(BF16), vwin[:, cols], preferred_element_type=F32)
            o = (o / total).astype(BF16)
            for i in range(3):
                hbuf[y, :, (3 * g + i) * HD : (3 * g + i + 1) * HD] = o[i * 64 : (i + 1) * 64]
    hy = [
        go(hbuf.at[y], hbuf.at[y], hy_r.at[d], pdev[(d, 0)]) for d in (1, 3, 2)
    ]

    rp = [
        go(rpb.at[0], rpb.at[SLOT[NZ - d]], rp_r.at[d], zdev[d]) for d in ZORDER
    ]
    cz = [
        go(cache_hbm.at[:, up(z, d, NZ)], cmid_ref.at[z], cz_r.at[d], zdev[d])
        for d in ZORDER
    ]
    with jax.named_scope("gate_up"):
        own_wg.wait()
        wgb[0, 0:768, 0:256] = raw[0, 0:768, 0, :]
        wgb[0, 0:768, 256:512] = raw[0, 0:768, 1, :]
    with jax.named_scope("wait_columns"):
        left, right = up(x, 3, NX), up(x, 1, NX)
        owx[1].wait_recv()
        lower = ocol.at[left, 0:48]
        fwd = [go(lower, lower, owx_r.at[0], pdev[(0, 1)])]
        owx[3].wait_recv()
        higher = ocol.at[right, 48:96]
        fwd.append(go(higher, higher, owx_r.at[2], pdev[(0, 3)]))
        for c in shy:
            c.wait_recv()
    with jax.named_scope("wait_far_columns"):
        for c in fwd:
            c.wait_recv()
    shx = [
        go(shb.at[:, x, h], shb.at[:, x, h], shx_r.at[d], pdev[(0, d)])
        for d in (1, 3, 2)
    ]
    with jax.named_scope("relay_gate"):
        ex2 = [second_hop(i, ex1[i]) for i in range(2)]
    with jax.named_scope("columns"):
        col, row = iota((384, 384), 0), iota((384, 384), 1)
        source = (
            lax.div(lax.rem(col, 48), 12) * 96 + lax.div(col, 48) * 12 + lax.rem(col, 12)
        )
        order = jnp.where(row == source, 1.0, 0.0).astype(BF16)
        wc[...] = jnp.dot(
            order, ocol[...].reshape(384, 768), preferred_element_type=F32
        ).astype(BF16)

    with jax.named_scope("wait_heads"):
        for c in hy:
            c.wait_recv()
    with jax.named_scope("project"):
        po = lax.dot_general(hbuf[...].reshape(256, 768), wc[...], NT, preferred_element_type=F32)
        part[...] = po.reshape(4, 2, 32, 384).astype(BF16)
    rs = []
    for d in (1, 3, 2):
        yd = up(y, d, NY)
        for i, hd in enumerate((h, 1 - h)):
            rs.append(
                go(part.at[yd, hd], rbuf.at[y, h], rs_r.at[i, d], (seq_of(yd, z, x), hd))
            )
    rs.append(go(part.at[y, 1 - h], rbuf.at[y, h], rs_r.at[1, 0], sib))
    rbuf[y, h] = part[y, h]
    with jax.named_scope("relay_gate_rest"):
        ex2 += [second_hop(i, ex1[i]) for i in range(2, 4)]
        ex1 += [first_hop(i) for i in range(4, 6)]
    with jax.named_scope("gate_up_rest"):
        wgb[0, 768:1536, 0:256] = raw[0, 768:1536, 0, :]
        wgb[0, 768:1536, 256:512] = raw[0, 768:1536, 1, :]
    with jax.named_scope("wait_projected"):
        for c in rs:
            c.wait_recv()
    with jax.named_scope("norm"):
        own_res.wait()
        attn = [rbuf[j, 0].astype(F32) + rbuf[j, 1].astype(F32) for j in range(NY)]
        mixed = resbuf[...].astype(F32) + jnp.concatenate(attn, axis=1)
        ms = jnp.mean(mixed * mixed, axis=-1, keepdims=True)
        xb[0] = (mixed * lax.rsqrt(ms + EPSILON) * gain_ref[...].reshape(1, 1536)).astype(BF16)
    xz = {
        d: go(xb.at[0], xb.at[SLOT[NZ - d]], xz_r.at[d], zdev[d]) for d in (2, 6, 1, 7)
    }
    with jax.named_scope("cache_plane"):
        own_cache.wait()
        for c in cz:
            c.wait_recv()
        cp = [
            go(
                cmid_ref.at[:, up(y, at[0], NY), up(x, at[1], NX)], chand_ref.at[y, :, x],
                cp_r.at[i], pdev[at],
            )
            for i, at in enumerate(plane)
        ]
        cp_own = here(cmid_ref.at[:, y, x], chand_ref.at[y, :, x])
    with jax.named_scope("choose"):
        for c in rp:
            c.wait_recv()
        lane = iota((128, COLS), 1)
        half = lax.div(lane, COLS // 2)
        expert = lax.rem(y + half, 2) * 32 + z * NX + lax.rem(lax.div(lane, ROWS), NX)
        row = iota((128, COLS), 0)
        of_rank = jnp.where(row == expert, 1.0, 0.0).astype(BF16)
        of_prob = jnp.where(row == expert + EXPERTS, 1.0, 0.0).astype(BF16)
        slot = lax.rem(iota((128, COLS), 1), ROWS)
        member = lax.div(row, 32) == lax.div(slot, CAP)
        number = lax.rem(slot, CAP).astype(F32)
        picks, weights = [], []
        for c in range(2):
            rpc = rpb[4 * c : 4 * c + 4].reshape(128, 128).astype(BF16)
            rank = jnp.dot(rpc, of_rank, preferred_element_type=F32)
            prob = jnp.dot(rpc, of_prob, preferred_element_type=F32)
            hit = member & (rank == number)
            picks.append(jnp.transpose(jnp.where(hit, 1.0, 0.0)).astype(BF16))
            weights.append(jnp.where(hit, prob, 0.0).astype(BF16))

    with jax.named_scope("wait_near_rows"):
        xz[2].wait_recv()
        low = pl.ds(0, 16)
        xz[4] = go(
            xb.at[SLOT[6], low], xb.at[SLOT[4], low], xz_r.at[4], zdev[2]
        )
        xz[3] = go(xb.at[SLOT[6]], xb.at[SLOT[5]], xz_r.at[3], zdev[1])
        xz[6].wait_recv()
        high = pl.ds(16, 16)
        xz[0] = go(
            xb.at[SLOT[2], high], xb.at[SLOT[4], high], xz_r.at[0], zdev[6]
        )
        xz[5] = go(xb.at[SLOT[2]], xb.at[SLOT[3]], xz_r.at[5], zdev[7])
        xz[1].wait_recv()
        xz[7].wait_recv()

    turn = 1 + 2 * lax.rem(x, 2)

    def to_expert(p, d):
        return pdev[(0, d)] if p == 0 else (seq_of(up(y, turn, NY), z, up(x, d, NX)), h)

    def to_source(p, d):
        xs = up(x, NX - d, NX)
        if p == 0:
            return pdev[(0, NX - d)]
        return (seq_of(up(y, 3 - 2 * lax.rem(xs, 2), NY), z, xs), h)

    hops = [(p, d) for p in range(2) for d in (2, 1, 3, 0) if (p, d) != (0, 0)]
    before = pdev[(0, 3)]

    def dispatch(c):
        xc = xb[4 * c : 4 * c + 4].reshape(128, 1536)
        rows = jnp.dot(picks[c], xc, preferred_element_type=F32)
        for j in range(8):
            dsend[c, j] = rows[j * ROWS : (j + 1) * ROWS].astype(BF16)
        copies = [go(dsend.at[c, up(x, 2, NX)], relay_x.at[c], q_r.at[c], before)]
        for i, (p, d) in enumerate(hops[1:], 1):
            copies.append(
                go(
                    dsend.at[c, p * NX + up(x, d, NX)], drecv.at[c, p * NX + x],
                    d_r.at[c, i], to_expert(p, d),
                )
            )
        drecv[c, x] = dsend[c, x]
        return copies

    def pass_on(c, copies):
        copies[0].wait_recv()
        copies[0] = go(
            relay_x.at[c], drecv.at[c, up(x, 1, NX)], d_r.at[c, 0], before
        )

    sent = {}
    with jax.named_scope("dispatch"):
        sent[1] = dispatch(1)
    with jax.named_scope("pass_on"):
        pass_on(1, sent[1])
    with jax.named_scope("wait_rows"):
        for d in (3, 5, 4, 0):
            xz[d].wait_recv()
    with jax.named_scope("dispatch"):
        sent[0] = dispatch(0)
    with jax.named_scope("relay_down"):
        ex2d = [second_hop(i, ex1[i]) for i in range(4, 6)]
    ex2g = ex2
    with jax.named_scope("gate_sibling"):
        for c in ex2g:
            c.wait_recv()
        sib_g = go(raw.at[1, rows_g], raw.at[1, rows_g], sib_r.at[1], sib)
    with jax.named_scope("shared_weights"):
        for m in shx:
            m.wait_recv()
        sib_sh = go(shb.at[:, :, h], shb.at[:, :, h], sib_r.at[0], sib)
    with jax.named_scope("shared"):
        sib_sh.wait_recv()
        xs = xb[...].reshape(256, 1536)
        sh = shb[...].reshape(512, 1536)
        both = lax.dot_general(xs, sh, NT, preferred_element_type=F32)
        act = silu(pltpu.roll(both, 8, 1)) * pltpu.roll(both, 4, 1)
        live = lax.rem(lax.div(iota((256, 512), 1), 4), 4) == 2
        act = jnp.where(live, act, 0.0).astype(BF16)
        shared = jnp.dot(act, sh, preferred_element_type=F32)
    with jax.named_scope("gate_up_other"):
        sib_g.wait_recv()
        wgb[1, :, 0:256] = raw[1, :, 0, :]
        wgb[1, :, 256:512] = raw[1, :, 1, :]
    with jax.named_scope("pass_on"):
        pass_on(0, sent[0])
    with jax.named_scope("down_sibling"):
        for c in ex2d:
            c.wait_recv()
        sib_d = go(wdb.at[1, rows_d], wdb.at[1, rows_d], sib_r.at[2], sib)
    with jax.named_scope("wait_exchange"):
        own_wd.wait()
        sib_d.wait_recv()

    def experts(c):
        for m in sent[c]:
            m.wait_recv()
        rows = jnp.concatenate([drecv[c, j].astype(F32) for j in range(8)], axis=0).astype(BF16)
        acc = None
        for j in range(2):
            gu = jnp.dot(rows, wgb[j], preferred_element_type=F32)
            a = (silu(gu[:, :256]) * gu[:, 256:]).astype(BF16)
            o = jnp.dot(a, wdb[j], preferred_element_type=F32)
            acc = o if acc is None else acc + o
        for j in range(8):
            rsend[c, j] = acc[j * ROWS : (j + 1) * ROWS].astype(BF16)
        rrecv[c, x] = rsend[c, x]

    def give_back(c):
        copies = [go(rsend.at[c, up(x, 2, NX)], relay_b.at[c], q_r.at[2 + c], before)]
        for i, (p, d) in enumerate(hops[1:], 1):
            copies.append(
                go(
                    rsend.at[c, p * NX + up(x, NX - d, NX)], rrecv.at[c, p * NX + x],
                    r_r.at[c, i], to_source(p, d),
                )
            )
        return copies

    def pass_back(c, copies):
        copies[0].wait_recv()
        copies[0] = go(relay_b.at[c], rrecv.at[c, up(x, 1, NX)], r_r.at[c, 0], before)

    back = {}
    with jax.named_scope("experts_near"):
        experts(1)
    with jax.named_scope("experts_far"):
        experts(0)
        back[0] = give_back(0)
    with jax.named_scope("pass_back_far"):
        pass_back(0, back[0])
        back[1] = give_back(1)

    with jax.named_scope("cache_order"):
        cp_own.wait()
        for c in cp:
            c.wait_recv()

        def take(b, carry):
            i = table_ref[b]
            taken[b] = chand_ref[lax.div(i, 32), lax.rem(lax.div(i, 4), 8), lax.rem(i, 4)]
            return carry

        lax.fori_loop(0, 128, take, 0)
        taken_out = here(taken, cache_ref)

    def combined(c):
        for m in back[c]:
            m.wait_recv()
        rows = jnp.concatenate([rrecv[c, j].astype(F32) for j in range(8)], axis=0).astype(BF16)
        return shared[128 * c : 128 * c + 128] + jnp.dot(
            weights[c], rows, preferred_element_type=F32
        )

    with jax.named_scope("combine_far"):
        pz[0:4] = combined(0).astype(BF16).reshape(4, 32, 1536)
        far = [
            go(pz.at[SLOT[3]], relay_3.at[0], z_r.at[0], zdev[1]),
            go(pz.at[SLOT[5]], relay_3.at[1], z_r.at[1], zdev[7]),
            go(pz.at[SLOT[4], low], relay_4.at[0], z_r.at[2], zdev[2]),
            go(pz.at[SLOT[4], high], relay_4.at[1], z_r.at[3], zdev[6]),
        ]
    with jax.named_scope("pass_back_near"):
        pass_back(1, back[1])
    with jax.named_scope("combine_near"):
        tot = combined(1)
        pz[4:6] = tot[0:64].astype(BF16).reshape(2, 32, 1536)

        def to_line(o):
            return go(
                pz.at[SLOT[o]], racc.at[SLOT[NZ - o] - 3], z_r.at[SLOT[o]], zdev[o]
            )
    with jax.named_scope("wait_far"):
        for m in far:
            m.wait_recv()
    with jax.named_scope("add_far"):
        none = jnp.zeros((16, 1536), F32)
        plus = (
            tot[64:96] + relay_3[0].astype(F32)
            + jnp.concatenate([relay_4[0].astype(F32), none], axis=0)
        )
        minus = (
            tot[96:128] + relay_3[1].astype(F32)
            + jnp.concatenate([none, relay_4[1].astype(F32)], axis=0)
        )
        pz[SLOT[2]] = plus.astype(BF16)
        pz[SLOT[6]] = minus.astype(BF16)
        red = [to_line(2), to_line(6), to_line(1), to_line(7)]
    racc[0] = pz[0]
    with jax.named_scope("wait_sum"):
        for c in red:
            c.wait_recv()
    out = mixed
    for j in range(5):
        out = out + racc[j].astype(F32)
    out_ref[...] = out.astype(BF16)
    with jax.named_scope("drain"):
        taken_out.wait()
        for c in pending[-POOL:]:
            c.wait_send()


def shards(
    queries, key_vectors, value_vectors, lengths, out_weight, residual, norm_gain, route_ids,
    route_logits, shared_gate_up, shared_down, expert_gate_up, expert_down, cache_blocks, block_table,
):
    hbm, vmem = pl.BlockSpec(memory_space=pltpu.HBM), pl.BlockSpec(memory_space=pltpu.VMEM)
    smem = pl.BlockSpec(memory_space=pltpu.SMEM)
    dma = pltpu.SemaphoreType.DMA
    sgu = jnp.transpose(shared_gate_up, (1, 2, 0))
    wg = expert_gate_up.reshape(1536, 2, 256)
    wd = expert_down.reshape(256, 1536)
    cache = cache_blocks.reshape(NY, NZ, NX, 8, 2, HD)
    sds = jax.ShapeDtypeStruct
    layer_out, _, taken = pl.pallas_call(
        layer_kernel,
        out_shape=(
            sds((32, 1536), BF16),
            sds((NZ, NY, NX, 8, 2, HD), BF16),
            sds((128, 8, 2, HD), BF16),
        ),
        in_specs=[hbm, hbm, hbm, vmem, vmem, hbm, vmem, vmem, vmem, vmem, vmem, hbm, hbm, hbm, smem],
        out_specs=(vmem, hbm, hbm),
        scratch_shapes=[
            pltpu.VMEM((64, 768), BF16),
            pltpu.VMEM((320, 256), BF16),
            pltpu.VMEM((320, 256), BF16),
            pltpu.VMEM((32, 1536), BF16),
            pltpu.VMEM((16, 768), BF16),
            pltpu.VMEM((NZ, 16, 768), BF16),
            pltpu.VMEM((NX, 96, 768), BF16),
            pltpu.VMEM((384, 768), BF16),
            pltpu.VMEM((NY, 64, 768), BF16),
            pltpu.VMEM((NY, 2, 32, 384), BF16),
            pltpu.VMEM((NY, 2, 32, 384), BF16),
            pltpu.VMEM((NZ, 32, 1536), BF16),
            pltpu.VMEM((NZ, 32, 128), F32),
            pltpu.VMEM((16, 1536), BF16),
            pltpu.VMEM((NY, NX, 2, 16, 1536), BF16),
            pltpu.VMEM((2, 1536, 2, 256), BF16),
            pltpu.VMEM((2, 1536, 512), BF16),
            pltpu.VMEM((2, 256, 1536), BF16),
            pltpu.VMEM((NY, NZ, NX, 8, 2, HD), BF16),
            pltpu.VMEM((128, 8, 2, HD), BF16),
            pltpu.VMEM((4, 192, 2, 256), BF16),
            pltpu.VMEM((2, 64, 1536), BF16),
            pltpu.VMEM((2, ROWS, 1536), BF16),
            pltpu.VMEM((2, ROWS, 1536), BF16),
            pltpu.VMEM((2, 32, 1536), BF16),
            pltpu.VMEM((2, 16, 1536), BF16),
            pltpu.VMEM((2, 8, ROWS, 1536), BF16),
            pltpu.VMEM((2, 8, ROWS, 1536), BF16),
            pltpu.VMEM((2, 8, ROWS, 1536), BF16),
            pltpu.VMEM((2, 8, ROWS, 1536), BF16),
            pltpu.VMEM((NZ, 32, 1536), BF16),
            pltpu.VMEM((5, 32, 1536), BF16),
            dma((POOL,)),
            dma((2, 4)),
            dma((8,)),
            dma((4,)),
            dma((8,)),
            dma((4,)),
            dma((4,)),
            dma((8,)),
            dma((15,)),
            dma((6,)),
            dma((6,)),
            dma((3,)),
            dma((4,)),
            dma((2, 4)),
            dma((8,)),
            dma((2, 7)),
            dma((4,)),
            dma((2, 7)),
            dma((9,)),
            dma((9,)),
        ],
        compiler_params=pltpu.CompilerParams(
            collective_id=0, has_side_effects=True, vmem_limit_bytes=56 << 20
        ),
        name="layer",
    )(
        queries, key_vectors, value_vectors, lengths, out_weight.T, residual, norm_gain,
        route_ids.T, route_logits.T, sgu, shared_down, wg, wd, cache, block_table,
    )
    cache_out = taken.reshape(128, 1, 8, 2, HD)
    return layer_out, cache_out


def solution(mesh):
    in_specs = (
        P("seq", "head"),
        P("seq", "head"),
        P("seq", "head"),
        P(),
        P("head", "seq"),
        P(("seq", "head"), None),
        P(),
        P(("seq", "head"), None),
        P(("seq", "head"), None),
        P(None, None, ("seq", "head")),
        P(("seq", "head"), None),
        P("seq", None, None, None),
        P("seq", None, None),
        P("seq", None, None, "head", None),
        P(),
    )
    out_specs = (P(("seq", "head"), None), P(None, "seq", None, "head", None))
    return jax.shard_map(shards, mesh=mesh, in_specs=in_specs, out_specs=out_specs, check_vma=False)
```
